256 devices in a mesh: patch: 32 (over z, x), frame: 8 (over y, core).
Axes of the slice: x: 4, y: 4, z: 8, core: 2. Of those that a mesh axis runs over, the one named last changes fastest.
Arguments:
- screens: float32 [2, 2048, 4096], P(None, 'patch'), may hold values from -6 to 6
- row_offsets: int32 [8, 2, 32], replicated, may hold values from 0 to 1792
- col_offsets: int32 [8, 2, 32], replicated, may hold values from 0 to 3840
- amplitude: float32 [256, 256], replicated, may hold values from 0.5 to 1.5
- object_strip: float32 [384, 8192], P(None, 'patch'), may hold values from 0.5 to 1.5
- observed: float32 [8, 256, 8192], P('frame', None, 'patch'), may hold values from 0.5 to 1.5
Outputs:
- screen_grad: float32 [2, 2048, 4096], P(None, 'patch', 'frame')
The draws below stay inside these ranges and needn't reach their ends.
All inputs are finite; a program needn't handle non-finite values.
Results may differ from the reference program's by a relative error of at most 0.0003.
Values sent between devices are 32-bit elements; how exact they have to be, the bound alone decides.
No kernel may reach another device: no remote copies, remote signals or barrier semaphores. Data moves between devices by JAX's collectives and lax.ppermute only.
A program may use at most 128 MiB of HBM per device.

```python
import jax
import jax.numpy as jnp
from jax import lax

CORE = 256
HALO = 64
WIN = 256
SPAN = 384
LAYERS = 2
SCOLS = 4096
FRAMES = 8
PATCHES = 32
SCREEN_ROWS = 2048


def draw_row_offsets(key, part):
    first_key, second_key = jax.random.split(jax.random.fold_in(key, 11))
    highest = SCREEN_ROWS - WIN
    jitter_span = WIN // 2
    base_rows = jax.random.randint(first_key, (FRAMES, LAYERS, 1), 0, highest - jitter_span + 1)
    jitter = jax.random.randint(second_key, (FRAMES, LAYERS, PATCHES), 0, jitter_span + 1)
    rows_all = base_rows + jitter
    rows_all = rows_all.at[0, 0, 0].set(0).at[FRAMES - 1, LAYERS - 1, PATCHES - 1].set(highest)
    return rows_all.astype(jnp.int32)


def draw_col_offsets(key, part):
    first_key, second_key = jax.random.split(jax.random.fold_in(key, 23))
    highest = SCOLS - WIN
    layer_step = jax.random.randint(first_key, (1, LAYERS, 1), 0, highest // PATCHES + 1)
    raw_base = jax.random.randint(second_key, (FRAMES, LAYERS, 1), 0, 1 << 20)
    base_cols = raw_base % (highest - layer_step * (PATCHES - 1) + 1)
    cols_all = base_cols + layer_step * jnp.arange(PATCHES, dtype=jnp.int32)[None, None, :]
    cols_all = cols_all.at[0, 0, 0].set(0).at[FRAMES - 1, LAYERS - 1, PATCHES - 1].set(highest)
    return cols_all.astype(jnp.int32)


def shard_levels(stream_key, shape, cuts, least, top_value):
    loudness = 1.0
    for dim, shards_of in cuts:
        steps = jax.random.uniform(jax.random.fold_in(jax.random.fold_in(stream_key, 6), dim), (shards_of,), jnp.float32, least / len(cuts), top_value / len(cuts))
        loudness = loudness * jnp.repeat(jnp.exp(steps), shape[dim] // shards_of).reshape((-1,) + (1,) * (len(shape) - 1 - dim))
    return loudness


def gaussian(rng, dims, scale, bound, cuts=(), kind=jnp.bfloat16):
    entries = jax.random.normal(rng, dims, jnp.float32) * scale
    if len(cuts) > 0:
        entries = shard_levels(rng, dims, cuts, -0.22, 0.18) * entries
    return jnp.clip(entries, min=-bound, max=bound).astype(kind)


def setup_inputs(seed: int = 0) -> dict:
    keys = jax.random.split(jax.random.key(seed), 7)
    return {
        "screens": gaussian(keys[0], (LAYERS, SCREEN_ROWS, SCOLS), 1.0, 6.0, ((1, 32),), jnp.float32),
        "row_offsets": draw_row_offsets(jax.random.fold_in(keys[6], 71), 0),
        "col_offsets": draw_col_offsets(jax.random.fold_in(keys[6], 71), 0),
        "amplitude": jnp.clip(jax.random.uniform(keys[3], (WIN, WIN), jnp.float32, 0.5, 1.5), 0.5, 1.5),
        "object_strip": jnp.clip(0.5 + 1.0 * jax.random.uniform(keys[4], (SPAN, PATCHES * CORE), jnp.float32) ** shard_levels(keys[4], (SPAN, PATCHES * CORE), ((1, 32),), -0.2, 0.2), 0.5, 1.5),
        "observed": jnp.clip(0.5 + 1.0 * jax.random.uniform(keys[5], (FRAMES, CORE, PATCHES * CORE), jnp.float32) ** shard_levels(keys[5], (FRAMES, CORE, PATCHES * CORE), ((0, 8), (2, 32)), -0.2, 0.2), 0.5, 1.5),
    }


def pair_gradient(phases, window, target, amplitude):
    extent = window.shape[0]
    win_size = phases.shape[0]
    core_size = target.shape[0]
    margin = (extent - core_size) // 2
    inverse_total = 1.0 / (extent * extent * jnp.sum(amplitude * amplitude))
    pupil_field = amplitude * jnp.exp(1j * phases)
    padded = jnp.zeros((extent, extent), pupil_field.dtype).at[:win_size, :win_size].set(pupil_field)
    far_field = jnp.fft.fft2(padded)
    spread = (jnp.real(far_field) ** 2 + jnp.imag(far_field) ** 2) * inverse_total
    object_spec = jnp.fft.fft2(window)
    model_image = jnp.real(jnp.fft.ifft2(jnp.fft.fft2(spread) * object_spec))
    residual = (model_image[margin:margin + core_size, margin:margin + core_size] - target) * (win_size * extent / core_size)
    model_grad = jnp.zeros((extent, extent), residual.dtype).at[margin:margin + core_size, margin:margin + core_size].set(residual)
    spread_grad = jnp.real(jnp.fft.ifft2(jnp.fft.fft2(model_grad) * jnp.conj(object_spec)))
    backward = (extent * extent) * jnp.fft.ifft2(far_field * spread_grad)[:win_size, :win_size]
    return 2.0 * inverse_total * (jnp.real(pupil_field) * jnp.imag(backward) - jnp.imag(pupil_field) * jnp.real(backward))


def reference(screens, row_offsets, col_offsets, amplitude, object_strip, observed):
    extent = object_strip.shape[0]
    padded_object = jnp.pad(object_strip, ((0, 0), (HALO, HALO)))

    def single(position):
        position = position.astype(jnp.int32)
        frame_id = position // PATCHES
        patch_id = position % PATCHES
        phases = jnp.zeros((WIN, WIN), screens.dtype)
        for layer_id in range(LAYERS):
            phases = phases + lax.dynamic_slice(screens[layer_id], (row_offsets[frame_id, layer_id, patch_id], col_offsets[frame_id, layer_id, patch_id]), (WIN, WIN))
        begin_col = (patch_id * CORE).astype(jnp.int32)
        window = lax.dynamic_slice(padded_object, (jnp.int32(0), begin_col), (extent, extent))
        target = lax.dynamic_slice(observed[frame_id], (jnp.int32(0), begin_col), (CORE, CORE))
        return pair_gradient(phases, window, target, amplitude)

    gradients = lax.map(single, jnp.arange(FRAMES * PATCHES, dtype=jnp.int32))

    def accumulate(position, running):
        position = position.astype(jnp.int32)
        frame_id = position // PATCHES
        patch_id = position % PATCHES
        for layer_id in range(LAYERS):
            corner = (jnp.int32(layer_id), row_offsets[frame_id, layer_id, patch_id], col_offsets[frame_id, layer_id, patch_id])
            current = lax.dynamic_slice(running, corner, (1, WIN, WIN))
            running = lax.dynamic_update_slice(running, current + gradients[position][None], corner)
        return running

    return lax.fori_loop(0, FRAMES * PATCHES, accumulate, jnp.zeros_like(screens))
```

```python
import functools
import math

import jax
import jax.numpy as jnp
import numpy as np
from jax import lax
from jax.experimental import pallas as pl
from jax.experimental.pallas import tpu as pltpu
from jax.sharding import Mesh, PartitionSpec as P

CORE = 256
HALO = 64
SPAN = 384
HALF = 256
SLAB = ("x", "y", "core")
FRAME = ("y", "core")


def split_constants():
    index = np.arange(SPAN)
    angles = (np.outer(index, index) % SPAN) * (2.0 * np.pi / SPAN)
    cosine, sine = np.cos(angles), np.sin(angles)
    parts = []
    for values in (cosine, sine):
        high = values.astype(jnp.bfloat16)
        low = (values - high.astype(np.float64)).astype(jnp.bfloat16)
        parts += [high, low]
    return parts


def split(values):
    high = values.astype(jnp.bfloat16)
    low = (values - high.astype(jnp.float32)).astype(jnp.bfloat16)
    return high, low


def dot(left, right):
    return jnp.dot(left, right, preferred_element_type=jnp.float32)


def product(left, right):
    return dot(left[0], right[0]) + (dot(left[0], right[1]) + dot(left[1], right[0]))


class Pair:
    def __init__(self, high, low):
        self.refs = (high, low)

    def __getitem__(self, index):
        return tuple(ref[index] for ref in self.refs)

    def put(self, index, values):
        for ref, part in zip(self.refs, split(values)):
            ref[index] = part


def sine_cosine(angle):
    turns = jnp.round(angle * (2.0 / math.pi))
    rest = angle - turns * 1.5703125
    rest = rest - turns * 4.837512969970703125e-4
    rest = rest - turns * 7.549789948768648e-8
    square = rest * rest
    sine = rest + rest * square * (
        -1.6666654611e-1 + square * (8.3321608736e-3 + square * -1.9515295891e-4)
    )
    cosine = 1.0 - 0.5 * square + square * square * (
        4.166664568298827e-2 + square * (-1.388731625493765e-3 + square * 2.443315711809948e-5)
    )
    quarter = turns.astype(jnp.int32)
    odd = (quarter & 1) == 1
    sine, cosine = jnp.where(odd, cosine, sine), jnp.where(odd, sine, cosine)
    sine = jnp.where((quarter & 2) == 2, -sine, sine)
    cosine = jnp.where(((quarter + 1) & 2) == 2, -cosine, cosine)
    return sine, cosine


LOW = slice(0, CORE)
HIGH = slice(SPAN, SPAN + CORE)
FULL = slice(0, SPAN)
REST = slice(SPAN, 2 * SPAN)
ALL = slice(None)


def object_kernel(ch, cl, sh, sl, window, forward_h, forward_l, inverse_h, inverse_l, spec_re, spec_im):
    for target_f, target_i, cos_ref, sin_ref in (
        (forward_h, inverse_h, ch, sh),
        (forward_l, inverse_l, cl, sl),
    ):
        cosine, sine = cos_ref[...], sin_ref[...]
        target_f[FULL, FULL] = cosine
        target_f[FULL, REST] = sine
        target_f[REST, FULL] = -sine
        target_f[REST, REST] = cosine
        target_i[FULL, FULL] = cosine
        target_i[FULL, REST] = -sine
        target_i[REST, FULL] = sine
        target_i[REST, REST] = cosine
    forward, inverse = Pair(forward_h, forward_l), Pair(inverse_h, inverse_l)
    seen = split(window[...])
    part_re = split(product(seen, inverse[FULL, LOW]))
    part_im = split(product(seen, inverse[FULL, HIGH]))
    out = product(forward[ALL, FULL], part_re) + product(forward[ALL, REST], part_im)
    column = lax.broadcasted_iota(jnp.int32, (SPAN, HALF), 1)
    ends = (column == 0) | (column == SPAN // 2)
    weight = jnp.where(ends, 1.0, jnp.where(column < SPAN // 2, 2.0, 0.0)) / (SPAN * SPAN)
    spec_re[...] = out[FULL] * weight
    spec_im[...] = out[REST] * weight


def select_kernel(place, rows, cols, gathered, out):
    slab, first = place[0], place[1]
    row_index = first + lax.broadcasted_iota(jnp.int32, (8, CORE), 0)
    lane = lax.broadcasted_iota(jnp.int32, (8, CORE), 1)

    def one(member, carry):
        patch = slab * 4 + member // 8
        frame = member % 8
        for layer in range(2):
            row = rows[frame, layer, patch]
            col = cols[frame, layer, patch]
            block, residue = row // CORE, row % CORE
            after = jnp.minimum(block + 1, 7)
            strip, turn = col // CORE, col % CORE
            at = pl.ds(pl.multiple_of(strip * CORE, CORE), CORE)
            beside = pl.ds(pl.multiple_of(jnp.minimum(strip + 1, 15) * CORE, CORE), CORE)
            right = lane >= turn
            upper = jnp.where(
                right, gathered[block * 2 + layer, :, at], gathered[block * 2 + layer, :, beside]
            )
            lower = jnp.where(
                right, gathered[after * 2 + layer, :, at], gathered[after * 2 + layer, :, beside]
            )
            out[member, layer] = jnp.where(row_index >= residue, upper, lower)
        return carry

    lax.fori_loop(0, 32, one, 0, unroll=4)


def scatter_kernel(place, rows, cols, values, out):
    slab, first = place[0], place[1]
    row_index = first + lax.broadcasted_iota(jnp.int32, (8, CORE), 0)
    lane = lax.broadcasted_iota(jnp.int32, (8, CORE), 1)
    out[...] = jnp.zeros_like(out)

    def one(member, carry):
        patch = slab * 4 + member // 8
        frame = member % 8
        for layer in range(2):
            row = rows[frame, layer, patch]
            col = cols[frame, layer, patch]
            block, residue = row // CORE, row % CORE
            after = jnp.minimum(block + 1, 7)
            strip, turn = col // CORE, col % CORE
            beside = jnp.minimum(strip + 1, 15)
            value = values[member, layer]
            here = row_index >= residue
            right = lane >= turn
            for where, keep_row in ((block, here), (after, ~here)):
                for place_col, keep_col in ((strip, right), (beside, ~right)):
                    at = pl.ds(pl.multiple_of((place_col % 2) * CORE, CORE), CORE)
                    chunk = place_col // 2
                    out[where, chunk, layer, :, at] = out[where, chunk, layer, :, at] + jnp.where(
                        keep_row & keep_col, value, 0.0
                    )
        return carry

    lax.fori_loop(0, 32, one, 0, unroll=2)


def gradient_kernel(
    turns, received, amp_ref, observed, forward_h, forward_l, inverse_h, inverse_l, spec_re, spec_im,
    out, pupil_re, pupil_im, far_re, far_im, mix_h, mix_l, wide_h, wide_l,
):
    forward, inverse = Pair(forward_h, forward_l), Pair(inverse_h, inverse_l)
    mix, wide = Pair(mix_h, mix_l), Pair(wide_h, wide_l)
    phases = None
    for layer in range(2):
        sheet = received[:, layer].reshape(CORE, CORE)
        sheet = pltpu.roll(sheet, (CORE - turns[layer, 0]) % CORE, 0)
        sheet = pltpu.roll(sheet, (CORE - turns[layer, 1]) % CORE, 1)
        phases = sheet if phases is None else phases + sheet
    amplitude = amp_ref[...]
    inverse_total = 1.0 / (SPAN * SPAN * jnp.sum(amplitude * amplitude))
    sine, cosine = sine_cosine(phases)
    pupil_re[...] = amplitude * cosine
    pupil_im[...] = amplitude * sine
    half = product(forward[ALL, LOW], split(pupil_re[...])) + product(
        forward[ALL, HIGH], split(pupil_im[...])
    )
    half_re, half_im = split(half[FULL]), split(half[REST])
    far_re[...] = product(half_re, inverse[LOW, FULL]) + product(half_im, inverse[HIGH, FULL])
    far_im[...] = product(half_re, inverse[LOW, REST]) + product(half_im, inverse[HIGH, REST])
    spread = split((far_re[...] * far_re[...] + far_im[...] * far_im[...]) * inverse_total)
    mix.put((FULL, ALL), product(spread, inverse[FULL, LOW]))
    mix.put((REST, ALL), product(spread, inverse[FULL, HIGH]))
    spectrum = product(forward[ALL, ALL], mix[ALL, ALL])
    first, second = spectrum[FULL], spectrum[REST]
    mix.put((FULL, ALL), first * spec_re[...] - second * spec_im[...])
    mix.put((REST, ALL), first * spec_im[...] + second * spec_re[...])
    rows_re = split(product(inverse[LOW, ALL], mix[ALL, ALL]))
    rows_im = split(product(inverse[HIGH, ALL], mix[ALL, ALL]))
    model = product(rows_re, forward[LOW, LOW]) + product(rows_im, forward[HIGH, LOW])
    residual = split((model - observed[0]) * float(SPAN))
    grad_re = split(product(residual, inverse[LOW, LOW]))
    grad_im = split(product(residual, inverse[LOW, HIGH]))
    spectrum = product(forward[ALL, LOW], grad_re) + product(forward[ALL, HIGH], grad_im)
    first, second = spectrum[FULL], spectrum[REST]
    mix.put((FULL, ALL), first * spec_re[...] + second * spec_im[...])
    mix.put((REST, ALL), second * spec_re[...] - first * spec_im[...])
    wave = product(inverse[ALL, ALL], mix[ALL, ALL])
    spread_grad = product(split(wave[FULL]), forward[LOW, FULL]) + product(
        split(wave[REST]), forward[HIGH, FULL]
    )
    wide.put((FULL, ALL), far_re[...] * spread_grad)
    wide.put((REST, ALL), far_im[...] * spread_grad)
    back_re = split(product(inverse[LOW, ALL], wide[ALL, ALL]))
    back_im = split(product(inverse[HIGH, ALL], wide[ALL, ALL]))
    out_re = product(back_re, forward[FULL, LOW]) + product(back_im, forward[REST, LOW])
    out_im = product(back_re, forward[FULL, HIGH]) + product(back_im, forward[REST, HIGH])
    gradient = (2.0 * inverse_total) * (pupil_re[...] * out_im - pupil_im[...] * out_re)
    for layer in range(2):
        sheet = pltpu.roll(gradient, turns[layer, 1], 1)
        sheet = pltpu.roll(sheet, turns[layer, 0], 0)
        out[:, layer] = sheet.reshape(32, 8, CORE)


SMEM = pl.BlockSpec(memory_space=pltpu.SMEM)
VMEM = pl.BlockSpec(memory_space=pltpu.VMEM)


def cost(flops, moved):
    return pl.CostEstimate(flops=flops, bytes_accessed=moved, transcendentals=0)


def f32(*shape):
    return jax.ShapeDtypeStruct(shape, jnp.float32)


def body(screens, row_offsets, col_offsets, amplitude, object_strip, observed):
    slab = lax.axis_index("z")
    across = lax.axis_index("x")
    frame_id = lax.axis_index(FRAME)
    patch = slab * 4 + across
    patches = lax.axis_size("z") * lax.axis_size("x")
    rows = lax.dynamic_slice_in_dim(screens, frame_id * 8, 8, 1)
    gathered = lax.all_gather(rows, "z", axis=0, tiled=True)
    ends = patches - 1
    left_tail = lax.ppermute(
        object_strip[:, CORE - HALO :], ("z", "x"), [(i, i + 1) for i in range(ends)]
    )
    right_head = lax.ppermute(object_strip[:, :HALO], ("z", "x"), [(i + 1, i) for i in range(ends)])
    window = jnp.concatenate([object_strip, right_head, left_tail], axis=1)
    window = jnp.concatenate([window[HALO:], window[:HALO]], axis=0)
    constants = [jnp.asarray(part) for part in split_constants()]
    big = jax.ShapeDtypeStruct((2 * SPAN, 2 * SPAN), jnp.bfloat16)
    forward_h, forward_l, inverse_h, inverse_l, spec_re, spec_im = pl.pallas_call(
        object_kernel,
        out_shape=[big] * 4 + [f32(SPAN, HALF)] * 2,
        in_specs=[VMEM] * 5,
        out_specs=[VMEM] * 6,
        cost_estimate=cost(3 * 2 * 226 * 10**6, 7 * 10**6),
        name="object_spectrum",
    )(*constants, window)

    place = jnp.stack([slab, across * 64 + frame_id * 8]).astype(jnp.int32)
    sent = pl.pallas_call(
        select_kernel,
        out_shape=f32(32, 2, 8, CORE),
        in_specs=[SMEM] * 3 + [VMEM],
        out_specs=VMEM,
        cost_estimate=cost(0, 3 * 10**6),
        name="select_rows",
    )(place, row_offsets, col_offsets, gathered)
    received = lax.all_to_all(sent, SLAB, split_axis=0, concat_axis=0, tiled=True)

    row_turns = lax.dynamic_slice(row_offsets, (frame_id, 0, patch), (1, 2, 1))[0, :, 0] % CORE
    col_turns = lax.dynamic_slice(col_offsets, (frame_id, 0, patch), (1, 2, 1))[0, :, 0] % CORE
    turns = jnp.stack([row_turns, col_turns], axis=1)
    placed = pl.pallas_call(
        gradient_kernel,
        out_shape=f32(32, 2, 8, CORE),
        in_specs=[SMEM] + [VMEM] * 9,
        out_specs=VMEM,
        scratch_shapes=[
            pltpu.VMEM((CORE, CORE), jnp.float32),
            pltpu.VMEM((CORE, CORE), jnp.float32),
            pltpu.VMEM((SPAN, SPAN), jnp.float32),
            pltpu.VMEM((SPAN, SPAN), jnp.float32),
            pltpu.VMEM((2 * SPAN, HALF), jnp.bfloat16),
            pltpu.VMEM((2 * SPAN, HALF), jnp.bfloat16),
            pltpu.VMEM((2 * SPAN, SPAN), jnp.bfloat16),
            pltpu.VMEM((2 * SPAN, SPAN), jnp.bfloat16),
        ],
        cost_estimate=cost(3 * 2 * 1222 * 10**6, 7 * 10**6),
        name="gradient",
    )(turns, received, amplitude, observed, forward_h, forward_l, inverse_h, inverse_l, spec_re, spec_im)
    returned = lax.all_to_all(placed, SLAB, split_axis=0, concat_axis=0, tiled=True)

    partial = pl.pallas_call(
        scatter_kernel,
        out_shape=f32(8, 8, 2, 8, 512),
        in_specs=[SMEM] * 3 + [VMEM],
        out_specs=VMEM,
        cost_estimate=cost(0, 3 * 10**6),
        name="scatter_rows",
    )(place, row_offsets, col_offsets, returned)
    summed = lax.psum_scatter(partial, "z", scatter_dimension=0, tiled=False)
    turned = lax.all_to_all(summed, FRAME, split_axis=0, concat_axis=0, tiled=True)
    return turned.transpose(1, 0, 2, 3).reshape(2, 64, 512)


def solution(mesh):
    fine = Mesh(mesh.devices.reshape(8, 4, 4, 2), ("z", "x", "y", "core"))
    patch = ("z", "x")
    in_specs = (
        P(None, patch, None), P(), P(), P(), P(None, patch), P(FRAME, None, patch),
    )
    out_specs = P(None, patch, FRAME)
    return jax.shard_map(body, mesh=fine, in_specs=in_specs, out_specs=out_specs, check_vma=False)
```

```python
import functools
import math

import jax
import jax.numpy as jnp
from jax import lax
from jax.experimental import pallas as pl
from jax.experimental.pallas import tpu as pltpu
from jax.sharding import Mesh, PartitionSpec as P

CORE = 256
HALO = 64
SPAN = 384
HALF = 256
SLAB = ("x", "y", "core")
FRAME = ("y", "core")


def split(values):
    high = values.astype(jnp.bfloat16)
    low = (values - high.astype(jnp.float32)).astype(jnp.bfloat16)
    return high, low


def dot(left, right):
    return jnp.dot(left, right, preferred_element_type=jnp.float32)


def product(left, right):
    return dot(left[0], right[0]) + (dot(left[0], right[1]) + dot(left[1], right[0]))


class Pair:
    def __init__(self, high, low):
        self.refs = (high, low)

    def __getitem__(self, index):
        return tuple(ref[index] for ref in self.refs)

    def put(self, index, values):
        for ref, part in zip(self.refs, split(values)):
            ref[index] = part


def sine_cosine(angle):
    turns = jnp.round(angle * (2.0 / math.pi))
    rest = angle - turns * 1.5703125
    rest = rest - turns * 4.837512969970703125e-4
    rest = rest - turns * 7.549789948768648e-8
    square = rest * rest
    sine = rest + rest * square * (
        -1.6666654611e-1 + square * (8.3321608736e-3 + square * -1.9515295891e-4)
    )
    cosine = 1.0 - 0.5 * square + square * square * (
        4.166664568298827e-2 + square * (-1.388731625493765e-3 + square * 2.443315711809948e-5)
    )
    quarter = turns.astype(jnp.int32)
    odd = (quarter & 1) == 1
    sine, cosine = jnp.where(odd, cosine, sine), jnp.where(odd, sine, cosine)
    sine = jnp.where((quarter & 2) == 2, -sine, sine)
    cosine = jnp.where(((quarter + 1) & 2) == 2, -cosine, cosine)
    return sine, cosine


LOW = slice(0, CORE)
HIGH = slice(SPAN, SPAN + CORE)
FULL = slice(0, SPAN)
REST = slice(SPAN, 2 * SPAN)
ALL = slice(None)


def object_kernel(window, forward_h, forward_l, inverse_h, inverse_l, spec_re, spec_im):
    row = lax.broadcasted_iota(jnp.int32, (SPAN, SPAN), 0)
    column = lax.broadcasted_iota(jnp.int32, (SPAN, SPAN), 1)
    steps = (row * column).astype(jnp.float32)
    steps = steps - SPAN * jnp.floor((steps + 0.5) * (1.0 / SPAN))
    sine, cosine = sine_cosine(steps * (2.0 * math.pi / SPAN))
    for target_f, target_i, cosine, sine in zip(
        (forward_h, forward_l), (inverse_h, inverse_l), split(cosine), split(sine)
    ):
        target_f[FULL, FULL] = cosine
        target_f[FULL, REST] = sine
        target_f[REST, FULL] = -sine
        target_f[REST, REST] = cosine
        target_i[FULL, FULL] = cosine
        target_i[FULL, REST] = -sine
        target_i[REST, FULL] = sine
        target_i[REST, REST] = cosine
    forward, inverse = Pair(forward_h, forward_l), Pair(inverse_h, inverse_l)
    seen = split(window[...])
    part_re = split(product(seen, inverse[FULL, LOW]))
    part_im = split(product(seen, inverse[FULL, HIGH]))
    out = product(forward[ALL, FULL], part_re) + product(forward[ALL, REST], part_im)
    column = lax.broadcasted_iota(jnp.int32, (SPAN, HALF), 1)
    ends = (column == 0) | (column == SPAN // 2)
    weight = jnp.where(ends, 1.0, jnp.where(column < SPAN // 2, 2.0, 0.0)) / (SPAN * SPAN)
    spec_re[...] = out[FULL] * weight
    spec_im[...] = out[REST] * weight


def cut_kernel(place, screens, out, sem):
    at = pl.ds(pl.multiple_of(place[2], 8), 8)
    copy = pltpu.make_async_copy(screens.at[:, at, :], out, sem)
    copy.start()
    copy.wait()


def select_kernel(place, rows, cols, *refs):
    chunks, out, gathered = refs[:9], refs[9], refs[10]
    slab, first = place[0], place[1]
    for step, chunk in zip((0, 1, 2, 3, 5, 6, 7), chunks):
        source = (slab + step) % 8
        gathered[pl.ds(source * 2, 2)] = chunk[...]
    source = (slab + 4) % 8
    gathered[pl.ds(source * 2, 1)] = chunks[7][...]
    gathered[pl.ds(source * 2 + 1, 1)] = chunks[8][...]
    row_index = first + lax.broadcasted_iota(jnp.int32, (8, CORE), 0)
    lane = lax.broadcasted_iota(jnp.int32, (8, CORE), 1)

    def one(member, carry):
        patch = slab * 4 + member // 8
        frame = member % 8
        for layer in range(2):
            row = rows[frame, layer, patch]
            col = cols[frame, layer, patch]
            block, residue = row // CORE, row % CORE
            after = jnp.minimum(block + 1, 7)
            strip, turn = col // CORE, col % CORE
            at = pl.ds(pl.multiple_of(strip * CORE, CORE), CORE)
            beside = pl.ds(pl.multiple_of(jnp.minimum(strip + 1, 15) * CORE, CORE), CORE)
            right = lane >= turn
            upper = jnp.where(
                right, gathered[block * 2 + layer, :, at], gathered[block * 2 + layer, :, beside]
            )
            lower = jnp.where(
                right, gathered[after * 2 + layer, :, at], gathered[after * 2 + layer, :, beside]
            )
            out[member, layer] = jnp.where(row_index >= residue, upper, lower)
        return carry

    lax.fori_loop(0, 32, one, 0, unroll=4)


def scatter_kernel(place, rows, cols, values, out, above, below):
    slab, first = place[0], place[1]
    row_index = first + lax.broadcasted_iota(jnp.int32, (8, CORE), 0)
    lane = lax.broadcasted_iota(jnp.int32, (8, CORE), 1)
    out[...] = jnp.zeros_like(out)

    def one(member, carry):
        patch = slab * 4 + member // 8
        frame = member % 8
        for layer in range(2):
            row = rows[frame, layer, patch]
            col = cols[frame, layer, patch]
            block, residue = row // CORE, row % CORE
            after = jnp.minimum(block + 1, 7)
            strip, turn = col // CORE, col % CORE
            beside = jnp.minimum(strip + 1, 15)
            value = values[member, layer]
            here = row_index >= residue
            right = lane >= turn
            for target, keep_row in ((block, here), (after, ~here)):
                where = (target + 8 - slab) % 8
                for place_col, keep_col in ((strip, right), (beside, ~right)):
                    at = pl.ds(pl.multiple_of((place_col % 2) * CORE, CORE), CORE)
                    chunk = place_col // 2
                    out[where, chunk, layer, :, at] = out[where, chunk, layer, :, at] + jnp.where(
                        keep_row & keep_col, value, 0.0
                    )
        return carry

    lax.fori_loop(0, 32, one, 0, unroll=2)
    above[...] = out[4, 0:4]
    below[...] = out[4, 4:8]


def gradient_kernel(
    turns, received, amp_ref, observed, forward_h, forward_l, inverse_h, inverse_l, spec_re, spec_im,
    out, pupil_re, pupil_im, far_re, far_im, mix_h, mix_l, wide_h, wide_l,
):
    forward, inverse = Pair(forward_h, forward_l), Pair(inverse_h, inverse_l)
    mix, wide = Pair(mix_h, mix_l), Pair(wide_h, wide_l)
    phases = None
    for layer in range(2):
        sheet = received[:, layer].reshape(CORE, CORE)
        sheet = pltpu.roll(sheet, (CORE - turns[layer, 0]) % CORE, 0)
        sheet = pltpu.roll(sheet, (CORE - turns[layer, 1]) % CORE, 1)
        phases = sheet if phases is None else phases + sheet
    amplitude = amp_ref[...]
    inverse_total = 1.0 / (SPAN * SPAN * jnp.sum(amplitude * amplitude))
    sine, cosine = sine_cosine(phases)
    pupil_re[...] = amplitude * cosine
    pupil_im[...] = amplitude * sine
    half = product(forward[ALL, LOW], split(pupil_re[...])) + product(
        forward[ALL, HIGH], split(pupil_im[...])
    )
    half_re, half_im = split(half[FULL]), split(half[REST])
    far_re[...] = product(half_re, inverse[LOW, FULL]) + product(half_im, inverse[HIGH, FULL])
    far_im[...] = product(half_re, inverse[LOW, REST]) + product(half_im, inverse[HIGH, REST])
    spread = split((far_re[...] * far_re[...] + far_im[...] * far_im[...]) * inverse_total)
    mix.put((FULL, ALL), product(spread, inverse[FULL, LOW]))
    mix.put((REST, ALL), product(spread, inverse[FULL, HIGH]))
    spectrum = product(forward[ALL, ALL], mix[ALL, ALL])
    first, second = spectrum[FULL], spectrum[REST]
    mix.put((FULL, ALL), first * spec_re[...] - second * spec_im[...])
    mix.put((REST, ALL), first * spec_im[...] + second * spec_re[...])
    rows_re = split(product(inverse[LOW, ALL], mix[ALL, ALL]))
    rows_im = split(product(inverse[HIGH, ALL], mix[ALL, ALL]))
    model = product(rows_re, forward[LOW, LOW]) + product(rows_im, forward[HIGH, LOW])
    residual = split((model - observed[0]) * float(SPAN))
    grad_re = split(product(residual, inverse[LOW, LOW]))
    grad_im = split(product(residual, inverse[LOW, HIGH]))
    spectrum = product(forward[ALL, LOW], grad_re) + product(forward[ALL, HIGH], grad_im)
    first, second = spectrum[FULL], spectrum[REST]
    mix.put((FULL, ALL), first * spec_re[...] + second * spec_im[...])
    mix.put((REST, ALL), second * spec_re[...] - first * spec_im[...])
    wave = product(inverse[ALL, ALL], mix[ALL, ALL])
    spread_grad = product(split(wave[FULL]), forward[LOW, FULL]) + product(
        split(wave[REST]), forward[HIGH, FULL]
    )
    wide.put((FULL, ALL), far_re[...] * spread_grad)
    wide.put((REST, ALL), far_im[...] * spread_grad)
    back_re = split(product(inverse[LOW, ALL], wide[ALL, ALL]))
    back_im = split(product(inverse[HIGH, ALL], wide[ALL, ALL]))
    out_re = product(back_re, forward[FULL, LOW]) + product(back_im, forward[REST, LOW])
    out_im = product(back_re, forward[FULL, HIGH]) + product(back_im, forward[REST, HIGH])
    gradient = (2.0 * inverse_total) * (pupil_re[...] * out_im - pupil_im[...] * out_re)
    for layer in range(2):
        sheet = pltpu.roll(gradient, turns[layer, 1], 1)
        sheet = pltpu.roll(sheet, turns[layer, 0], 0)
        out[:, layer] = sheet.reshape(32, 8, CORE)


SMEM = pl.BlockSpec(memory_space=pltpu.SMEM)
VMEM = pl.BlockSpec(memory_space=pltpu.VMEM)


def limit(mib):
    return pltpu.CompilerParams(vmem_limit_bytes=mib << 20)


def cost(flops, moved):
    return pl.CostEstimate(flops=flops, bytes_accessed=moved, transcendentals=0)


def f32(*shape):
    return jax.ShapeDtypeStruct(shape, jnp.float32)


def up(values):
    count = lax.axis_size("z")
    return lax.ppermute(values, "z", [(i, (i + 1) % count) for i in range(count)])


def down(values):
    count = lax.axis_size("z")
    return lax.ppermute(values, "z", [((i + 1) % count, i) for i in range(count)])


def ring_gather(own):
    rise, fall = [own], [own]
    for _ in range(3):
        rise.append(up(rise[-1]))
        fall.append(down(fall[-1]))
    halves = [up(rise[3][0:1]), down(fall[3][1:2])]
    return fall + [rise[3], rise[2], rise[1]] + halves


def ring_scatter(partial, above, below):
    above = up(above)
    below = down(below)
    rise = jnp.concatenate([partial[3, :4] + above, partial[3, 4:]])
    fall = jnp.concatenate([partial[5, :4], partial[5, 4:] + below])
    for step in (2, 1, 0):
        rise = up(rise)
        fall = down(fall)
        if step:
            rise = rise + partial[step]
            fall = fall + partial[8 - step]
    return partial[0] + rise + fall


def body(screens, row_offsets, col_offsets, amplitude, object_strip, observed):
    slab = lax.axis_index("z")
    across = lax.axis_index("x")
    frame_id = lax.axis_index(FRAME)
    patch = slab * 4 + across
    patches = lax.axis_size("z") * lax.axis_size("x")
    place = jnp.stack([slab, across * 64 + frame_id * 8, frame_id * 8]).astype(jnp.int32)
    own = pl.pallas_call(
        cut_kernel,
        out_shape=f32(2, 8, screens.shape[2]),
        in_specs=[SMEM, pl.BlockSpec(memory_space=pltpu.HBM)],
        out_specs=VMEM,
        scratch_shapes=[pltpu.SemaphoreType.DMA],
        compiler_params=limit(61),
        name="cut_rows",
    )(place, screens)
    chunks = ring_gather(own)
    ends = patches - 1
    left_tail = lax.ppermute(
        object_strip[:, CORE - HALO :], ("z", "x"), [(i, i + 1) for i in range(ends)]
    )
    right_head = lax.ppermute(object_strip[:, :HALO], ("z", "x"), [(i + 1, i) for i in range(ends)])
    window = jnp.concatenate([object_strip, right_head, left_tail], axis=1)
    window = jnp.concatenate([window[HALO:], window[:HALO]], axis=0)
    big = jax.ShapeDtypeStruct((2 * SPAN, 2 * SPAN), jnp.bfloat16)
    forward_h, forward_l, inverse_h, inverse_l, spec_re, spec_im = pl.pallas_call(
        object_kernel,
        out_shape=[big] * 4 + [f32(SPAN, HALF)] * 2,
        in_specs=[VMEM],
        out_specs=[VMEM] * 6,
        compiler_params=limit(20),
        cost_estimate=cost(3 * 2 * 226 * 10**6, 7 * 10**6),
        name="object_spectrum",
    )(window)

    sent = pl.pallas_call(
        select_kernel,
        out_shape=f32(32, 2, 8, CORE),
        in_specs=[SMEM] * 3 + [VMEM] * 9,
        out_specs=VMEM,
        scratch_shapes=[pltpu.VMEM((16, 8, screens.shape[2]), jnp.float32)],
        compiler_params=limit(20),
        cost_estimate=cost(0, 3 * 10**6),
        name="select_rows",
    )(place, row_offsets, col_offsets, *chunks)
    received = lax.all_to_all(sent, SLAB, split_axis=0, concat_axis=0, tiled=True)

    row_turns = lax.dynamic_slice(row_offsets, (frame_id, 0, patch), (1, 2, 1))[0, :, 0] % CORE
    col_turns = lax.dynamic_slice(col_offsets, (frame_id, 0, patch), (1, 2, 1))[0, :, 0] % CORE
    turns = jnp.stack([row_turns, col_turns], axis=1)
    placed = pl.pallas_call(
        gradient_kernel,
        out_shape=f32(32, 2, 8, CORE),
        in_specs=[SMEM] + [VMEM] * 9,
        out_specs=VMEM,
        scratch_shapes=[
            pltpu.VMEM((CORE, CORE), jnp.float32),
            pltpu.VMEM((CORE, CORE), jnp.float32),
            pltpu.VMEM((SPAN, SPAN), jnp.float32),
            pltpu.VMEM((SPAN, SPAN), jnp.float32),
            pltpu.VMEM((2 * SPAN, HALF), jnp.bfloat16),
            pltpu.VMEM((2 * SPAN, HALF), jnp.bfloat16),
            pltpu.VMEM((2 * SPAN, SPAN), jnp.bfloat16),
            pltpu.VMEM((2 * SPAN, SPAN), jnp.bfloat16),
        ],
        compiler_params=limit(20),
        cost_estimate=cost(3 * 2 * 1222 * 10**6, 7 * 10**6),
        name="gradient",
    )(turns, received, amplitude, observed, forward_h, forward_l, inverse_h, inverse_l, spec_re, spec_im)
    returned = lax.all_to_all(placed, SLAB, split_axis=0, concat_axis=0, tiled=True)

    partial, above, below = pl.pallas_call(
        scatter_kernel,
        out_shape=[f32(8, 8, 2, 8, 512)] + [f32(4, 2, 8, 512)] * 2,
        in_specs=[SMEM] * 3 + [VMEM],
        out_specs=[VMEM] * 3,
        compiler_params=limit(20),
        cost_estimate=cost(0, 3 * 10**6),
        name="scatter_rows",
    )(place, row_offsets, col_offsets, returned)
    summed = ring_scatter(partial, above, below)
    turned = lax.all_to_all(summed, FRAME, split_axis=0, concat_axis=0, tiled=True)
    return turned.transpose(1, 0, 2, 3).reshape(2, 64, 512)


def solution(mesh):
    fine = Mesh(mesh.devices.reshape(8, 4, 4, 2), ("z", "x", "y", "core"))
    patch = ("z", "x")
    in_specs = (
        P(None, patch, None), P(), P(), P(), P(None, patch), P(FRAME, None, patch),
    )
    out_specs = P(None, patch, FRAME)
    return jax.shard_map(body, mesh=fine, in_specs=in_specs, out_specs=out_specs, check_vma=False)
```

```python
import functools
import math

import jax
import jax.numpy as jnp
from jax import lax
from jax.experimental import pallas as pl
from jax.experimental.pallas import tpu as pltpu
from jax.sharding import Mesh, PartitionSpec as P

CORE = 256
HALO = 64
SPAN = 384
HALF = 256
SLAB = ("x", "y", "core")
FRAME = ("y", "core")


def split(values):
    high = values.astype(jnp.bfloat16)
    low = (values - high.astype(jnp.float32)).astype(jnp.bfloat16)
    return high, low


def dot(left, right):
    return jnp.dot(left, right, preferred_element_type=jnp.float32)


def product(left, right):
    return dot(left[0], right[0]) + (dot(left[0], right[1]) + dot(left[1], right[0]))


class Pair:
    def __init__(self, high, low):
        self.refs = (high, low)

    def __getitem__(self, index):
        return tuple(ref[index] for ref in self.refs)

    def put(self, index, values):
        for ref, part in zip(self.refs, split(values)):
            ref[index] = part


def sine_cosine(angle):
    turns = jnp.round(angle * (2.0 / math.pi))
    rest = angle - turns * 1.5703125
    rest = rest - turns * 4.837512969970703125e-4
    rest = rest - turns * 7.549789948768648e-8
    square = rest * rest
    sine = rest + rest * square * (
        -1.6666654611e-1 + square * (8.3321608736e-3 + square * -1.9515295891e-4)
    )
    cosine = 1.0 - 0.5 * square + square * square * (
        4.166664568298827e-2 + square * (-1.388731625493765e-3 + square * 2.443315711809948e-5)
    )
    quarter = turns.astype(jnp.int32)
    odd = (quarter & 1) == 1
    sine, cosine = jnp.where(odd, cosine, sine), jnp.where(odd, sine, cosine)
    sine = jnp.where((quarter & 2) == 2, -sine, sine)
    cosine = jnp.where(((quarter + 1) & 2) == 2, -cosine, cosine)
    return sine, cosine


LOW = slice(0, CORE)
HIGH = slice(SPAN, SPAN + CORE)
FULL = slice(0, SPAN)
REST = slice(SPAN, 2 * SPAN)
ALL = slice(None)


def object_kernel(window, forward_h, forward_l, inverse_h, inverse_l, spec_re, spec_im):
    row = lax.broadcasted_iota(jnp.int32, (SPAN, SPAN), 0)
    column = lax.broadcasted_iota(jnp.int32, (SPAN, SPAN), 1)
    steps = (row * column).astype(jnp.float32)
    steps = steps - SPAN * jnp.floor((steps + 0.5) * (1.0 / SPAN))
    sine, cosine = sine_cosine(steps * (2.0 * math.pi / SPAN))
    for target_f, target_i, cosine, sine in zip(
        (forward_h, forward_l), (inverse_h, inverse_l), split(cosine), split(sine)
    ):
        target_f[FULL, FULL] = cosine
        target_f[FULL, REST] = sine
        target_f[REST, FULL] = -sine
        target_f[REST, REST] = cosine
        target_i[FULL, FULL] = cosine
        target_i[FULL, REST] = -sine
        target_i[REST, FULL] = sine
        target_i[REST, REST] = cosine
    forward, inverse = Pair(forward_h, forward_l), Pair(inverse_h, inverse_l)
    seen = split(window[...])
    part_re = split(product(seen, inverse[FULL, LOW]))
    part_im = split(product(seen, inverse[FULL, HIGH]))
    out = product(forward[ALL, FULL], part_re) + product(forward[ALL, REST], part_im)
    column = lax.broadcasted_iota(jnp.int32, (SPAN, HALF), 1)
    ends = (column == 0) | (column == SPAN // 2)
    weight = jnp.where(ends, 1.0, jnp.where(column < SPAN // 2, 2.0, 0.0)) / (SPAN * SPAN)
    spec_re[...] = out[FULL] * weight
    spec_im[...] = out[REST] * weight


def cut_kernel(place, screens, out, sem):
    at = pl.ds(pl.multiple_of(place[2], 8), 8)
    copy = pltpu.make_async_copy(screens.at[:, at, :], out, sem)
    copy.start()
    copy.wait()


def select_kernel(place, rows, cols, *refs):
    chunks, out, gathered = refs[:9], refs[9], refs[10]
    slab, first = place[0], place[1]
    for step, chunk in zip((0, 1, 2, 3, 5, 6, 7), chunks):
        source = (slab + step) % 8
        gathered[pl.ds(source * 2, 2)] = chunk[...]
    source = (slab + 4) % 8
    gathered[pl.ds(source * 2, 1)] = chunks[7][...]
    gathered[pl.ds(source * 2 + 1, 1)] = chunks[8][...]
    row_index = first + lax.broadcasted_iota(jnp.int32, (8, CORE), 0)
    lane = lax.broadcasted_iota(jnp.int32, (8, CORE), 1)

    def one(member, carry):
        patch = slab * 4 + member // 8
        frame = member % 8
        for layer in range(2):
            row = rows[frame, layer, patch]
            col = cols[frame, layer, patch]
            block, residue = row // CORE, row % CORE
            after = jnp.minimum(block + 1, 7)
            strip, turn = col // CORE, col % CORE
            at = pl.ds(pl.multiple_of(strip * CORE, CORE), CORE)
            beside = pl.ds(pl.multiple_of(jnp.minimum(strip + 1, 15) * CORE, CORE), CORE)
            right = lane >= turn
            upper = jnp.where(
                right, gathered[block * 2 + layer, :, at], gathered[block * 2 + layer, :, beside]
            )
            lower = jnp.where(
                right, gathered[after * 2 + layer, :, at], gathered[after * 2 + layer, :, beside]
            )
            out[member, layer] = jnp.where(row_index >= residue, upper, lower)
        return carry

    lax.fori_loop(0, 32, one, 0, unroll=4)


def scatter_kernel(place, rows, cols, values, out, above, below):
    slab, first = place[0], place[1]
    row_index = first + lax.broadcasted_iota(jnp.int32, (8, CORE), 0)
    lane = lax.broadcasted_iota(jnp.int32, (8, CORE), 1)
    out[...] = jnp.zeros_like(out)

    def one(member, carry):
        patch = slab * 4 + member // 8
        frame = member % 8
        for layer in range(2):
            row = rows[frame, layer, patch]
            col = cols[frame, layer, patch]
            block, residue = row // CORE, row % CORE
            after = jnp.minimum(block + 1, 7)
            strip, turn = col // CORE, col % CORE
            beside = jnp.minimum(strip + 1, 15)
            value = values[member, layer]
            here = row_index >= residue
            right = lane >= turn
            for target, keep_row in ((block, here), (after, ~here)):
                where = (target + 8 - slab) % 8
                for place_col, keep_col in ((strip, right), (beside, ~right)):
                    at = pl.ds(pl.multiple_of((place_col % 2) * CORE, CORE), CORE)
                    chunk = place_col // 2
                    out[where, chunk, layer, :, at] = out[where, chunk, layer, :, at] + jnp.where(
                        keep_row & keep_col, value, 0.0
                    )
        return carry

    lax.fori_loop(0, 32, one, 0, unroll=2)
    above[...] = out[4, 0:4]
    below[...] = out[4, 4:8]


def gradient_kernel(
    turns, received, amp_ref, observed, far_fh, far_fl, far_ih, far_il, spec_re, spec_im, out,
    forward_h, forward_l, inverse_h, inverse_l, pupil_re, pupil_im, far_re, far_im,
    mix_h, mix_l, wide_h, wide_l, sems,
):
    copies = [
        pltpu.make_async_copy(source, target, sems.at[index])
        for index, (source, target) in enumerate(
            (
                (far_fh, forward_h), (far_fl, forward_l), (far_ih, inverse_h), (far_il, inverse_l),
            )
        )
    ]
    for copy in copies:
        copy.start()
    forward, inverse = Pair(forward_h, forward_l), Pair(inverse_h, inverse_l)
    mix, wide = Pair(mix_h, mix_l), Pair(wide_h, wide_l)
    phases = None
    for layer in range(2):
        sheet = received[:, layer].reshape(CORE, CORE)
        sheet = pltpu.roll(sheet, (CORE - turns[layer, 0]) % CORE, 0)
        sheet = pltpu.roll(sheet, (CORE - turns[layer, 1]) % CORE, 1)
        phases = sheet if phases is None else phases + sheet
    amplitude = amp_ref[...]
    inverse_total = 1.0 / (SPAN * SPAN * jnp.sum(amplitude * amplitude))
    sine, cosine = sine_cosine(phases)
    pupil_re[...] = amplitude * cosine
    pupil_im[...] = amplitude * sine
    for copy in copies:
        copy.wait()
    half = product(forward[ALL, LOW], split(pupil_re[...])) + product(
        forward[ALL, HIGH], split(pupil_im[...])
    )
    half_re, half_im = split(half[FULL]), split(half[REST])
    far_re[...] = product(half_re, inverse[LOW, FULL]) + product(half_im, inverse[HIGH, FULL])
    far_im[...] = product(half_re, inverse[LOW, REST]) + product(half_im, inverse[HIGH, REST])
    spread = split((far_re[...] * far_re[...] + far_im[...] * far_im[...]) * inverse_total)
    mix.put((FULL, ALL), product(spread, inverse[FULL, LOW]))
    mix.put((REST, ALL), product(spread, inverse[FULL, HIGH]))
    spectrum = product(forward[ALL, ALL], mix[ALL, ALL])
    first, second = spectrum[FULL], spectrum[REST]
    mix.put((FULL, ALL), first * spec_re[...] - second * spec_im[...])
    mix.put((REST, ALL), first * spec_im[...] + second * spec_re[...])
    rows_re = split(product(inverse[LOW, ALL], mix[ALL, ALL]))
    rows_im = split(product(inverse[HIGH, ALL], mix[ALL, ALL]))
    model = product(rows_re, forward[LOW, LOW]) + product(rows_im, forward[HIGH, LOW])
    residual = split((model - observed[0]) * float(SPAN))
    grad_re = split(product(residual, inverse[LOW, LOW]))
    grad_im = split(product(residual, inverse[LOW, HIGH]))
    spectrum = product(forward[ALL, LOW], grad_re) + product(forward[ALL, HIGH], grad_im)
    first, second = spectrum[FULL], spectrum[REST]
    mix.put((FULL, ALL), first * spec_re[...] + second * spec_im[...])
    mix.put((REST, ALL), second * spec_re[...] - first * spec_im[...])
    wave = product(inverse[ALL, ALL], mix[ALL, ALL])
    spread_grad = product(split(wave[FULL]), forward[LOW, FULL]) + product(
        split(wave[REST]), forward[HIGH, FULL]
    )
    wide.put((FULL, ALL), far_re[...] * spread_grad)
    wide.put((REST, ALL), far_im[...] * spread_grad)
    back_re = split(product(inverse[LOW, ALL], wide[ALL, ALL]))
    back_im = split(product(inverse[HIGH, ALL], wide[ALL, ALL]))
    out_re = product(back_re, forward[FULL, LOW]) + product(back_im, forward[REST, LOW])
    out_im = product(back_re, forward[FULL, HIGH]) + product(back_im, forward[REST, HIGH])
    gradient = (2.0 * inverse_total) * (pupil_re[...] * out_im - pupil_im[...] * out_re)
    for layer in range(2):
        sheet = pltpu.roll(gradient, turns[layer, 1], 1)
        sheet = pltpu.roll(sheet, turns[layer, 0], 0)
        out[:, layer] = sheet.reshape(32, 8, CORE)


SMEM = pl.BlockSpec(memory_space=pltpu.SMEM)
VMEM = pl.BlockSpec(memory_space=pltpu.VMEM)
ANY = pl.BlockSpec(memory_space=pl.ANY)


def limit(mib):
    return pltpu.CompilerParams(vmem_limit_bytes=mib << 20)


def cost(flops, moved):
    return pl.CostEstimate(flops=flops, bytes_accessed=moved, transcendentals=0)


def f32(*shape):
    return jax.ShapeDtypeStruct(shape, jnp.float32)


def gradient_call(*operands, name="gradient"):
    return pl.pallas_call(
        gradient_kernel,
        out_shape=f32(32, 2, 8, CORE),
        in_specs=[SMEM] + [VMEM] * 3 + [ANY] * 4 + [VMEM] * 2,
        out_specs=VMEM,
        scratch_shapes=[
            pltpu.VMEM((2 * SPAN, 2 * SPAN), jnp.bfloat16),
            pltpu.VMEM((2 * SPAN, 2 * SPAN), jnp.bfloat16),
            pltpu.VMEM((2 * SPAN, 2 * SPAN), jnp.bfloat16),
            pltpu.VMEM((2 * SPAN, 2 * SPAN), jnp.bfloat16),
            pltpu.VMEM((CORE, CORE), jnp.float32),
            pltpu.VMEM((CORE, CORE), jnp.float32),
            pltpu.VMEM((SPAN, SPAN), jnp.float32),
            pltpu.VMEM((SPAN, SPAN), jnp.float32),
            pltpu.VMEM((2 * SPAN, HALF), jnp.bfloat16),
            pltpu.VMEM((2 * SPAN, HALF), jnp.bfloat16),
            pltpu.VMEM((2 * SPAN, SPAN), jnp.bfloat16),
            pltpu.VMEM((2 * SPAN, SPAN), jnp.bfloat16),
            pltpu.SemaphoreType.DMA((4,)),
        ],
        compiler_params=limit(61),
        cost_estimate=cost(3 * 2 * 1222 * 10**6, 7 * 10**6),
        name=name,
    )(*operands)


def up(values):
    count = lax.axis_size("z")
    return lax.ppermute(values, "z", [(i, (i + 1) % count) for i in range(count)])


def down(values):
    count = lax.axis_size("z")
    return lax.ppermute(values, "z", [((i + 1) % count, i) for i in range(count)])


def ring_gather(own, beside):
    rise, fall = [own], [own]
    for step in range(3):
        rise.append(up(rise[-1]))
        fall.append(down(fall[-1]))
    rise[3], fall[3], beside = lax.optimization_barrier((rise[3], fall[3], beside))
    halves = [up(rise[3][0:1]), down(fall[3][1:2])]
    return fall + [rise[3], rise[2], rise[1]] + halves, beside


def ring_scatter(partial, above, below):
    above = up(above)
    below = down(below)
    rise = jnp.concatenate([partial[3, :4] + above, partial[3, 4:]])
    fall = jnp.concatenate([partial[5, :4], partial[5, 4:] + below])
    for step in (2, 1, 0):
        rise = up(rise)
        fall = down(fall)
        if step:
            rise = rise + partial[step]
            fall = fall + partial[8 - step]
    return partial[0] + rise + fall


def body(screens, row_offsets, col_offsets, amplitude, object_strip, observed):
    slab = lax.axis_index("z")
    across = lax.axis_index("x")
    frame_id = lax.axis_index(FRAME)
    patch = slab * 4 + across
    patches = lax.axis_size("z") * lax.axis_size("x")
    place = jnp.stack([slab, across * 64 + frame_id * 8, frame_id * 8]).astype(jnp.int32)
    own = pl.pallas_call(
        cut_kernel,
        out_shape=f32(2, 8, screens.shape[2]),
        in_specs=[SMEM, ANY],
        out_specs=VMEM,
        scratch_shapes=[pltpu.SemaphoreType.DMA],
        compiler_params=limit(61),
        name="cut_rows",
    )(place, screens)
    ends = patches - 1
    own, strip = lax.optimization_barrier((own, object_strip))
    left_tail = lax.ppermute(
        strip[:, CORE - HALO :], ("z", "x"), [(i, i + 1) for i in range(ends)]
    )
    right_head = lax.ppermute(strip[:, :HALO], ("z", "x"), [(i + 1, i) for i in range(ends)])
    window = jnp.concatenate([object_strip, right_head, left_tail], axis=1)
    window = jnp.concatenate([window[HALO:], window[:HALO]], axis=0)
    big = jax.ShapeDtypeStruct((2 * SPAN, 2 * SPAN), jnp.bfloat16)
    object_parts = pl.pallas_call(
        object_kernel,
        out_shape=[big] * 4 + [f32(SPAN, HALF)] * 2,
        in_specs=[VMEM],
        out_specs=[VMEM] * 6,
        compiler_params=limit(61),
        cost_estimate=cost(3 * 2 * 226 * 10**6, 7 * 10**6),
        name="object_spectrum",
    )(window)

    chunks, object_parts = ring_gather(own, object_parts)
    forward_h, forward_l, inverse_h, inverse_l, spec_re, spec_im = object_parts
    sent = pl.pallas_call(
        select_kernel,
        out_shape=f32(32, 2, 8, CORE),
        in_specs=[SMEM] * 3 + [VMEM] * 9,
        out_specs=VMEM,
        scratch_shapes=[pltpu.VMEM((16, 8, screens.shape[2]), jnp.float32)],
        compiler_params=limit(20),
        cost_estimate=cost(0, 3 * 10**6),
        name="select_rows",
    )(place, row_offsets, col_offsets, *chunks)
    received = lax.all_to_all(sent, SLAB, split_axis=0, concat_axis=0, tiled=True)

    row_turns = lax.dynamic_slice(row_offsets, (frame_id, 0, patch), (1, 2, 1))[0, :, 0] % CORE
    col_turns = lax.dynamic_slice(col_offsets, (frame_id, 0, patch), (1, 2, 1))[0, :, 0] % CORE
    turns = jnp.stack([row_turns, col_turns], axis=1)
    placed = gradient_call(
        turns, received, amplitude, observed, forward_h, forward_l, inverse_h, inverse_l, spec_re, spec_im
    )
    returned = lax.all_to_all(placed, SLAB, split_axis=0, concat_axis=0, tiled=True)

    partial, above, below = pl.pallas_call(
        scatter_kernel,
        out_shape=[f32(8, 8, 2, 8, 512)] + [f32(4, 2, 8, 512)] * 2,
        in_specs=[SMEM] * 3 + [VMEM],
        out_specs=[VMEM] * 3,
        compiler_params=limit(20),
        cost_estimate=cost(0, 3 * 10**6),
        name="scatter_rows",
    )(place, row_offsets, col_offsets, returned)
    summed = ring_scatter(partial, above, below)
    turned = lax.all_to_all(summed, FRAME, split_axis=0, concat_axis=0, tiled=True)
    return turned.transpose(1, 0, 2, 3).reshape(2, 64, 512)


def solution(mesh):
    fine = Mesh(mesh.devices.reshape(8, 4, 4, 2), ("z", "x", "y", "core"))
    patch = ("z", "x")
    in_specs = (
        P(None, patch, None), P(), P(), P(), P(None, patch), P(FRAME, None, patch),
    )
    out_specs = P(None, patch, FRAME)
    return jax.shard_map(body, mesh=fine, in_specs=in_specs, out_specs=out_specs, check_vma=False)
```

```python
import functools
import math

import jax
import jax.numpy as jnp
from jax import lax
from jax.experimental import pallas as pl
from jax.experimental.pallas import tpu as pltpu
from jax.sharding import Mesh, PartitionSpec as P

CORE = 256
HALO = 64
SPAN = 384
HALF = 256
SLAB = ("x", "y", "core")
FRAME = ("y", "core")


def split(values):
    high = values.astype(jnp.bfloat16)
    low = (values - high.astype(jnp.float32)).astype(jnp.bfloat16)
    return high, low


def dot(left, right):
    return jnp.dot(left, right, preferred_element_type=jnp.float32)


def product(left, right):
    return dot(left[0], right[0]) + (dot(left[0], right[1]) + dot(left[1], right[0]))


def left(matrix, rows, parts):
    stacked, extra = None, None
    for lanes, (high, low) in parts:
        four = matrix[:, 0:rows, lanes].reshape(4 * rows, high.shape[0])
        term, small = dot(four, high), dot(four[0 : 2 * rows], low)
        stacked = term if stacked is None else stacked + term
        extra = small if extra is None else extra + small
    real = stacked[0:rows] + (stacked[2 * rows : 3 * rows] + extra[0:rows])
    imag = stacked[rows : 2 * rows] + (stacked[3 * rows : 4 * rows] + extra[rows : 2 * rows])
    return real, imag


def right(parts, matrix, lanes):
    stacked, extra = None, None
    for part, (high, low) in enumerate(parts):
        depth = high.shape[1]
        term = dot(jnp.concatenate([high, low], axis=0), matrix[part, 0:depth, lanes])
        small = dot(high, matrix[2 + part, 0:depth, lanes])
        stacked = term if stacked is None else stacked + term
        extra = small if extra is None else extra + small
    rows = extra.shape[0]
    return stacked[0:rows] + (stacked[rows : 2 * rows] + extra)


def build(matrix, base, sign):
    for part in range(2):
        cosine, sine = base[2 * part], base[2 * part + 1]
        matrix[2 * part, :, FULL] = cosine
        matrix[2 * part, :, REST] = sine if sign > 0 else -sine
        matrix[2 * part + 1, :, FULL] = -sine if sign > 0 else sine
        matrix[2 * part + 1, :, REST] = cosine


def sine_cosine(angle):
    turns = jnp.round(angle * (2.0 / math.pi))
    rest = angle - turns * 1.5703125
    rest = rest - turns * 4.837512969970703125e-4
    rest = rest - turns * 7.549789948768648e-8
    square = rest * rest
    sine = rest + rest * square * (
        -1.6666654611e-1 + square * (8.3321608736e-3 + square * -1.9515295891e-4)
    )
    cosine = 1.0 - 0.5 * square + square * square * (
        4.166664568298827e-2 + square * (-1.388731625493765e-3 + square * 2.443315711809948e-5)
    )
    quarter = turns.astype(jnp.int32)
    odd = (quarter & 1) == 1
    sine, cosine = jnp.where(odd, cosine, sine), jnp.where(odd, sine, cosine)
    sine = jnp.where((quarter & 2) == 2, -sine, sine)
    cosine = jnp.where(((quarter + 1) & 2) == 2, -cosine, cosine)
    return sine, cosine


LOW = slice(0, CORE)
HIGH = slice(SPAN, SPAN + CORE)
FULL = slice(0, SPAN)
REST = slice(SPAN, 2 * SPAN)
ALL = slice(None)


def object_kernel(window, base, spec_re, spec_im, forward, inverse):
    block = SPAN // 8
    row = lax.broadcasted_iota(jnp.int32, (block, SPAN), 0)
    column = lax.broadcasted_iota(jnp.int32, (block, SPAN), 1)

    def fill(index, carry):
        begin = pl.multiple_of(index * block, block)
        steps = ((row + begin) * column).astype(jnp.float32)
        steps = steps - SPAN * jnp.floor((steps + 0.5) * (1.0 / SPAN))
        sine, cosine = sine_cosine(steps * (2.0 * math.pi / SPAN))
        at = pl.ds(begin, block)
        base[0, at], base[2, at] = split(cosine)
        base[1, at], base[3, at] = split(sine)
        return carry

    lax.fori_loop(0, 8, fill, 0)
    build(forward, base, 1)
    build(inverse, base, -1)
    seen = split(window[...])
    part_re = split(right([seen], inverse, LOW))
    part_im = split(right([seen], inverse, HIGH))
    real, imag = left(forward, SPAN, [(FULL, part_re), (REST, part_im)])
    column = lax.broadcasted_iota(jnp.int32, (SPAN, HALF), 1)
    ends = (column == 0) | (column == SPAN // 2)
    weight = jnp.where(ends, 1.0, jnp.where(column < SPAN // 2, 2.0, 0.0)) / (SPAN * SPAN)
    spec_re[...] = real * weight
    spec_im[...] = imag * weight


def cut_kernel(place, screens, first, second, sems):
    at = pl.ds(pl.multiple_of(place[2], 8), 8)
    copies = [
        pltpu.make_async_copy(screens.at[layer, at, :], target, sems.at[layer])
        for layer, target in enumerate((first, second))
    ]
    for copy in copies:
        copy.start()
    for copy in copies:
        copy.wait()


def select_kernel(place, rows, cols, *refs):
    chunks, out, gathered = refs[:16], refs[16], refs[17]
    slab, first = place[0], place[1]
    for step in range(8):
        source = (slab + step) % 8
        for layer in range(2):
            gathered[source * 2 + layer] = chunks[step * 2 + layer][...]
    row_index = first + lax.broadcasted_iota(jnp.int32, (8, CORE), 0)
    lane = lax.broadcasted_iota(jnp.int32, (8, CORE), 1)

    def one(member, carry):
        patch = slab * 4 + member // 8
        frame = member % 8
        for layer in range(2):
            row = rows[frame, layer, patch]
            col = cols[frame, layer, patch]
            block, residue = row // CORE, row % CORE
            after = jnp.minimum(block + 1, 7)
            strip, turn = col // CORE, col % CORE
            at = pl.ds(pl.multiple_of(strip * CORE, CORE), CORE)
            beside = pl.ds(pl.multiple_of(jnp.minimum(strip + 1, 15) * CORE, CORE), CORE)
            right = lane >= turn
            upper = jnp.where(
                right, gathered[block * 2 + layer, :, at], gathered[block * 2 + layer, :, beside]
            )
            lower = jnp.where(
                right, gathered[after * 2 + layer, :, at], gathered[after * 2 + layer, :, beside]
            )
            out[member, layer] = jnp.where(row_index >= residue, upper, lower)
        return carry

    lax.fori_loop(0, 32, one, 0, unroll=2)


def scatter_kernel(place, rows, cols, values, *refs):
    pieces, out = refs[:16], refs[16]
    slab, first = place[0], place[1]
    row_index = first + lax.broadcasted_iota(jnp.int32, (8, CORE), 0)
    lane = lax.broadcasted_iota(jnp.int32, (8, CORE), 1)
    out[...] = jnp.zeros_like(out)

    def one(member, carry):
        patch = slab * 4 + member // 8
        frame = member % 8
        for layer in range(2):
            row = rows[frame, layer, patch]
            col = cols[frame, layer, patch]
            block, residue = row // CORE, row % CORE
            after = jnp.minimum(block + 1, 7)
            strip, turn = col // CORE, col % CORE
            beside = jnp.minimum(strip + 1, 15)
            value = values[member, layer]
            here = row_index >= residue
            right = lane >= turn
            for target, keep_row in ((block, here), (after, ~here)):
                where = (target + 8 - slab) % 8
                for place_col, keep_col in ((strip, right), (beside, ~right)):
                    at = pl.ds(pl.multiple_of((place_col % 2) * CORE, CORE), CORE)
                    chunk = place_col // 2
                    out[where, chunk, layer, :, at] = out[where, chunk, layer, :, at] + jnp.where(
                        keep_row & keep_col, value, 0.0
                    )
        return carry

    lax.fori_loop(0, 32, one, 0, unroll=2)
    for index, piece in enumerate(pieces):
        piece[...] = out[index // 2, 4 * (index % 2) : 4 * (index % 2) + 4]


def gradient_kernel(
    turns, received, amp_ref, observed, base, spec_re, spec_im, out,
    forward, inverse, pupil_re, pupil_im, far_re, far_im, mix_h, mix_l, wide_h, wide_l,
):
    def put(high, low, at, values):
        high[at], low[at] = split(values)

    build(forward, base, 1)
    build(inverse, base, -1)
    phases = None
    for layer in range(2):
        sheet = received[:, layer].reshape(CORE, CORE)
        sheet = pltpu.roll(sheet, (CORE - turns[layer, 0]) % CORE, 0)
        sheet = pltpu.roll(sheet, (CORE - turns[layer, 1]) % CORE, 1)
        phases = sheet if phases is None else phases + sheet
    amplitude = amp_ref[...]
    inverse_total = 1.0 / (SPAN * SPAN * jnp.sum(amplitude * amplitude))
    sine, cosine = sine_cosine(phases)
    pupil_re[...] = amplitude * cosine
    pupil_im[...] = amplitude * sine
    half_re, half_im = left(
        forward, SPAN, [(LOW, split(pupil_re[...])), (HIGH, split(pupil_im[...]))]
    )
    half = [split(half_re), split(half_im)]
    far_re[...] = right(half, inverse, FULL)
    far_im[...] = right(half, inverse, REST)
    spread = [split((far_re[...] * far_re[...] + far_im[...] * far_im[...]) * inverse_total)]
    put(mix_h, mix_l, FULL, right(spread, inverse, LOW))
    put(mix_h, mix_l, REST, right(spread, inverse, HIGH))
    first, second = left(forward, SPAN, [(ALL, (mix_h[...], mix_l[...]))])
    put(mix_h, mix_l, FULL, first * spec_re[...] - second * spec_im[...])
    put(mix_h, mix_l, REST, first * spec_im[...] + second * spec_re[...])
    first, second = left(inverse, CORE, [(ALL, (mix_h[...], mix_l[...]))])
    model = right([split(first), split(second)], forward, LOW)
    residual = [split((model - observed[0]) * float(SPAN))]
    grad_re = split(right(residual, inverse, LOW))
    grad_im = split(right(residual, inverse, HIGH))
    first, second = left(forward, SPAN, [(LOW, grad_re), (HIGH, grad_im)])
    put(mix_h, mix_l, FULL, first * spec_re[...] + second * spec_im[...])
    put(mix_h, mix_l, REST, second * spec_re[...] - first * spec_im[...])
    first, second = left(inverse, SPAN, [(ALL, (mix_h[...], mix_l[...]))])
    spread_grad = right([split(first), split(second)], forward, FULL)
    put(wide_h, wide_l, FULL, far_re[...] * spread_grad)
    put(wide_h, wide_l, REST, far_im[...] * spread_grad)
    first, second = left(inverse, CORE, [(ALL, (wide_h[...], wide_l[...]))])
    back = [split(first), split(second)]
    out_re = right(back, forward, LOW)
    out_im = right(back, forward, HIGH)
    gradient = (2.0 * inverse_total) * (pupil_re[...] * out_im - pupil_im[...] * out_re)
    for layer in range(2):
        sheet = pltpu.roll(gradient, turns[layer, 1], 1)
        sheet = pltpu.roll(sheet, turns[layer, 0], 0)
        out[:, layer] = sheet.reshape(32, 8, CORE)


SMEM = pl.BlockSpec(memory_space=pltpu.SMEM)
VMEM = pl.BlockSpec(memory_space=pltpu.VMEM)
ANY = pl.BlockSpec(memory_space=pl.ANY)


def limit(mib):
    return pltpu.CompilerParams(vmem_limit_bytes=mib << 20)


def cost(flops, moved):
    return pl.CostEstimate(flops=flops, bytes_accessed=moved, transcendentals=0)


def f32(*shape):
    return jax.ShapeDtypeStruct(shape, jnp.float32)


def gradient_call(*operands, name="gradient"):
    return pl.pallas_call(
        gradient_kernel,
        out_shape=f32(32, 2, 8, CORE),
        in_specs=[SMEM] + [VMEM] * 6,
        out_specs=VMEM,
        scratch_shapes=[
            pltpu.VMEM((4, SPAN, 2 * SPAN), jnp.bfloat16),
            pltpu.VMEM((4, SPAN, 2 * SPAN), jnp.bfloat16),
            pltpu.VMEM((CORE, CORE), jnp.float32),
            pltpu.VMEM((CORE, CORE), jnp.float32),
            pltpu.VMEM((SPAN, SPAN), jnp.float32),
            pltpu.VMEM((SPAN, SPAN), jnp.float32),
            pltpu.VMEM((2 * SPAN, HALF), jnp.bfloat16),
            pltpu.VMEM((2 * SPAN, HALF), jnp.bfloat16),
            pltpu.VMEM((2 * SPAN, SPAN), jnp.bfloat16),
            pltpu.VMEM((2 * SPAN, SPAN), jnp.bfloat16),
        ],
        compiler_params=limit(28),
        cost_estimate=cost(3 * 2 * 1222 * 10**6, 7 * 10**6),
        name=name,
    )(*operands)


def up(values):
    count = lax.axis_size("z")
    return lax.ppermute(values, "z", [(i, (i + 1) % count) for i in range(count)])


def down(values):
    count = lax.axis_size("z")
    return lax.ppermute(values, "z", [((i + 1) % count, i) for i in range(count)])


def ring_gather(own):
    chunks = {(0, 0): own[0], (0, 1): own[1]}
    for step in range(1, 4):
        for layer in range(2):
            chunks[8 - step, layer] = up(chunks[(9 - step) % 8, layer])
            chunks[step, layer] = down(chunks[step - 1, layer])
    chunks[4, 0] = up(chunks[5, 0])
    chunks[4, 1] = down(chunks[3, 1])
    return [chunks[step, layer] for step in range(8) for layer in range(2)]


def ring_scatter(partial):
    top, bottom = (4, 3), (3, 4)
    rise = [partial[2 * top[half] + half] for half in range(2)]
    fall = [partial[2 * (8 - bottom[half]) + half] for half in range(2)]
    for step in range(1, 5):
        for half in range(2):
            if step <= top[half]:
                rise[half] = up(rise[half])
                if step < top[half]:
                    rise[half] = rise[half] + partial[2 * (top[half] - step) + half]
            if step <= bottom[half]:
                fall[half] = down(fall[half])
                if step < bottom[half]:
                    fall[half] = fall[half] + partial[2 * (8 - bottom[half] + step) + half]
    return jnp.concatenate([partial[half] + rise[half] + fall[half] for half in range(2)])


def body(screens, row_offsets, col_offsets, amplitude, object_strip, observed):
    slab = lax.axis_index("z")
    across = lax.axis_index("x")
    frame_id = lax.axis_index(FRAME)
    patch = slab * 4 + across
    patches = lax.axis_size("z") * lax.axis_size("x")
    place = jnp.stack([slab, across * 64 + frame_id * 8, frame_id * 8]).astype(jnp.int32)
    own = pl.pallas_call(
        cut_kernel,
        out_shape=[f32(8, screens.shape[2])] * 2,
        in_specs=[SMEM, ANY],
        out_specs=[VMEM] * 2,
        scratch_shapes=[pltpu.SemaphoreType.DMA((2,))],
        compiler_params=limit(61),
        name="cut_rows",
    )(place, screens)
    chunks = ring_gather(own)
    sent = pl.pallas_call(
        select_kernel,
        out_shape=f32(32, 2, 8, CORE),
        in_specs=[SMEM] * 3 + [VMEM] * 16,
        out_specs=VMEM,
        scratch_shapes=[pltpu.VMEM((16, 8, screens.shape[2]), jnp.float32)],
        compiler_params=limit(20),
        cost_estimate=cost(0, 3 * 10**6),
        name="select_rows",
    )(place, row_offsets, col_offsets, *chunks)
    sent, strip = lax.optimization_barrier((sent, object_strip))
    received = lax.all_to_all(sent, SLAB, split_axis=0, concat_axis=0, tiled=True)

    ends = patches - 1
    left_tail = lax.ppermute(
        strip[:, CORE - HALO :], ("z", "x"), [(i, i + 1) for i in range(ends)]
    )
    right_head = lax.ppermute(strip[:, :HALO], ("z", "x"), [(i + 1, i) for i in range(ends)])
    window = jnp.concatenate([strip, right_head, left_tail], axis=1)
    window = jnp.concatenate([window[HALO:], window[:HALO]], axis=0)
    base, spec_re, spec_im = pl.pallas_call(
        object_kernel,
        out_shape=[jax.ShapeDtypeStruct((4, SPAN, SPAN), jnp.bfloat16)] + [f32(SPAN, HALF)] * 2,
        in_specs=[VMEM],
        out_specs=[VMEM] * 3,
        scratch_shapes=[pltpu.VMEM((4, SPAN, 2 * SPAN), jnp.bfloat16)] * 2,
        compiler_params=limit(28),
        cost_estimate=cost(3 * 2 * 226 * 10**6, 7 * 10**6),
        name="object_spectrum",
    )(window)

    row_turns = lax.dynamic_slice(row_offsets, (frame_id, 0, patch), (1, 2, 1))[0, :, 0] % CORE
    col_turns = lax.dynamic_slice(col_offsets, (frame_id, 0, patch), (1, 2, 1))[0, :, 0] % CORE
    turns = jnp.stack([row_turns, col_turns], axis=1)
    placed = gradient_call(
        turns, received, amplitude, observed, base, spec_re, spec_im
    )
    returned = lax.all_to_all(placed, SLAB, split_axis=0, concat_axis=0, tiled=True)

    partial = pl.pallas_call(
        scatter_kernel,
        out_shape=[f32(4, 2, 8, 512)] * 16,
        in_specs=[SMEM] * 3 + [VMEM],
        out_specs=[VMEM] * 16,
        scratch_shapes=[pltpu.VMEM((8, 8, 2, 8, 512), jnp.float32)],
        compiler_params=limit(20),
        cost_estimate=cost(0, 3 * 10**6),
        name="scatter_rows",
    )(place, row_offsets, col_offsets, returned)
    summed = ring_scatter(partial)
    turned = lax.all_to_all(summed, FRAME, split_axis=0, concat_axis=0, tiled=True)
    return turned.transpose(1, 0, 2, 3).reshape(2, 64, 512)


def solution(mesh):
    fine = Mesh(mesh.devices.reshape(8, 4, 4, 2), ("z", "x", "y", "core"))
    patch = ("z", "x")
    in_specs = (
        P(None, patch, None), P(), P(), P(), P(None, patch), P(FRAME, None, patch),
    )
    out_specs = P(None, patch, FRAME)
    return jax.shard_map(body, mesh=fine, in_specs=in_specs, out_specs=out_specs, check_vma=False)
```

```python
import math

import jax
import jax.numpy as jnp
from jax import lax
from jax.experimental import pallas as pl
from jax.experimental.pallas import tpu as pltpu
from jax.sharding import Mesh, PartitionSpec as P


CORE = 256
HALO = 64
SPAN = 384
HALF = 256
SLAB = ("x", "y", "core")
FRAME = ("y", "core")


def split(values):
    high = values.astype(jnp.bfloat16)
    low = (values - high.astype(jnp.float32)).astype(jnp.bfloat16)
    return high, low


def dot(left, right):
    return jnp.dot(left, right, preferred_element_type=jnp.float32)


def left(matrix, rows, parts):
    totals = [None, None]
    for lanes, (high, low) in parts:
        for block in range(2):
            both = matrix[2 * block : 2 * block + 2, 0:rows, lanes].reshape(2 * rows, high.shape[0])
            term, small = dot(both, high), dot(both[0:rows], low)
            before = totals[block]
            totals[block] = (term, small) if before is None else (before[0] + term, before[1] + small)
    return tuple(term[0:rows] + (term[rows : 2 * rows] + small) for term, small in totals)


def right(parts, matrix, lanes):
    rows = parts[0][0].shape[0] // 2
    totals = [None, None]
    for part, (high, low) in enumerate(parts):
        depth = high.shape[1]
        weights = (matrix[2 * part, 0:depth, lanes], matrix[2 * part + 1, 0:depth, lanes])
        for block in range(2):
            at = slice(block * rows, block * rows + rows)
            term = dot(jnp.concatenate([high[at], low[at]], axis=0), weights[0])
            small = dot(high[at], weights[1])
            before = totals[block]
            totals[block] = (term, small) if before is None else (before[0] + term, before[1] + small)
    return jnp.concatenate(
        [term[0:rows] + (term[rows : 2 * rows] + small) for term, small in totals], axis=0
    )


def build(matrix, base, sign):
    for part in range(2):
        cosine, sine = base[2 * part], base[2 * part + 1]
        matrix[part, :, FULL] = cosine
        matrix[part, :, REST] = sine if sign > 0 else -sine
        matrix[2 + part, :, FULL] = -sine if sign > 0 else sine
        matrix[2 + part, :, REST] = cosine


def sine_cosine(angle):
    turns = jnp.round(angle * (2.0 / math.pi))
    rest = angle - turns * 1.5703125
    rest = rest - turns * 4.83826794896619e-4
    square = rest * rest
    sine = rest + rest * square * (
        -1.6666654611e-1 + square * (8.3321608736e-3 + square * -1.9515295891e-4)
    )
    cosine = 1.0 - 0.5 * square + square * square * (
        4.166664568298827e-2 + square * (-1.388731625493765e-3 + square * 2.443315711809948e-5)
    )
    quarter = turns.astype(jnp.int32)
    odd = (quarter & 1) == 1
    sine, cosine = jnp.where(odd, cosine, sine), jnp.where(odd, sine, cosine)
    sine = jnp.where((quarter & 2) == 2, -sine, sine)
    cosine = jnp.where(((quarter + 1) & 2) == 2, -cosine, cosine)
    return sine, cosine


LOW = slice(0, CORE)
HIGH = slice(SPAN, SPAN + CORE)
FULL = slice(0, SPAN)
REST = slice(SPAN, 2 * SPAN)
ALL = slice(None)


def object_kernel(window, base, spec_re, spec_im, forward, inverse):
    block = SPAN // 8
    row = lax.broadcasted_iota(jnp.int32, (block, SPAN), 0)
    column = lax.broadcasted_iota(jnp.int32, (block, SPAN), 1)

    def fill(index, carry):
        begin = pl.multiple_of(index * block, block)
        steps = ((row + begin) * column).astype(jnp.float32)
        steps = steps - SPAN * jnp.floor((steps + 0.5) * (1.0 / SPAN))
        sine, cosine = sine_cosine(steps * (2.0 * math.pi / SPAN))
        at = pl.ds(begin, block)
        base[0, at], base[2, at] = split(cosine)
        base[1, at], base[3, at] = split(sine)
        return carry

    lax.fori_loop(0, 8, fill, 0)
    build(forward, base, 1)
    build(inverse, base, -1)
    seen = split(window[...])
    part_re = split(right([seen], inverse, LOW))
    part_im = split(right([seen], inverse, HIGH))
    real, imag = left(forward, SPAN, [(FULL, part_re), (REST, part_im)])
    column = lax.broadcasted_iota(jnp.int32, (SPAN, HALF), 1)
    ends = (column == 0) | (column == SPAN // 2)
    weight = jnp.where(ends, 1.0, jnp.where(column < SPAN // 2, 2.0, 0.0)) / (SPAN * SPAN)
    spec_re[...] = real * weight
    spec_im[...] = imag * weight


def cut_kernel(place, screens, first, second, sems):
    at = pl.ds(pl.multiple_of(place[2], 8), 8)
    copies = [
        pltpu.make_async_copy(screens.at[layer, at, :], target, sems.at[layer])
        for layer, target in enumerate((first, second))
    ]
    for copy in copies:
        copy.start()
    for copy in copies:
        copy.wait()


def select_kernel(place, rows, cols, *refs):
    chunks, out, gathered = refs[:16], refs[16], refs[17]
    slab, first = place[0], place[1]
    for step in range(8):
        source = (slab + step) % 8
        for layer in range(2):
            gathered[source * 2 + layer] = chunks[step * 2 + layer][...]
    row_index = first + lax.broadcasted_iota(jnp.int32, (8, CORE), 0)
    lane = lax.broadcasted_iota(jnp.int32, (8, CORE), 1)

    def one(member, carry):
        patch = slab * 4 + member // 8
        frame = member % 8
        for layer in range(2):
            row = rows[frame, layer, patch]
            col = cols[frame, layer, patch]
            block, residue = row // CORE, row % CORE
            after = jnp.minimum(block + 1, 7)
            strip, turn = col // CORE, col % CORE
            at = pl.ds(pl.multiple_of(strip * CORE, CORE), CORE)
            beside = pl.ds(pl.multiple_of(jnp.minimum(strip + 1, 15) * CORE, CORE), CORE)
            right = lane >= turn
            upper = jnp.where(
                right, gathered[block * 2 + layer, :, at], gathered[block * 2 + layer, :, beside]
            )
            lower = jnp.where(
                right, gathered[after * 2 + layer, :, at], gathered[after * 2 + layer, :, beside]
            )
            out[member, layer] = jnp.where(row_index >= residue, upper, lower)
        return carry

    lax.fori_loop(0, 32, one, 0, unroll=2)


def scatter_kernel(place, rows, cols, values, *refs):
    pieces, out = refs[:16], refs[16]
    slab, first = place[0], place[1]
    row_index = first + lax.broadcasted_iota(jnp.int32, (8, CORE), 0)
    lane = lax.broadcasted_iota(jnp.int32, (8, CORE), 1)
    out[...] = jnp.zeros_like(out)

    def one(member, carry):
        patch = slab * 4 + member // 8
        frame = member % 8
        for layer in range(2):
            row = rows[frame, layer, patch]
            col = cols[frame, layer, patch]
            block, residue = row // CORE, row % CORE
            after = jnp.minimum(block + 1, 7)
            strip, turn = col // CORE, col % CORE
            beside = jnp.minimum(strip + 1, 15)
            value = values[member, layer]
            here = row_index >= residue
            right = lane >= turn
            for target, keep_row in ((block, here), (after, ~here)):
                where = (target + 8 - slab) % 8
                for place_col, keep_col in ((strip, right), (beside, ~right)):
                    at = pl.ds(pl.multiple_of((place_col % 2) * CORE, CORE), CORE)
                    chunk = place_col // 2
                    out[where, chunk, layer, :, at] = out[where, chunk, layer, :, at] + jnp.where(
                        keep_row & keep_col, value, 0.0
                    )
        return carry

    lax.fori_loop(0, 32, one, 0, unroll=2)
    for index, piece in enumerate(pieces):
        piece[...] = out[index // 2, 4 * (index % 2) : 4 * (index % 2) + 4]


def gradient_kernel(
    turns, received, amp_ref, observed, base, spec_re, spec_im, out,
    forward, inverse, pupil_re, pupil_im, far_re, far_im, mix_h, mix_l, wide_h, wide_l,
):
    def put(high, low, at, values):
        high[at], low[at] = split(values)

    build(forward, base, 1)
    build(inverse, base, -1)
    phases = None
    for layer in range(2):
        sheet = received[:, layer].reshape(CORE, CORE)
        sheet = pltpu.roll(sheet, (CORE - turns[layer, 0]) % CORE, 0)
        sheet = pltpu.roll(sheet, (CORE - turns[layer, 1]) % CORE, 1)
        phases = sheet if phases is None else phases + sheet
    amplitude = amp_ref[...]
    inverse_total = 1.0 / (SPAN * SPAN * jnp.sum(amplitude * amplitude))
    sine, cosine = sine_cosine(phases)
    pupil_re[...] = amplitude * cosine
    pupil_im[...] = amplitude * sine
    half_re, half_im = left(
        forward, SPAN, [(LOW, split(pupil_re[...])), (HIGH, split(pupil_im[...]))]
    )
    half = [split(half_re), split(half_im)]
    far = right(half, inverse, ALL)
    far_re[...] = far[:, FULL]
    far_im[...] = far[:, REST]
    spread = [split((far_re[...] * far_re[...] + far_im[...] * far_im[...]) * inverse_total)]
    put(mix_h, mix_l, FULL, right(spread, inverse, LOW))
    put(mix_h, mix_l, REST, right(spread, inverse, HIGH))
    first, second = left(forward, SPAN, [(ALL, (mix_h[...], mix_l[...]))])
    put(mix_h, mix_l, FULL, first * spec_re[...] - second * spec_im[...])
    put(mix_h, mix_l, REST, first * spec_im[...] + second * spec_re[...])
    first, second = left(inverse, CORE, [(ALL, (mix_h[...], mix_l[...]))])
    model = right([split(first), split(second)], forward, LOW)
    residual = [split((model - observed[0]) * float(SPAN))]
    grad_re = split(right(residual, inverse, LOW))
    grad_im = split(right(residual, inverse, HIGH))
    first, second = left(forward, SPAN, [(LOW, grad_re), (HIGH, grad_im)])
    put(mix_h, mix_l, FULL, first * spec_re[...] + second * spec_im[...])
    put(mix_h, mix_l, REST, second * spec_re[...] - first * spec_im[...])
    first, second = left(inverse, SPAN, [(ALL, (mix_h[...], mix_l[...]))])
    spread_grad = right([split(first), split(second)], forward, FULL)
    put(wide_h, wide_l, FULL, far_re[...] * spread_grad)
    put(wide_h, wide_l, REST, far_im[...] * spread_grad)
    first, second = left(inverse, CORE, [(ALL, (wide_h[...], wide_l[...]))])
    back = [split(first), split(second)]
    out_re = right(back, forward, LOW)
    out_im = right(back, forward, HIGH)
    gradient = (2.0 * inverse_total) * (pupil_re[...] * out_im - pupil_im[...] * out_re)
    for layer in range(2):
        sheet = pltpu.roll(gradient, turns[layer, 1], 1)
        sheet = pltpu.roll(sheet, turns[layer, 0], 0)
        out[:, layer] = sheet.reshape(32, 8, CORE)


SMEM = pl.BlockSpec(memory_space=pltpu.SMEM)
VMEM = pl.BlockSpec(memory_space=pltpu.VMEM)
ANY = pl.BlockSpec(memory_space=pl.ANY)


def limit(mib):
    return pltpu.CompilerParams(vmem_limit_bytes=mib << 20)


def cost(flops, moved):
    return pl.CostEstimate(flops=flops, bytes_accessed=moved, transcendentals=0)


def f32(*shape):
    return jax.ShapeDtypeStruct(shape, jnp.float32)


def gradient_call(*operands):
    return pl.pallas_call(
        gradient_kernel,
        out_shape=f32(32, 2, 8, CORE),
        in_specs=[SMEM] + [VMEM] * 6,
        out_specs=VMEM,
        scratch_shapes=[
            pltpu.VMEM((4, SPAN, 2 * SPAN), jnp.bfloat16),
            pltpu.VMEM((4, SPAN, 2 * SPAN), jnp.bfloat16),
            pltpu.VMEM((CORE, CORE), jnp.float32),
            pltpu.VMEM((CORE, CORE), jnp.float32),
            pltpu.VMEM((SPAN, SPAN), jnp.float32),
            pltpu.VMEM((SPAN, SPAN), jnp.float32),
            pltpu.VMEM((2 * SPAN, HALF), jnp.bfloat16),
            pltpu.VMEM((2 * SPAN, HALF), jnp.bfloat16),
            pltpu.VMEM((2 * SPAN, SPAN), jnp.bfloat16),
            pltpu.VMEM((2 * SPAN, SPAN), jnp.bfloat16),
        ],
        compiler_params=limit(28),
        cost_estimate=cost(3 * 2 * 1222 * 10**6, 7 * 10**6),
    )(*operands)


def up(values):
    count = lax.axis_size("z")
    return lax.ppermute(values, "z", [(i, (i + 1) % count) for i in range(count)])


def down(values):
    count = lax.axis_size("z")
    return lax.ppermute(values, "z", [((i + 1) % count, i) for i in range(count)])


def ring_gather(own):
    chunks = {(0, 0): own[0], (0, 1): own[1]}
    for step in range(1, 4):
        for layer in range(2):
            chunks[8 - step, layer] = up(chunks[(9 - step) % 8, layer])
            chunks[step, layer] = down(chunks[step - 1, layer])
    chunks[4, 0] = up(chunks[5, 0])
    chunks[4, 1] = down(chunks[3, 1])
    return [chunks[step, layer] for step in range(8) for layer in range(2)]


def ring_scatter(partial):
    top, bottom = (4, 3), (3, 4)
    rise = [partial[2 * top[half] + half] for half in range(2)]
    fall = [partial[2 * (8 - bottom[half]) + half] for half in range(2)]
    for step in range(1, 5):
        for half in range(2):
            if step <= top[half]:
                rise[half] = up(rise[half])
                if step < top[half]:
                    rise[half] = rise[half] + partial[2 * (top[half] - step) + half]
            if step <= bottom[half]:
                fall[half] = down(fall[half])
                if step < bottom[half]:
                    fall[half] = fall[half] + partial[2 * (8 - bottom[half] + step) + half]
    return jnp.concatenate([partial[half] + rise[half] + fall[half] for half in range(2)])


def body(screens, row_offsets, col_offsets, amplitude, object_strip, observed):
    slab = lax.axis_index("z")
    across = lax.axis_index("x")
    frame_id = lax.axis_index(FRAME)
    patch = slab * 4 + across
    patches = lax.axis_size("z") * lax.axis_size("x")
    place = jnp.stack([slab, across * 64 + frame_id * 8, frame_id * 8]).astype(jnp.int32)
    ends = patches - 1
    left_tail = lax.ppermute(
        object_strip[:, CORE - HALO :], ("z", "x"), [(i, i + 1) for i in range(ends)]
    )
    right_head = lax.ppermute(object_strip[:, :HALO], ("z", "x"), [(i + 1, i) for i in range(ends)])
    own = pl.pallas_call(
        cut_kernel,
        out_shape=[f32(8, screens.shape[2])] * 2,
        in_specs=[SMEM, ANY],
        out_specs=[VMEM] * 2,
        scratch_shapes=[pltpu.SemaphoreType.DMA((2,))],
        compiler_params=limit(20),
        name="cut_rows",
    )(place, screens)
    chunks = ring_gather(own)
    sent = pl.pallas_call(
        select_kernel,
        out_shape=f32(32, 2, 8, CORE),
        in_specs=[SMEM] * 3 + [VMEM] * 16,
        out_specs=VMEM,
        scratch_shapes=[pltpu.VMEM((16, 8, screens.shape[2]), jnp.float32)],
        compiler_params=limit(20),
        cost_estimate=cost(0, 3 * 10**6),
        name="select_rows",
    )(place, row_offsets, col_offsets, *chunks)
    sent, left_tail, right_head = lax.optimization_barrier((sent, left_tail, right_head))
    received = lax.all_to_all(sent, SLAB, split_axis=0, concat_axis=0, tiled=True)
    window = jnp.concatenate([object_strip, right_head, left_tail], axis=1)
    window = jnp.concatenate([window[HALO:], window[:HALO]], axis=0)
    base, spec_re, spec_im = pl.pallas_call(
        object_kernel,
        out_shape=[jax.ShapeDtypeStruct((4, SPAN, SPAN), jnp.bfloat16)] + [f32(SPAN, HALF)] * 2,
        in_specs=[VMEM],
        out_specs=[VMEM] * 3,
        scratch_shapes=[pltpu.VMEM((4, SPAN, 2 * SPAN), jnp.bfloat16)] * 2,
        compiler_params=limit(28),
        cost_estimate=cost(3 * 2 * 226 * 10**6, 7 * 10**6),
        name="object_spectrum",
    )(window)

    row_turns = lax.dynamic_slice(row_offsets, (frame_id, 0, patch), (1, 2, 1))[0, :, 0] % CORE
    col_turns = lax.dynamic_slice(col_offsets, (frame_id, 0, patch), (1, 2, 1))[0, :, 0] % CORE
    turns = jnp.stack([row_turns, col_turns], axis=1)
    placed = gradient_call(
        turns, received, amplitude, observed, base, spec_re, spec_im
    )
    returned = lax.all_to_all(placed, SLAB, split_axis=0, concat_axis=0, tiled=True)

    partial = pl.pallas_call(
        scatter_kernel,
        out_shape=[f32(4, 2, 8, 512)] * 16,
        in_specs=[SMEM] * 3 + [VMEM],
        out_specs=[VMEM] * 16,
        scratch_shapes=[pltpu.VMEM((8, 8, 2, 8, 512), jnp.float32)],
        compiler_params=limit(20),
        cost_estimate=cost(0, 3 * 10**6),
        name="scatter_rows",
    )(place, row_offsets, col_offsets, returned)
    summed = ring_scatter(partial)
    turned = lax.all_to_all(summed, FRAME, split_axis=0, concat_axis=0, tiled=True)
    return turned.transpose(1, 0, 2, 3).reshape(2, 64, 512)


def solution(mesh):
    fine = Mesh(mesh.devices.reshape(8, 4, 4, 2), ("z", "x", "y", "core"))
    patch = ("z", "x")
    in_specs = (
        P(None, patch, None), P(), P(), P(), P(None, patch), P(FRAME, None, patch),
    )
    out_specs = P(None, patch, FRAME)
    return jax.shard_map(body, mesh=fine, in_specs=in_specs, out_specs=out_specs, check_vma=False)
```

```python
import math

import jax
import jax.numpy as jnp
from jax import lax
from jax.experimental import pallas as pl
from jax.experimental.pallas import tpu as pltpu
from jax.sharding import Mesh, PartitionSpec as P


CORE = 256
HALO = 64
SPAN = 384
HALF = 256
SLAB = ("x", "y", "core")
FRAME = ("y", "core")


def split(values):
    high = values.astype(jnp.bfloat16)
    low = (values - high.astype(jnp.float32)).astype(jnp.bfloat16)
    return high, low


def dot(left, right):
    return jnp.dot(left, right, preferred_element_type=jnp.float32)


def left(matrix, rows, parts):
    totals = [None, None]
    for lanes, (high, low) in parts:
        for block in range(2):
            both = matrix[2 * block : 2 * block + 2, 0:rows, lanes].reshape(2 * rows, high.shape[0])
            term, small = dot(both, high), dot(both[0:rows], low)
            before = totals[block]
            totals[block] = (term, small) if before is None else (before[0] + term, before[1] + small)
    return tuple(term[0:rows] + (term[rows : 2 * rows] + small) for term, small in totals)


def right(parts, matrix, lanes):
    rows = parts[0][0].shape[0] // 2
    totals = [None, None]
    for part, (high, low) in enumerate(parts):
        depth = high.shape[1]
        weights = (matrix[2 * part, 0:depth, lanes], matrix[2 * part + 1, 0:depth, lanes])
        for block in range(2):
            at = slice(block * rows, block * rows + rows)
            term = dot(jnp.concatenate([high[at], low[at]], axis=0), weights[0])
            small = dot(high[at], weights[1])
            before = totals[block]
            totals[block] = (term, small) if before is None else (before[0] + term, before[1] + small)
    return jnp.concatenate(
        [term[0:rows] + (term[rows : 2 * rows] + small) for term, small in totals], axis=0
    )


def build(matrix, base, sign):
    for part in range(2):
        cosine, sine = base[2 * part], base[2 * part + 1]
        matrix[part, :, FULL] = cosine
        matrix[part, :, REST] = sine if sign > 0 else -sine
        matrix[2 + part, :, FULL] = -sine if sign > 0 else sine
        matrix[2 + part, :, REST] = cosine


def sine_cosine(angle):
    turns = jnp.round(angle * (2.0 / math.pi))
    rest = angle - turns * 1.5703125
    rest = rest - turns * 4.83826794896619e-4
    square = rest * rest
    sine = rest + rest * square * (
        -1.6666654611e-1 + square * (8.3321608736e-3 + square * -1.9515295891e-4)
    )
    cosine = 1.0 - 0.5 * square + square * square * (
        4.166664568298827e-2 + square * (-1.388731625493765e-3 + square * 2.443315711809948e-5)
    )
    quarter = turns.astype(jnp.int32)
    odd = (quarter & 1) == 1
    sine, cosine = jnp.where(odd, cosine, sine), jnp.where(odd, sine, cosine)
    sine = jnp.where((quarter & 2) == 2, -sine, sine)
    cosine = jnp.where(((quarter + 1) & 2) == 2, -cosine, cosine)
    return sine, cosine


LOW = slice(0, CORE)
HIGH = slice(SPAN, SPAN + CORE)
FULL = slice(0, SPAN)
REST = slice(SPAN, 2 * SPAN)
ALL = slice(None)


def base_kernel(base):
    block = SPAN // 8
    row = lax.broadcasted_iota(jnp.int32, (block, SPAN), 0)
    column = lax.broadcasted_iota(jnp.int32, (block, SPAN), 1)

    def fill(index, carry):
        begin = pl.multiple_of(index * block, block)
        steps = ((row + begin) * column).astype(jnp.float32)
        steps = steps - SPAN * jnp.floor((steps + 0.5) * (1.0 / SPAN))
        sine, cosine = sine_cosine(steps * (2.0 * math.pi / SPAN))
        at = pl.ds(begin, block)
        base[0, at], base[2, at] = split(cosine)
        base[1, at], base[3, at] = split(sine)
        return carry

    lax.fori_loop(0, 8, fill, 0)


def object_kernel(base, strip, right_ref, left_ref, spec_re, spec_im, forward, inverse):
    lane = lax.broadcasted_iota(jnp.int32, (SPAN // 2, 2 * HALO), 1)
    after, before = right_ref[...], left_ref[...]
    top = jnp.where(lane < HALO, after, pltpu.roll(before, HALO, 1))
    bottom = jnp.where(lane < HALO, pltpu.roll(after, HALO, 1), before)
    halo = jnp.concatenate([top, bottom], axis=0)
    window = jnp.concatenate([strip[...], halo], axis=1)
    window = jnp.concatenate([window[HALO:], window[:HALO]], axis=0)
    build(forward, base, 1)
    build(inverse, base, -1)
    seen = split(window)
    part_re = split(right([seen], inverse, LOW))
    part_im = split(right([seen], inverse, HIGH))
    real, imag = left(forward, SPAN, [(FULL, part_re), (REST, part_im)])
    column = lax.broadcasted_iota(jnp.int32, (SPAN, HALF), 1)
    ends = (column == 0) | (column == SPAN // 2)
    weight = jnp.where(ends, 1.0, jnp.where(column < SPAN // 2, 2.0, 0.0)) / (SPAN * SPAN)
    spec_re[...] = real * weight
    spec_im[...] = imag * weight


def cut_kernel(place, screens, first, second, sems):
    at = pl.ds(pl.multiple_of(place[2], 8), 8)
    copies = [
        pltpu.make_async_copy(screens.at[layer, at, :], target, sems.at[layer])
        for layer, target in enumerate((first, second))
    ]
    for copy in copies:
        copy.start()
    for copy in copies:
        copy.wait()


def select_kernel(place, rows, cols, *refs):
    chunks, out, gathered = refs[:16], refs[16], refs[17]
    slab, first = place[0], place[1]
    for step in range(8):
        source = (slab + step) % 8
        for layer in range(2):
            gathered[source * 2 + layer] = chunks[step * 2 + layer][...]
    row_index = first + lax.broadcasted_iota(jnp.int32, (8, CORE), 0)
    lane = lax.broadcasted_iota(jnp.int32, (8, CORE), 1)

    def one(member, carry):
        patch = slab * 4 + member // 8
        frame = member % 8
        for layer in range(2):
            row = rows[frame, layer, patch]
            col = cols[frame, layer, patch]
            block, residue = row // CORE, row % CORE
            after = jnp.minimum(block + 1, 7)
            strip, turn = col // CORE, col % CORE
            at = pl.ds(pl.multiple_of(strip * CORE, CORE), CORE)
            beside = pl.ds(pl.multiple_of(jnp.minimum(strip + 1, 15) * CORE, CORE), CORE)
            right = lane >= turn
            upper = jnp.where(
                right, gathered[block * 2 + layer, :, at], gathered[block * 2 + layer, :, beside]
            )
            lower = jnp.where(
                right, gathered[after * 2 + layer, :, at], gathered[after * 2 + layer, :, beside]
            )
            out[member, layer] = jnp.where(row_index >= residue, upper, lower)
        return carry

    lax.fori_loop(0, 32, one, 0, unroll=8)


def scatter_kernel(place, rows, cols, values, *refs):
    pieces, out = refs[:16], refs[16]
    slab, first = place[0], place[1]
    row_index = first + lax.broadcasted_iota(jnp.int32, (8, CORE), 0)
    lane = lax.broadcasted_iota(jnp.int32, (8, CORE), 1)
    out[...] = jnp.zeros_like(out)

    def one(member, carry):
        patch = slab * 4 + member // 8
        frame = member % 8
        for layer in range(2):
            row = rows[frame, layer, patch]
            col = cols[frame, layer, patch]
            block, residue = row // CORE, row % CORE
            after = jnp.minimum(block + 1, 7)
            strip, turn = col // CORE, col % CORE
            beside = jnp.minimum(strip + 1, 15)
            value = values[member, layer]
            here = row_index >= residue
            right = lane >= turn
            for target, keep_row in ((block, here), (after, ~here)):
                where = (target + 8 - slab) % 8
                for place_col, keep_col in ((strip, right), (beside, ~right)):
                    at = pl.ds(pl.multiple_of((place_col % 2) * CORE, CORE), CORE)
                    chunk = place_col // 2
                    out[where, chunk, layer, :, at] = out[where, chunk, layer, :, at] + jnp.where(
                        keep_row & keep_col, value, 0.0
                    )
        return carry

    lax.fori_loop(0, 32, one, 0, unroll=4)
    for index, piece in enumerate(pieces):
        piece[...] = out[index // 2, 4 * (index % 2) : 4 * (index % 2) + 4]


def gradient_kernel(
    turns, received, amp_ref, observed, base, spec_re, spec_im, out,
    forward, inverse, pupil_re, pupil_im, far_re, far_im, mix_h, mix_l, wide_h, wide_l,
):
    def put(high, low, at, values):
        high[at], low[at] = split(values)

    build(forward, base, 1)
    build(inverse, base, -1)
    phases = None
    for layer in range(2):
        sheet = received[:, layer].reshape(CORE, CORE)
        sheet = pltpu.roll(sheet, (CORE - turns[layer, 0]) % CORE, 0)
        sheet = pltpu.roll(sheet, (CORE - turns[layer, 1]) % CORE, 1)
        phases = sheet if phases is None else phases + sheet
    amplitude = amp_ref[...]
    inverse_total = 1.0 / (SPAN * SPAN * jnp.sum(amplitude * amplitude))
    sine, cosine = sine_cosine(phases)
    pupil_re[...] = amplitude * cosine
    pupil_im[...] = amplitude * sine
    half_re, half_im = left(
        forward, SPAN, [(LOW, split(pupil_re[...])), (HIGH, split(pupil_im[...]))]
    )
    half = [split(half_re), split(half_im)]
    far = right(half, inverse, ALL)
    far_re[...] = far[:, FULL]
    far_im[...] = far[:, REST]
    spread = [split((far_re[...] * far_re[...] + far_im[...] * far_im[...]) * inverse_total)]
    put(mix_h, mix_l, FULL, right(spread, inverse, LOW))
    put(mix_h, mix_l, REST, right(spread, inverse, HIGH))
    first, second = left(forward, SPAN, [(ALL, (mix_h[...], mix_l[...]))])
    put(mix_h, mix_l, FULL, first * spec_re[...] - second * spec_im[...])
    put(mix_h, mix_l, REST, first * spec_im[...] + second * spec_re[...])
    first, second = left(inverse, CORE, [(ALL, (mix_h[...], mix_l[...]))])
    model = right([split(first), split(second)], forward, LOW)
    residual = [split((model - observed[0]) * float(SPAN))]
    grad_re = split(right(residual, inverse, LOW))
    grad_im = split(right(residual, inverse, HIGH))
    first, second = left(forward, SPAN, [(LOW, grad_re), (HIGH, grad_im)])
    put(mix_h, mix_l, FULL, first * spec_re[...] + second * spec_im[...])
    put(mix_h, mix_l, REST, second * spec_re[...] - first * spec_im[...])
    first, second = left(inverse, SPAN, [(ALL, (mix_h[...], mix_l[...]))])
    spread_grad = right([split(first), split(second)], forward, FULL)
    put(wide_h, wide_l, FULL, far_re[...] * spread_grad)
    put(wide_h, wide_l, REST, far_im[...] * spread_grad)
    first, second = left(inverse, CORE, [(ALL, (wide_h[...], wide_l[...]))])
    back = [split(first), split(second)]
    out_re = right(back, forward, LOW)
    out_im = right(back, forward, HIGH)
    gradient = (2.0 * inverse_total) * (pupil_re[...] * out_im - pupil_im[...] * out_re)
    for layer in range(2):
        sheet = pltpu.roll(gradient, turns[layer, 1], 1)
        sheet = pltpu.roll(sheet, turns[layer, 0], 0)
        out[:, layer] = sheet.reshape(32, 8, CORE)


SMEM = pl.BlockSpec(memory_space=pltpu.SMEM)
VMEM = pl.BlockSpec(memory_space=pltpu.VMEM)
ANY = pl.BlockSpec(memory_space=pl.ANY)


def limit(mib):
    return pltpu.CompilerParams(vmem_limit_bytes=mib << 20)


def cost(flops, moved):
    return pl.CostEstimate(flops=flops, bytes_accessed=moved, transcendentals=0)


def f32(*shape):
    return jax.ShapeDtypeStruct(shape, jnp.float32)


def gradient_call(*operands):
    return pl.pallas_call(
        gradient_kernel,
        out_shape=f32(32, 2, 8, CORE),
        in_specs=[SMEM] + [VMEM] * 6,
        out_specs=VMEM,
        scratch_shapes=[
            pltpu.VMEM((4, SPAN, 2 * SPAN), jnp.bfloat16),
            pltpu.VMEM((4, SPAN, 2 * SPAN), jnp.bfloat16),
            pltpu.VMEM((CORE, CORE), jnp.float32),
            pltpu.VMEM((CORE, CORE), jnp.float32),
            pltpu.VMEM((SPAN, SPAN), jnp.float32),
            pltpu.VMEM((SPAN, SPAN), jnp.float32),
            pltpu.VMEM((2 * SPAN, HALF), jnp.bfloat16),
            pltpu.VMEM((2 * SPAN, HALF), jnp.bfloat16),
            pltpu.VMEM((2 * SPAN, SPAN), jnp.bfloat16),
            pltpu.VMEM((2 * SPAN, SPAN), jnp.bfloat16),
        ],
        compiler_params=limit(28),
        cost_estimate=cost(3 * 2 * 1222 * 10**6, 7 * 10**6),
    )(*operands)


def up(values):
    count = lax.axis_size("z")
    return lax.ppermute(values, "z", [(i, (i + 1) % count) for i in range(count)])


def down(values):
    count = lax.axis_size("z")
    return lax.ppermute(values, "z", [((i + 1) % count, i) for i in range(count)])


def ring_gather(own):
    chunks = {(0, 0): own[0], (0, 1): own[1]}
    for step in range(1, 4):
        for layer in range(2):
            chunks[8 - step, layer] = up(chunks[(9 - step) % 8, layer])
            chunks[step, layer] = down(chunks[step - 1, layer])
    chunks[4, 0] = up(chunks[5, 0])
    chunks[4, 1] = down(chunks[3, 1])
    return [chunks[step, layer] for step in range(8) for layer in range(2)]


def ring_scatter(partial):
    top, bottom = (4, 3), (3, 4)
    rise = [partial[2 * top[half] + half] for half in range(2)]
    fall = [partial[2 * (8 - bottom[half]) + half] for half in range(2)]
    for step in range(1, 5):
        for half in range(2):
            if step <= top[half]:
                rise[half] = up(rise[half])
                if step < top[half]:
                    rise[half] = rise[half] + partial[2 * (top[half] - step) + half]
            if step <= bottom[half]:
                fall[half] = down(fall[half])
                if step < bottom[half]:
                    fall[half] = fall[half] + partial[2 * (8 - bottom[half] + step) + half]
    return jnp.concatenate([partial[half] + rise[half] + fall[half] for half in range(2)])


def body(screens, row_offsets, col_offsets, amplitude, object_strip, observed):
    slab = lax.axis_index("z")
    across = lax.axis_index("x")
    frame_id = lax.axis_index(FRAME)
    patch = slab * 4 + across
    patches = lax.axis_size("z") * lax.axis_size("x")
    place = jnp.stack([slab, across * 64 + frame_id * 8, frame_id * 8]).astype(jnp.int32)
    own = pl.pallas_call(
        cut_kernel,
        out_shape=[f32(8, screens.shape[2])] * 2,
        in_specs=[SMEM, ANY],
        out_specs=[VMEM] * 2,
        scratch_shapes=[pltpu.SemaphoreType.DMA((2,))],
        compiler_params=limit(20),
        name="cut_rows",
    )(place, screens)
    chunks = ring_gather(own)
    sent = pl.pallas_call(
        select_kernel,
        out_shape=f32(32, 2, 8, CORE),
        in_specs=[SMEM] * 3 + [VMEM] * 16,
        out_specs=VMEM,
        scratch_shapes=[pltpu.VMEM((16, 8, screens.shape[2]), jnp.float32)],
        compiler_params=limit(20),
        cost_estimate=cost(0, 3 * 10**6),
        name="select_rows",
    )(place, row_offsets, col_offsets, *chunks)
    sent, strip = lax.optimization_barrier((sent, object_strip))
    received = lax.all_to_all(sent, SLAB, split_axis=0, concat_axis=0, tiled=True)
    ends = patches - 1
    half = SPAN // 2
    tail = strip[:, CORE - HALO :]
    left_tail = lax.ppermute(
        jnp.concatenate([tail[:half], tail[half:]], axis=1),
        ("z", "x"),
        [(i, i + 1) for i in range(ends)],
    )
    head = strip[:, :HALO]
    right_head = lax.ppermute(
        jnp.concatenate([head[:half], head[half:]], axis=1),
        ("z", "x"),
        [(i + 1, i) for i in range(ends)],
    )
    base = pl.pallas_call(
        base_kernel,
        out_shape=jax.ShapeDtypeStruct((4, SPAN, SPAN), jnp.bfloat16),
        out_specs=VMEM,
        compiler_params=limit(20),
        cost_estimate=cost(10**6, 10**6),
        name="dft_base",
    )()
    spec_re, spec_im = pl.pallas_call(
        object_kernel,
        out_shape=[f32(SPAN, HALF)] * 2,
        in_specs=[VMEM] * 4,
        out_specs=[VMEM] * 2,
        scratch_shapes=[pltpu.VMEM((4, SPAN, 2 * SPAN), jnp.bfloat16)] * 2,
        compiler_params=limit(28),
        cost_estimate=cost(3 * 2 * 226 * 10**6, 7 * 10**6),
        name="object_spectrum",
    )(base, strip, right_head, left_tail)

    row_turns = lax.dynamic_slice(row_offsets, (frame_id, 0, patch), (1, 2, 1))[0, :, 0] % CORE
    col_turns = lax.dynamic_slice(col_offsets, (frame_id, 0, patch), (1, 2, 1))[0, :, 0] % CORE
    turns = jnp.stack([row_turns, col_turns], axis=1)
    placed = gradient_call(
        turns, received, amplitude, observed, base, spec_re, spec_im
    )
    returned = lax.all_to_all(placed, SLAB, split_axis=0, concat_axis=0, tiled=True)

    partial = pl.pallas_call(
        scatter_kernel,
        out_shape=[f32(4, 2, 8, 512)] * 16,
        in_specs=[SMEM] * 3 + [VMEM],
        out_specs=[VMEM] * 16,
        scratch_shapes=[pltpu.VMEM((8, 8, 2, 8, 512), jnp.float32)],
        compiler_params=limit(20),
        cost_estimate=cost(0, 3 * 10**6),
        name="scatter_rows",
    )(place, row_offsets, col_offsets, returned)
    summed = ring_scatter(partial)
    turned = lax.all_to_all(summed, FRAME, split_axis=0, concat_axis=0, tiled=True)
    return turned.transpose(1, 0, 2, 3).reshape(2, 64, 512)


def solution(mesh):
    fine = Mesh(mesh.devices.reshape(8, 4, 4, 2), ("z", "x", "y", "core"))
    patch = ("z", "x")
    in_specs = (
        P(None, patch, None), P(), P(), P(), P(None, patch), P(FRAME, None, patch),
    )
    out_specs = P(None, patch, FRAME)
    return jax.shard_map(body, mesh=fine, in_specs=in_specs, out_specs=out_specs, check_vma=False)
```

```python
import math

import jax
import jax.numpy as jnp
from jax import lax
from jax.experimental import pallas as pl
from jax.experimental.pallas import tpu as pltpu
from jax.sharding import Mesh, PartitionSpec as P


CORE = 256
HALO = 64
SPAN = 384
HALF = 256
SLAB = ("x", "y", "core")
FRAME = ("y", "core")


def split(values):
    high = values.astype(jnp.bfloat16)
    low = (values - high.astype(jnp.float32)).astype(jnp.bfloat16)
    return high, low


def dot(left, right):
    return jnp.dot(left, right, preferred_element_type=jnp.float32)


def left(matrix, rows, parts):
    totals = [None, None]
    for lanes, (high, low) in parts:
        for block in range(2):
            both = matrix[2 * block : 2 * block + 2, 0:rows, lanes].reshape(2 * rows, high.shape[0])
            term, small = dot(both, high), dot(both[0:rows], low)
            before = totals[block]
            totals[block] = (term, small) if before is None else (before[0] + term, before[1] + small)
    return tuple(term[0:rows] + (term[rows : 2 * rows] + small) for term, small in totals)


def right(parts, matrix, lanes):
    rows = parts[0][0].shape[0] // 2
    totals = [None, None]
    for part, (high, low) in enumerate(parts):
        depth = high.shape[1]
        weights = (matrix[2 * part, 0:depth, lanes], matrix[2 * part + 1, 0:depth, lanes])
        for block in range(2):
            at = slice(block * rows, block * rows + rows)
            term = dot(jnp.concatenate([high[at], low[at]], axis=0), weights[0])
            small = dot(high[at], weights[1])
            before = totals[block]
            totals[block] = (term, small) if before is None else (before[0] + term, before[1] + small)
    return jnp.concatenate(
        [term[0:rows] + (term[rows : 2 * rows] + small) for term, small in totals], axis=0
    )


def build(matrix, base, sign):
    for part in range(2):
        cosine, sine = base[2 * part], base[2 * part + 1]
        matrix[part, :, FULL] = cosine
        matrix[part, :, REST] = sine if sign > 0 else -sine
        matrix[2 + part, :, FULL] = -sine if sign > 0 else sine
        matrix[2 + part, :, REST] = cosine


def sine_cosine(angle):
    turns = jnp.round(angle * (2.0 / math.pi))
    rest = angle - turns * 1.5703125
    rest = rest - turns * 4.83826794896619e-4
    square = rest * rest
    sine = rest + rest * square * (
        -1.6666654611e-1 + square * (8.3321608736e-3 + square * -1.9515295891e-4)
    )
    cosine = 1.0 - 0.5 * square + square * square * (
        4.166664568298827e-2 + square * (-1.388731625493765e-3 + square * 2.443315711809948e-5)
    )
    quarter = turns.astype(jnp.int32)
    odd = (quarter & 1) == 1
    sine, cosine = jnp.where(odd, cosine, sine), jnp.where(odd, sine, cosine)
    sine = jnp.where((quarter & 2) == 2, -sine, sine)
    cosine = jnp.where(((quarter + 1) & 2) == 2, -cosine, cosine)
    return sine, cosine


LOW = slice(0, CORE)
HIGH = slice(SPAN, SPAN + CORE)
FULL = slice(0, SPAN)
REST = slice(SPAN, 2 * SPAN)
ALL = slice(None)


def base_kernel(base):
    block = SPAN // 8
    row = lax.broadcasted_iota(jnp.int32, (block, SPAN), 0)
    column = lax.broadcasted_iota(jnp.int32, (block, SPAN), 1)

    def fill(index, carry):
        begin = pl.multiple_of(index * block, block)
        steps = ((row + begin) * column).astype(jnp.float32)
        steps = steps - SPAN * jnp.floor((steps + 0.5) * (1.0 / SPAN))
        sine, cosine = sine_cosine(steps * (2.0 * math.pi / SPAN))
        at = pl.ds(begin, block)
        base[0, at], base[2, at] = split(cosine)
        base[1, at], base[3, at] = split(sine)
        return carry

    lax.fori_loop(0, 8, fill, 0)


def object_kernel(forward, inverse, strip, right_ref, left_ref, spec_re, spec_im):
    lane = lax.broadcasted_iota(jnp.int32, (SPAN // 2, 2 * HALO), 1)
    after, before = right_ref[...], left_ref[...]
    top = jnp.where(lane < HALO, after, pltpu.roll(before, HALO, 1))
    bottom = jnp.where(lane < HALO, pltpu.roll(after, HALO, 1), before)
    halo = jnp.concatenate([top, bottom], axis=0)
    window = jnp.concatenate([strip[...], halo], axis=1)
    window = jnp.concatenate([window[HALO:], window[:HALO]], axis=0)
    seen = split(window)
    part_re = split(right([seen], inverse, LOW))
    part_im = split(right([seen], inverse, HIGH))
    real, imag = left(forward, SPAN, [(FULL, part_re), (REST, part_im)])
    column = lax.broadcasted_iota(jnp.int32, (SPAN, HALF), 1)
    ends = (column == 0) | (column == SPAN // 2)
    weight = jnp.where(ends, 1.0, jnp.where(column < SPAN // 2, 2.0, 0.0)) / (SPAN * SPAN)
    spec_re[...] = real * weight
    spec_im[...] = imag * weight


def cut_kernel(place, screens, first, second, sems):
    at = pl.ds(pl.multiple_of(place[2], 8), 8)
    copies = [
        pltpu.make_async_copy(screens.at[layer, at, :], target, sems.at[layer])
        for layer, target in enumerate((first, second))
    ]
    for copy in copies:
        copy.start()
    for copy in copies:
        copy.wait()


def select_kernel(place, rows, cols, *refs):
    chunks, out, gathered = refs[:16], refs[16], refs[17]
    slab, first = place[0], place[1]
    for step in range(8):
        source = (slab + step) % 8
        for layer in range(2):
            gathered[source * 2 + layer] = chunks[step * 2 + layer][...]
    row_index = first + lax.broadcasted_iota(jnp.int32, (8, CORE), 0)
    lane = lax.broadcasted_iota(jnp.int32, (8, CORE), 1)

    def one(member, carry):
        patch = slab * 4 + member // 8
        frame = member % 8
        for layer in range(2):
            row = rows[frame, layer, patch]
            col = cols[frame, layer, patch]
            block, residue = row // CORE, row % CORE
            after = jnp.minimum(block + 1, 7)
            strip, turn = col // CORE, col % CORE
            at = pl.ds(pl.multiple_of(strip * CORE, CORE), CORE)
            beside = pl.ds(pl.multiple_of(jnp.minimum(strip + 1, 15) * CORE, CORE), CORE)
            right = lane >= turn
            upper = jnp.where(
                right, gathered[block * 2 + layer, :, at], gathered[block * 2 + layer, :, beside]
            )
            lower = jnp.where(
                right, gathered[after * 2 + layer, :, at], gathered[after * 2 + layer, :, beside]
            )
            out[member, layer] = jnp.where(row_index >= residue, upper, lower)
        return carry

    lax.fori_loop(0, 32, one, 0, unroll=8)


def scatter_kernel(place, rows, cols, values, *refs):
    pieces, out = refs[:16], refs[16]
    slab, first = place[0], place[1]
    row_index = first + lax.broadcasted_iota(jnp.int32, (8, CORE), 0)
    lane = lax.broadcasted_iota(jnp.int32, (8, CORE), 1)
    out[...] = jnp.zeros_like(out)

    def one(member, carry):
        patch = slab * 4 + member // 8
        frame = member % 8
        for layer in range(2):
            row = rows[frame, layer, patch]
            col = cols[frame, layer, patch]
            block, residue = row // CORE, row % CORE
            after = jnp.minimum(block + 1, 7)
            strip, turn = col // CORE, col % CORE
            beside = jnp.minimum(strip + 1, 15)
            value = values[member, layer]
            here = row_index >= residue
            right = lane >= turn
            for target, keep_row in ((block, here), (after, ~here)):
                where = (target + 8 - slab) % 8
                for place_col, keep_col in ((strip, right), (beside, ~right)):
                    at = pl.ds(pl.multiple_of((place_col % 2) * CORE, CORE), CORE)
                    chunk = place_col // 2
                    out[where, chunk, layer, :, at] = out[where, chunk, layer, :, at] + jnp.where(
                        keep_row & keep_col, value, 0.0
                    )
        return carry

    lax.fori_loop(0, 32, one, 0, unroll=4)
    for index, piece in enumerate(pieces):
        piece[...] = out[index // 2, 4 * (index % 2) : 4 * (index % 2) + 4]


def put(high, low, at, values):
    high[at], low[at] = split(values)


def inverse_sum(amplitude):
    return 1.0 / (SPAN * SPAN * jnp.sum(amplitude * amplitude))


def far_kernel(
    turns, received, amp_ref, base, forward, inverse, pupil_re, pupil_im, far_re, far_im,
    spread_re, spread_im, mix_h, mix_l,
):
    build(forward, base, 1)
    build(inverse, base, -1)
    phases = None
    for layer in range(2):
        sheet = received[:, layer].reshape(CORE, CORE)
        sheet = pltpu.roll(sheet, (CORE - turns[layer, 0]) % CORE, 0)
        sheet = pltpu.roll(sheet, (CORE - turns[layer, 1]) % CORE, 1)
        phases = sheet if phases is None else phases + sheet
    amplitude = amp_ref[...]
    inverse_total = inverse_sum(amplitude)
    sine, cosine = sine_cosine(phases)
    pupil_re[...] = amplitude * cosine
    pupil_im[...] = amplitude * sine
    half_re, half_im = left(
        forward, SPAN, [(LOW, split(pupil_re[...])), (HIGH, split(pupil_im[...]))]
    )
    half = [split(half_re), split(half_im)]
    far = right(half, inverse, ALL)
    far_re[...] = far[:, FULL]
    far_im[...] = far[:, REST]
    spread = [split((far_re[...] * far_re[...] + far_im[...] * far_im[...]) * inverse_total)]
    put(mix_h, mix_l, FULL, right(spread, inverse, LOW))
    put(mix_h, mix_l, REST, right(spread, inverse, HIGH))
    spread_re[...], spread_im[...] = left(forward, SPAN, [(ALL, (mix_h[...], mix_l[...]))])


def gradient_kernel(
    turns, amp_ref, observed, forward, inverse, pupil_re, pupil_im, far_re, far_im,
    spread_re, spread_im, spec_re, spec_im, out, mix_h, mix_l, wide_h, wide_l,
):
    inverse_total = inverse_sum(amp_ref[...])
    first, second = spread_re[...], spread_im[...]
    put(mix_h, mix_l, FULL, first * spec_re[...] - second * spec_im[...])
    put(mix_h, mix_l, REST, first * spec_im[...] + second * spec_re[...])
    first, second = left(inverse, CORE, [(ALL, (mix_h[...], mix_l[...]))])
    model = right([split(first), split(second)], forward, LOW)
    residual = [split((model - observed[0]) * float(SPAN))]
    grad_re = split(right(residual, inverse, LOW))
    grad_im = split(right(residual, inverse, HIGH))
    first, second = left(forward, SPAN, [(LOW, grad_re), (HIGH, grad_im)])
    put(mix_h, mix_l, FULL, first * spec_re[...] + second * spec_im[...])
    put(mix_h, mix_l, REST, second * spec_re[...] - first * spec_im[...])
    first, second = left(inverse, SPAN, [(ALL, (mix_h[...], mix_l[...]))])
    spread_grad = right([split(first), split(second)], forward, FULL)
    put(wide_h, wide_l, FULL, far_re[...] * spread_grad)
    put(wide_h, wide_l, REST, far_im[...] * spread_grad)
    first, second = left(inverse, CORE, [(ALL, (wide_h[...], wide_l[...]))])
    back = [split(first), split(second)]
    out_re = right(back, forward, LOW)
    out_im = right(back, forward, HIGH)
    gradient = (2.0 * inverse_total) * (pupil_re[...] * out_im - pupil_im[...] * out_re)
    for layer in range(2):
        sheet = pltpu.roll(gradient, turns[layer, 1], 1)
        sheet = pltpu.roll(sheet, turns[layer, 0], 0)
        out[:, layer] = sheet.reshape(32, 8, CORE)


SMEM = pl.BlockSpec(memory_space=pltpu.SMEM)
VMEM = pl.BlockSpec(memory_space=pltpu.VMEM)
ANY = pl.BlockSpec(memory_space=pl.ANY)


def limit(mib):
    return pltpu.CompilerParams(vmem_limit_bytes=mib << 20)


def cost(flops, moved):
    return pl.CostEstimate(flops=flops, bytes_accessed=moved, transcendentals=0)


def f32(*shape):
    return jax.ShapeDtypeStruct(shape, jnp.float32)


def far_call(*operands):
    matrix = jax.ShapeDtypeStruct((4, SPAN, 2 * SPAN), jnp.bfloat16)
    return pl.pallas_call(
        far_kernel,
        out_shape=[matrix] * 2 + [f32(CORE, CORE)] * 2 + [f32(SPAN, SPAN)] * 2 + [f32(SPAN, HALF)] * 2,
        in_specs=[SMEM] + [VMEM] * 3,
        out_specs=[VMEM] * 8,
        scratch_shapes=[pltpu.VMEM((2 * SPAN, HALF), jnp.bfloat16)] * 2,
        compiler_params=limit(28),
        cost_estimate=cost(3 * 2 * 500 * 10**6, 7 * 10**6),
        name="far_field",
    )(*operands)


def gradient_call(*operands):
    return pl.pallas_call(
        gradient_kernel,
        out_shape=f32(32, 2, 8, CORE),
        in_specs=[SMEM] + [VMEM] * 12,
        out_specs=VMEM,
        scratch_shapes=[
            pltpu.VMEM((2 * SPAN, HALF), jnp.bfloat16),
            pltpu.VMEM((2 * SPAN, HALF), jnp.bfloat16),
            pltpu.VMEM((2 * SPAN, SPAN), jnp.bfloat16),
            pltpu.VMEM((2 * SPAN, SPAN), jnp.bfloat16),
        ],
        compiler_params=limit(28),
        cost_estimate=cost(3 * 2 * 722 * 10**6, 7 * 10**6),
        name="gradient",
    )(*operands)


def up(values):
    count = lax.axis_size("z")
    return lax.ppermute(values, "z", [(i, (i + 1) % count) for i in range(count)])


def down(values):
    count = lax.axis_size("z")
    return lax.ppermute(values, "z", [((i + 1) % count, i) for i in range(count)])


def ring_gather(own):
    chunks = {(0, 0): own[0], (0, 1): own[1]}
    for step in range(1, 4):
        for layer in range(2):
            chunks[8 - step, layer] = up(chunks[(9 - step) % 8, layer])
            chunks[step, layer] = down(chunks[step - 1, layer])
    chunks[4, 0] = up(chunks[5, 0])
    chunks[4, 1] = down(chunks[3, 1])
    return [chunks[step, layer] for step in range(8) for layer in range(2)]


def ring_scatter(partial):
    top, bottom = (4, 3), (3, 4)
    rise = [partial[2 * top[half] + half] for half in range(2)]
    fall = [partial[2 * (8 - bottom[half]) + half] for half in range(2)]
    for step in range(1, 5):
        for half in range(2):
            if step <= top[half]:
                rise[half] = up(rise[half])
                if step < top[half]:
                    rise[half] = rise[half] + partial[2 * (top[half] - step) + half]
            if step <= bottom[half]:
                fall[half] = down(fall[half])
                if step < bottom[half]:
                    fall[half] = fall[half] + partial[2 * (8 - bottom[half] + step) + half]
    return jnp.concatenate([partial[half] + rise[half] + fall[half] for half in range(2)])


def body(screens, row_offsets, col_offsets, amplitude, object_strip, observed):
    slab = lax.axis_index("z")
    across = lax.axis_index("x")
    frame_id = lax.axis_index(FRAME)
    patch = slab * 4 + across
    patches = lax.axis_size("z") * lax.axis_size("x")
    place = jnp.stack([slab, across * 64 + frame_id * 8, frame_id * 8]).astype(jnp.int32)
    own = pl.pallas_call(
        cut_kernel,
        out_shape=[f32(8, screens.shape[2])] * 2,
        in_specs=[SMEM, ANY],
        out_specs=[VMEM] * 2,
        scratch_shapes=[pltpu.SemaphoreType.DMA((2,))],
        compiler_params=limit(20),
        name="cut_rows",
    )(place, screens)
    chunks = ring_gather(own)
    sent = pl.pallas_call(
        select_kernel,
        out_shape=f32(32, 2, 8, CORE),
        in_specs=[SMEM] * 3 + [VMEM] * 16,
        out_specs=VMEM,
        scratch_shapes=[pltpu.VMEM((16, 8, screens.shape[2]), jnp.float32)],
        compiler_params=limit(20),
        cost_estimate=cost(0, 3 * 10**6),
        name="select_rows",
    )(place, row_offsets, col_offsets, *chunks)
    sent, strip = lax.optimization_barrier((sent, object_strip))
    received = lax.all_to_all(sent, SLAB, split_axis=0, concat_axis=0, tiled=True)
    ends = patches - 1
    half = SPAN // 2
    tail = strip[:, CORE - HALO :]
    left_tail = lax.ppermute(
        jnp.concatenate([tail[:half], tail[half:]], axis=1),
        ("z", "x"),
        [(i, i + 1) for i in range(ends)],
    )
    head = strip[:, :HALO]
    right_head = lax.ppermute(
        jnp.concatenate([head[:half], head[half:]], axis=1),
        ("z", "x"),
        [(i + 1, i) for i in range(ends)],
    )
    base = pl.pallas_call(
        base_kernel,
        out_shape=jax.ShapeDtypeStruct((4, SPAN, SPAN), jnp.bfloat16),
        out_specs=VMEM,
        compiler_params=limit(20),
        cost_estimate=cost(10**6, 10**6),
        name="dft_base",
    )()
    row_turns = lax.dynamic_slice(row_offsets, (frame_id, 0, patch), (1, 2, 1))[0, :, 0] % CORE
    col_turns = lax.dynamic_slice(col_offsets, (frame_id, 0, patch), (1, 2, 1))[0, :, 0] % CORE
    turns = jnp.stack([row_turns, col_turns], axis=1)
    forward, inverse, *fields = far_call(turns, received, amplitude, base)
    spec_re, spec_im = pl.pallas_call(
        object_kernel,
        out_shape=[f32(SPAN, HALF)] * 2,
        in_specs=[VMEM] * 5,
        out_specs=[VMEM] * 2,
        compiler_params=limit(28),
        cost_estimate=cost(3 * 2 * 226 * 10**6, 7 * 10**6),
        name="object_spectrum",
    )(forward, inverse, strip, right_head, left_tail)
    placed = gradient_call(
        turns, amplitude, observed, forward, inverse, *fields, spec_re, spec_im
    )
    returned = lax.all_to_all(placed, SLAB, split_axis=0, concat_axis=0, tiled=True)

    partial = pl.pallas_call(
        scatter_kernel,
        out_shape=[f32(4, 2, 8, 512)] * 16,
        in_specs=[SMEM] * 3 + [VMEM],
        out_specs=[VMEM] * 16,
        scratch_shapes=[pltpu.VMEM((8, 8, 2, 8, 512), jnp.float32)],
        compiler_params=limit(20),
        cost_estimate=cost(0, 3 * 10**6),
        name="scatter_rows",
    )(place, row_offsets, col_offsets, returned)
    summed = ring_scatter(partial)
    turned = lax.all_to_all(summed, FRAME, split_axis=0, concat_axis=0, tiled=True)
    return turned.transpose(1, 0, 2, 3).reshape(2, 64, 512)


def solution(mesh):
    fine = Mesh(mesh.devices.reshape(8, 4, 4, 2), ("z", "x", "y", "core"))
    patch = ("z", "x")
    in_specs = (
        P(None, patch, None), P(), P(), P(), P(None, patch), P(FRAME, None, patch),
    )
    out_specs = P(None, patch, FRAME)
    return jax.shard_map(body, mesh=fine, in_specs=in_specs, out_specs=out_specs, check_vma=False)
```

```python
import math

import jax
import jax.numpy as jnp
from jax import lax
from jax.experimental import pallas as pl
from jax.experimental.pallas import tpu as pltpu
from jax.sharding import Mesh, PartitionSpec as P


CORE = 256
HALO = 64
SPAN = 384
HALF = 256
SLAB = ("x", "y", "core")
FRAME = ("y", "core")


def split(values):
    high = values.astype(jnp.bfloat16)
    low = (values - high.astype(jnp.float32)).astype(jnp.bfloat16)
    return high, low


def dot(left, right):
    return jnp.dot(left, right, preferred_element_type=jnp.float32)


def left(matrix, rows, parts):
    totals = [None, None]
    for lanes, (high, low) in parts:
        for block in range(2):
            both = matrix[2 * block : 2 * block + 2, 0:rows, lanes].reshape(2 * rows, high.shape[0])
            term, small = dot(both, high), dot(both[0:rows], low)
            before = totals[block]
            totals[block] = (term, small) if before is None else (before[0] + term, before[1] + small)
    return tuple(term[0:rows] + (term[rows : 2 * rows] + small) for term, small in totals)


def right(parts, matrix, lanes):
    rows = parts[0][0].shape[0] // 2
    totals = [None, None]
    for part, (high, low) in enumerate(parts):
        depth = high.shape[1]
        weights = (matrix[2 * part, 0:depth, lanes], matrix[2 * part + 1, 0:depth, lanes])
        for block in range(2):
            at = slice(block * rows, block * rows + rows)
            term = dot(jnp.concatenate([high[at], low[at]], axis=0), weights[0])
            small = dot(high[at], weights[1])
            before = totals[block]
            totals[block] = (term, small) if before is None else (before[0] + term, before[1] + small)
    return jnp.concatenate(
        [term[0:rows] + (term[rows : 2 * rows] + small) for term, small in totals], axis=0
    )


def build(matrix, base, sign):
    for part in range(2):
        cosine, sine = base[2 * part], base[2 * part + 1]
        matrix[part, :, FULL] = cosine
        matrix[part, :, REST] = sine if sign > 0 else -sine
        matrix[2 + part, :, FULL] = -sine if sign > 0 else sine
        matrix[2 + part, :, REST] = cosine


def sine_cosine(angle):
    turns = jnp.round(angle * (2.0 / math.pi))
    rest = angle - turns * 1.5703125
    rest = rest - turns * 4.83826794896619e-4
    square = rest * rest
    sine = rest + rest * square * (
        -1.6666654611e-1 + square * (8.3321608736e-3 + square * -1.9515295891e-4)
    )
    cosine = 1.0 - 0.5 * square + square * square * (
        4.166664568298827e-2 + square * (-1.388731625493765e-3 + square * 2.443315711809948e-5)
    )
    quarter = turns.astype(jnp.int32)
    odd = (quarter & 1) == 1
    sine, cosine = jnp.where(odd, cosine, sine), jnp.where(odd, sine, cosine)
    sine = jnp.where((quarter & 2) == 2, -sine, sine)
    cosine = jnp.where(((quarter + 1) & 2) == 2, -cosine, cosine)
    return sine, cosine


LOW = slice(0, CORE)
HIGH = slice(SPAN, SPAN + CORE)
FULL = slice(0, SPAN)
REST = slice(SPAN, 2 * SPAN)
ALL = slice(None)


def base_kernel(base):
    block = SPAN // 8
    row = lax.broadcasted_iota(jnp.int32, (block, SPAN), 0)
    column = lax.broadcasted_iota(jnp.int32, (block, SPAN), 1)

    def fill(index, carry):
        begin = pl.multiple_of(index * block, block)
        steps = ((row + begin) * column).astype(jnp.float32)
        steps = steps - SPAN * jnp.floor((steps + 0.5) * (1.0 / SPAN))
        sine, cosine = sine_cosine(steps * (2.0 * math.pi / SPAN))
        at = pl.ds(begin, block)
        base[0, at], base[2, at] = split(cosine)
        base[1, at], base[3, at] = split(sine)
        return carry

    lax.fori_loop(0, 8, fill, 0)


def object_kernel(forward, inverse, strip, right_ref, left_ref, spec_re, spec_im):
    lane = lax.broadcasted_iota(jnp.int32, (SPAN // 2, 2 * HALO), 1)
    after, before = right_ref[...], left_ref[...]
    top = jnp.where(lane < HALO, after, pltpu.roll(before, HALO, 1))
    bottom = jnp.where(lane < HALO, pltpu.roll(after, HALO, 1), before)
    halo = jnp.concatenate([top, bottom], axis=0)
    window = jnp.concatenate([strip[...], halo], axis=1)
    window = jnp.concatenate([window[HALO:], window[:HALO]], axis=0)
    seen = split(window)
    part_re = split(right([seen], inverse, LOW))
    part_im = split(right([seen], inverse, HIGH))
    real, imag = left(forward, SPAN, [(FULL, part_re), (REST, part_im)])
    column = lax.broadcasted_iota(jnp.int32, (SPAN, HALF), 1)
    ends = (column == 0) | (column == SPAN // 2)
    weight = jnp.where(ends, 1.0, jnp.where(column < SPAN // 2, 2.0, 0.0)) / (SPAN * SPAN)
    spec_re[...] = real * weight
    spec_im[...] = imag * weight


def cut_kernel(place, screens, first, second, sems):
    at = pl.ds(pl.multiple_of(place[0] * 8, 8), 8)
    copies = [
        pltpu.make_async_copy(screens.at[layer, at, :], target, sems.at[layer])
        for layer, target in enumerate((first, second))
    ]
    for copy in copies:
        copy.start()
    for copy in copies:
        copy.wait()


def select_kernel(place, table, *refs):
    chunks, out, gathered = refs[:16], refs[16], refs[17]
    slab, first = place[0], place[1]
    for step in range(8):
        source = (slab + step) & 7
        for layer in range(2):
            gathered[source * 2 + layer] = chunks[step * 2 + layer][...]
    row_index = first + lax.broadcasted_iota(jnp.int32, (8, CORE), 0)
    lane = lax.broadcasted_iota(jnp.int32, (8, CORE), 1)

    def one(member, carry):
        patch = slab * 4 + (member >> 3)
        frame = member & 7
        for layer in range(2):
            row = table[frame, layer, patch]
            col = table[8 + frame, layer, patch]
            block, residue = row >> 8, row & 255
            after = jnp.minimum(block + 1, 7)
            strip, turn = col >> 8, col & 255
            at = pl.ds(pl.multiple_of(strip * CORE, CORE), CORE)
            beside = pl.ds(pl.multiple_of(jnp.minimum(strip + 1, 15) * CORE, CORE), CORE)
            right = lane >= turn
            upper = jnp.where(
                right, gathered[block * 2 + layer, :, at], gathered[block * 2 + layer, :, beside]
            )
            lower = jnp.where(
                right, gathered[after * 2 + layer, :, at], gathered[after * 2 + layer, :, beside]
            )
            out[member, layer] = jnp.where(row_index >= residue, upper, lower)
        return carry

    lax.fori_loop(0, 32, one, 0, unroll=8)


def scatter_kernel(place, table, values, *refs):
    pieces, out = refs[:16], refs[16]
    slab, first = place[0], place[1]
    row_index = first + lax.broadcasted_iota(jnp.int32, (8, CORE), 0)
    lane = lax.broadcasted_iota(jnp.int32, (8, CORE), 1)
    out[...] = jnp.zeros_like(out)

    def one(member, carry):
        patch = slab * 4 + (member >> 3)
        frame = member & 7
        for layer in range(2):
            row = table[frame, layer, patch]
            col = table[8 + frame, layer, patch]
            block, residue = row >> 8, row & 255
            after = jnp.minimum(block + 1, 7)
            strip, turn = col >> 8, col & 255
            beside = jnp.minimum(strip + 1, 15)
            value = values[member, layer]
            here = row_index >= residue
            right = lane >= turn
            for target, keep_row in ((block, here), (after, ~here)):
                where = (target + 8 - slab) & 7
                for place_col, keep_col in ((strip, right), (beside, ~right)):
                    at = pl.ds(pl.multiple_of((place_col & 1) * CORE, CORE), CORE)
                    chunk = place_col >> 1
                    out[where, chunk, layer, :, at] = out[where, chunk, layer, :, at] + jnp.where(
                        keep_row & keep_col, value, 0.0
                    )
        return carry

    lax.fori_loop(0, 32, one, 0, unroll=4)
    for index, piece in enumerate(pieces):
        piece[...] = out[index // 2, 4 * (index % 2) : 4 * (index % 2) + 4]


def put(high, low, at, values):
    high[at], low[at] = split(values)


def inverse_sum(amplitude):
    return 1.0 / (SPAN * SPAN * jnp.sum(amplitude * amplitude))


def turns_of(place, table):
    frame = place[2] >> 3
    patch = place[0] * 4 + (place[1] >> 6)
    return [(table[frame, layer, patch] & 255, table[8 + frame, layer, patch] & 255) for layer in range(2)]


def far_kernel(
    place, table, received, amp_ref, base, forward, inverse, pupil_re, pupil_im, far_re, far_im,
    spread_re, spread_im, mix_h, mix_l,
):
    build(forward, base, 1)
    build(inverse, base, -1)
    turns = turns_of(place, table)
    phases = None
    for layer in range(2):
        sheet = received[:, layer].reshape(CORE, CORE)
        sheet = pltpu.roll(sheet, (CORE - turns[layer][0]) & 255, 0)
        sheet = pltpu.roll(sheet, (CORE - turns[layer][1]) & 255, 1)
        phases = sheet if phases is None else phases + sheet
    amplitude = amp_ref[...]
    inverse_total = inverse_sum(amplitude)
    sine, cosine = sine_cosine(phases)
    pupil_re[...] = amplitude * cosine
    pupil_im[...] = amplitude * sine
    half_re, half_im = left(
        forward, SPAN, [(LOW, split(pupil_re[...])), (HIGH, split(pupil_im[...]))]
    )
    half = [split(half_re), split(half_im)]
    far = right(half, inverse, ALL)
    far_re[...] = far[:, FULL]
    far_im[...] = far[:, REST]
    spread = [split((far_re[...] * far_re[...] + far_im[...] * far_im[...]) * inverse_total)]
    put(mix_h, mix_l, FULL, right(spread, inverse, LOW))
    put(mix_h, mix_l, REST, right(spread, inverse, HIGH))
    spread_re[...], spread_im[...] = left(forward, SPAN, [(ALL, (mix_h[...], mix_l[...]))])


def gradient_kernel(
    place, table, amp_ref, observed, forward, inverse, pupil_re, pupil_im, far_re, far_im,
    spread_re, spread_im, spec_re, spec_im, out, mix_h, mix_l, wide_h, wide_l,
):
    inverse_total = inverse_sum(amp_ref[...])
    first, second = spread_re[...], spread_im[...]
    put(mix_h, mix_l, FULL, first * spec_re[...] - second * spec_im[...])
    put(mix_h, mix_l, REST, first * spec_im[...] + second * spec_re[...])
    first, second = left(inverse, CORE, [(ALL, (mix_h[...], mix_l[...]))])
    model = right([split(first), split(second)], forward, LOW)
    residual = [split((model - observed[0]) * float(SPAN))]
    grad_re = split(right(residual, inverse, LOW))
    grad_im = split(right(residual, inverse, HIGH))
    first, second = left(forward, SPAN, [(LOW, grad_re), (HIGH, grad_im)])
    put(mix_h, mix_l, FULL, first * spec_re[...] + second * spec_im[...])
    put(mix_h, mix_l, REST, second * spec_re[...] - first * spec_im[...])
    first, second = left(inverse, SPAN, [(ALL, (mix_h[...], mix_l[...]))])
    spread_grad = right([split(first), split(second)], forward, FULL)
    put(wide_h, wide_l, FULL, far_re[...] * spread_grad)
    put(wide_h, wide_l, REST, far_im[...] * spread_grad)
    first, second = left(inverse, CORE, [(ALL, (wide_h[...], wide_l[...]))])
    back = [split(first), split(second)]
    out_re = right(back, forward, LOW)
    out_im = right(back, forward, HIGH)
    gradient = (2.0 * inverse_total) * (pupil_re[...] * out_im - pupil_im[...] * out_re)
    turns = turns_of(place, table)
    for layer in range(2):
        sheet = pltpu.roll(gradient, turns[layer][1], 1)
        sheet = pltpu.roll(sheet, turns[layer][0], 0)
        out[:, layer] = sheet.reshape(32, 8, CORE)


SMEM = pl.BlockSpec(memory_space=pltpu.SMEM)
VMEM = pl.BlockSpec(memory_space=pltpu.VMEM)
ANY = pl.BlockSpec(memory_space=pl.ANY)


def limit(mib):
    return pltpu.CompilerParams(vmem_limit_bytes=mib << 20)


def cost(flops, moved):
    return pl.CostEstimate(flops=flops, bytes_accessed=moved, transcendentals=0)


def f32(*shape):
    return jax.ShapeDtypeStruct(shape, jnp.float32)


def far_call(*operands):
    matrix = jax.ShapeDtypeStruct((4, SPAN, 2 * SPAN), jnp.bfloat16)
    return pl.pallas_call(
        far_kernel,
        out_shape=[matrix] * 2 + [f32(CORE, CORE)] * 2 + [f32(SPAN, SPAN)] * 2 + [f32(SPAN, HALF)] * 2,
        in_specs=[SMEM] * 2 + [VMEM] * 3,
        out_specs=[VMEM] * 8,
        scratch_shapes=[pltpu.VMEM((2 * SPAN, HALF), jnp.bfloat16)] * 2,
        compiler_params=limit(28),
        cost_estimate=cost(3 * 2 * 500 * 10**6, 7 * 10**6),
        name="far_field",
    )(*operands)


def gradient_call(*operands):
    return pl.pallas_call(
        gradient_kernel,
        out_shape=f32(32, 2, 8, CORE),
        in_specs=[SMEM] * 2 + [VMEM] * 12,
        out_specs=VMEM,
        scratch_shapes=[
            pltpu.VMEM((2 * SPAN, HALF), jnp.bfloat16),
            pltpu.VMEM((2 * SPAN, HALF), jnp.bfloat16),
            pltpu.VMEM((2 * SPAN, SPAN), jnp.bfloat16),
            pltpu.VMEM((2 * SPAN, SPAN), jnp.bfloat16),
        ],
        compiler_params=limit(28),
        cost_estimate=cost(3 * 2 * 722 * 10**6, 7 * 10**6),
        name="gradient",
    )(*operands)


def up(values):
    count = lax.axis_size("z")
    return lax.ppermute(values, "z", [(i, (i + 1) % count) for i in range(count)])


def down(values):
    count = lax.axis_size("z")
    return lax.ppermute(values, "z", [((i + 1) % count, i) for i in range(count)])


def ring_gather(own):
    chunks = {(0, 0): own[0], (0, 1): own[1]}
    for step in range(1, 4):
        for layer in range(2):
            chunks[8 - step, layer] = up(chunks[(9 - step) % 8, layer])
            chunks[step, layer] = down(chunks[step - 1, layer])
    chunks[4, 0] = up(chunks[5, 0])
    chunks[4, 1] = down(chunks[3, 1])
    return [chunks[step, layer] for step in range(8) for layer in range(2)]


def ring_scatter(partial):
    top, bottom = (4, 3), (3, 4)
    rise = [partial[2 * top[half] + half] for half in range(2)]
    fall = [partial[2 * (8 - bottom[half]) + half] for half in range(2)]
    for step in range(1, 5):
        for half in range(2):
            if step <= top[half]:
                rise[half] = up(rise[half])
                if step < top[half]:
                    rise[half] = rise[half] + partial[2 * (top[half] - step) + half]
            if step <= bottom[half]:
                fall[half] = down(fall[half])
                if step < bottom[half]:
                    fall[half] = fall[half] + partial[2 * (8 - bottom[half] + step) + half]
    return jnp.concatenate([partial[half] + rise[half] + fall[half] for half in range(2)])


def body(screens, row_offsets, col_offsets, amplitude, object_strip, observed):
    slab = lax.axis_index("z")
    across = lax.axis_index("x")
    frame_id = lax.axis_index(FRAME)
    patches = lax.axis_size("z") * lax.axis_size("x")
    place = jnp.stack([slab, across * 64 + frame_id * 8, frame_id * 8]).astype(jnp.int32)
    table = jnp.concatenate([row_offsets, col_offsets], axis=0)
    own = pl.pallas_call(
        cut_kernel,
        out_shape=[pltpu.VMEM((8, screens.shape[2]), jnp.float32)] * 2,
        in_specs=[SMEM, ANY],
        out_specs=[VMEM] * 2,
        scratch_shapes=[pltpu.SemaphoreType.DMA((2,))],
        compiler_params=limit(58),
        name="cut_rows",
    )(jnp.reshape(frame_id, (1,)).astype(jnp.int32), screens)
    chunks = ring_gather(own)
    sent = pl.pallas_call(
        select_kernel,
        out_shape=f32(32, 2, 8, CORE),
        in_specs=[SMEM] * 2 + [VMEM] * 16,
        out_specs=VMEM,
        scratch_shapes=[pltpu.VMEM((16, 8, screens.shape[2]), jnp.float32)],
        compiler_params=limit(20),
        cost_estimate=cost(0, 3 * 10**6),
        name="select_rows",
    )(place, table, *chunks)
    sent, strip = lax.optimization_barrier((sent, object_strip))
    received = lax.all_to_all(sent, SLAB, split_axis=0, concat_axis=0, tiled=True)
    ends = patches - 1
    half = SPAN // 2
    tail = strip[:, CORE - HALO :]
    left_tail = lax.ppermute(
        jnp.concatenate([tail[:half], tail[half:]], axis=1),
        ("z", "x"),
        [(i, i + 1) for i in range(ends)],
    )
    head = strip[:, :HALO]
    right_head = lax.ppermute(
        jnp.concatenate([head[:half], head[half:]], axis=1),
        ("z", "x"),
        [(i + 1, i) for i in range(ends)],
    )
    base = pl.pallas_call(
        base_kernel,
        out_shape=jax.ShapeDtypeStruct((4, SPAN, SPAN), jnp.bfloat16),
        out_specs=VMEM,
        compiler_params=limit(20),
        cost_estimate=cost(10**6, 10**6),
        name="dft_base",
    )()
    forward, inverse, *fields = far_call(place, table, received, amplitude, base)
    spec_re, spec_im = pl.pallas_call(
        object_kernel,
        out_shape=[f32(SPAN, HALF)] * 2,
        in_specs=[VMEM] * 5,
        out_specs=[VMEM] * 2,
        compiler_params=limit(28),
        cost_estimate=cost(3 * 2 * 226 * 10**6, 7 * 10**6),
        name="object_spectrum",
    )(forward, inverse, strip, right_head, left_tail)
    placed = gradient_call(
        place, table, amplitude, observed, forward, inverse, *fields, spec_re, spec_im
    )
    returned = lax.all_to_all(placed, SLAB, split_axis=0, concat_axis=0, tiled=True)

    partial = pl.pallas_call(
        scatter_kernel,
        out_shape=[f32(4, 2, 8, 512)] * 16,
        in_specs=[SMEM] * 2 + [VMEM],
        out_specs=[VMEM] * 16,
        scratch_shapes=[pltpu.VMEM((8, 8, 2, 8, 512), jnp.float32)],
        compiler_params=limit(20),
        cost_estimate=cost(0, 3 * 10**6),
        name="scatter_rows",
    )(place, table, returned)
    summed = ring_scatter(partial)
    turned = lax.all_to_all(summed, FRAME, split_axis=0, concat_axis=0, tiled=True)
    return turned.transpose(1, 0, 2, 3).reshape(2, 64, 512)


def solution(mesh):
    fine = Mesh(mesh.devices.reshape(8, 4, 4, 2), ("z", "x", "y", "core"))
    patch = ("z", "x")
    in_specs = (
        P(None, patch, None), P(), P(), P(), P(None, patch), P(FRAME, None, patch),
    )
    out_specs = P(None, patch, FRAME)
    return jax.shard_map(body, mesh=fine, in_specs=in_specs, out_specs=out_specs, check_vma=False)
```

```python
import math

import jax
import jax.numpy as jnp
from jax import lax
from jax.experimental import pallas as pl
from jax.experimental.pallas import tpu as pltpu
from jax.sharding import Mesh, PartitionSpec as P


CORE = 256
HALO = 64
SPAN = 384
SCOLS = 4096
HALF = 256
SLAB = ("x", "y", "core")
FRAME = ("y", "core")


def split(values):
    high = values.astype(jnp.bfloat16)
    low = (values - high.astype(jnp.float32)).astype(jnp.bfloat16)
    return high, low


def dot(left, right):
    return jnp.dot(left, right, preferred_element_type=jnp.float32)


def left(matrix, rows, parts):
    totals = [None, None]
    for lanes, (high, low) in parts:
        for block in range(2):
            both = matrix[2 * block : 2 * block + 2, 0:rows, lanes].reshape(2 * rows, high.shape[0])
            term, small = dot(both, high), dot(both[0:rows], low)
            before = totals[block]
            totals[block] = (term, small) if before is None else (before[0] + term, before[1] + small)
    return tuple(term[0:rows] + (term[rows : 2 * rows] + small) for term, small in totals)


def right(parts, matrix, lanes):
    rows = parts[0][0].shape[0] // 2
    totals = [None, None]
    for part, (high, low) in enumerate(parts):
        depth = high.shape[1]
        weights = (matrix[2 * part, 0:depth, lanes], matrix[2 * part + 1, 0:depth, lanes])
        for block in range(2):
            at = slice(block * rows, block * rows + rows)
            term = dot(jnp.concatenate([high[at], low[at]], axis=0), weights[0])
            small = dot(high[at], weights[1])
            before = totals[block]
            totals[block] = (term, small) if before is None else (before[0] + term, before[1] + small)
    return jnp.concatenate(
        [term[0:rows] + (term[rows : 2 * rows] + small) for term, small in totals], axis=0
    )


def build(matrix, base, sign):
    for part in range(2):
        cosine, sine = base[2 * part], base[2 * part + 1]
        matrix[part, :, FULL] = cosine
        matrix[part, :, REST] = sine if sign > 0 else -sine
        matrix[2 + part, :, FULL] = -sine if sign > 0 else sine
        matrix[2 + part, :, REST] = cosine


def sine_cosine(angle):
    turns = jnp.round(angle * (2.0 / math.pi))
    rest = angle - turns * 1.5703125
    rest = rest - turns * 4.83826794896619e-4
    square = rest * rest
    sine = rest + rest * square * (
        -1.6666654611e-1 + square * (8.3321608736e-3 + square * -1.9515295891e-4)
    )
    cosine = 1.0 - 0.5 * square + square * square * (
        4.166664568298827e-2 + square * (-1.388731625493765e-3 + square * 2.443315711809948e-5)
    )
    quarter = turns.astype(jnp.int32)
    odd = (quarter & 1) == 1
    sine, cosine = jnp.where(odd, cosine, sine), jnp.where(odd, sine, cosine)
    sine = jnp.where((quarter & 2) == 2, -sine, sine)
    cosine = jnp.where(((quarter + 1) & 2) == 2, -cosine, cosine)
    return sine, cosine


LOW = slice(0, CORE)
HIGH = slice(SPAN, SPAN + CORE)
FULL = slice(0, SPAN)
REST = slice(SPAN, 2 * SPAN)
ALL = slice(None)


def base_kernel(base):
    block = SPAN // 8
    row = lax.broadcasted_iota(jnp.int32, (block, SPAN), 0)
    column = lax.broadcasted_iota(jnp.int32, (block, SPAN), 1)

    def fill(index, carry):
        begin = pl.multiple_of(index * block, block)
        steps = ((row + begin) * column).astype(jnp.float32)
        steps = steps - SPAN * jnp.floor((steps + 0.5) * (1.0 / SPAN))
        sine, cosine = sine_cosine(steps * (2.0 * math.pi / SPAN))
        at = pl.ds(begin, block)
        base[0, at], base[2, at] = split(cosine)
        base[1, at], base[3, at] = split(sine)
        return carry

    lax.fori_loop(0, 8, fill, 0)


def object_kernel(place, forward, inverse, strip, mine, other, spec_re, spec_im):
    lane = lax.broadcasted_iota(jnp.int32, (SPAN // 2, 2 * HALO), 1)
    first = ((place[2] >> 3) & 1) == 0
    before = jnp.where(first, mine[...], other[...])
    after = jnp.where(first, other[...], mine[...])
    top = jnp.where(lane < HALO, after, pltpu.roll(before, HALO, 1))
    bottom = jnp.where(lane < HALO, pltpu.roll(after, HALO, 1), before)
    halo = jnp.concatenate([top, bottom], axis=0)
    window = jnp.concatenate([strip[...], halo], axis=1)
    window = jnp.concatenate([window[HALO:], window[:HALO]], axis=0)
    seen = split(window)
    part_re = split(right([seen], inverse, LOW))
    part_im = split(right([seen], inverse, HIGH))
    real, imag = left(forward, SPAN, [(FULL, part_re), (REST, part_im)])
    column = lax.broadcasted_iota(jnp.int32, (SPAN, HALF), 1)
    ends = (column == 0) | (column == SPAN // 2)
    weight = jnp.where(ends, 1.0, jnp.where(column < SPAN // 2, 2.0, 0.0)) / (SPAN * SPAN)
    spec_re[...] = real * weight
    spec_im[...] = imag * weight


def cut_kernel(place, screens, first, second, sems):
    at = pl.ds(pl.multiple_of(place[0] * 8, 8), 8)
    copies = [
        pltpu.make_async_copy(screens.at[layer, at, :], target, sems.at[layer])
        for layer, target in enumerate((first, second))
    ]
    for copy in copies:
        copy.start()
    for copy in copies:
        copy.wait()


def select_kernel(place, table, *refs):
    chunks, out, gathered = refs[:16], refs[16], refs[17]
    slab, first = place[0], place[1]
    for step in range(8):
        source = (slab + step) & 7
        for layer in range(2):
            gathered[source * 2 + layer] = chunks[step * 2 + layer][...]
    row_index = first + lax.broadcasted_iota(jnp.int32, (8, CORE), 0)
    lane = lax.broadcasted_iota(jnp.int32, (8, CORE), 1)

    def one(member, carry):
        patch = slab * 4 + (member >> 3)
        frame = member & 7
        for layer in range(2):
            both = table[frame, layer, patch]
            row, col = both >> 12, both & (SCOLS - 1)
            block, residue = row >> 8, row & 255
            after = jnp.minimum(block + 1, 7)
            strip, turn = col >> 8, col & 255
            at = pl.ds(pl.multiple_of(strip * CORE, CORE), CORE)
            beside = pl.ds(pl.multiple_of(jnp.minimum(strip + 1, 15) * CORE, CORE), CORE)
            right = lane >= turn
            upper = jnp.where(
                right, gathered[block * 2 + layer, :, at], gathered[block * 2 + layer, :, beside]
            )
            lower = jnp.where(
                right, gathered[after * 2 + layer, :, at], gathered[after * 2 + layer, :, beside]
            )
            out[member, layer] = jnp.where(row_index >= residue, upper, lower)
        return carry

    lax.fori_loop(0, 32, one, 0, unroll=8)


def scatter_kernel(place, table, values, *refs):
    pieces, out = refs[:16], refs[16]
    slab, first = place[0], place[1]
    row_index = first + lax.broadcasted_iota(jnp.int32, (8, CORE), 0)
    lane = lax.broadcasted_iota(jnp.int32, (8, CORE), 1)
    out[...] = jnp.zeros_like(out)

    def one(member, carry):
        patch = slab * 4 + (member >> 3)
        frame = member & 7
        for layer in range(2):
            both = table[frame, layer, patch]
            row, col = both >> 12, both & (SCOLS - 1)
            block, residue = row >> 8, row & 255
            after = jnp.minimum(block + 1, 7)
            strip, turn = col >> 8, col & 255
            beside = jnp.minimum(strip + 1, 15)
            value = values[member, layer]
            here = row_index >= residue
            right = lane >= turn
            for target, keep_row in ((block, here), (after, ~here)):
                where = (target + 8 - slab) & 7
                for place_col, keep_col in ((strip, right), (beside, ~right)):
                    at = pl.ds(pl.multiple_of((place_col & 1) * CORE, CORE), CORE)
                    chunk = place_col >> 1
                    out[where, chunk, layer, :, at] = out[where, chunk, layer, :, at] + jnp.where(
                        keep_row & keep_col, value, 0.0
                    )
        return carry

    lax.fori_loop(0, 32, one, 0, unroll=4)
    for index, piece in enumerate(pieces):
        piece[...] = out[index // 2, 4 * (index % 2) : 4 * (index % 2) + 4]


def put(high, low, at, values):
    high[at], low[at] = split(values)


def inverse_sum(amplitude):
    return 1.0 / (SPAN * SPAN * jnp.sum(amplitude * amplitude))


def turns_of(place, table):
    frame = place[2] >> 3
    patch = place[0] * 4 + (place[1] >> 6)
    both = [table[frame, layer, patch] for layer in range(2)]
    return [((value >> 12) & 255, value & 255) for value in both]


def far_kernel(
    place, table, received, amp_ref, base, forward, inverse, pupil_re, pupil_im, far_re, far_im,
    spread_re, spread_im, mix_h, mix_l,
):
    build(forward, base, 1)
    build(inverse, base, -1)
    turns = turns_of(place, table)
    phases = None
    for layer in range(2):
        sheet = received[:, layer].reshape(CORE, CORE)
        sheet = pltpu.roll(sheet, (CORE - turns[layer][0]) & 255, 0)
        sheet = pltpu.roll(sheet, (CORE - turns[layer][1]) & 255, 1)
        phases = sheet if phases is None else phases + sheet
    amplitude = amp_ref[...]
    inverse_total = inverse_sum(amplitude)
    sine, cosine = sine_cosine(phases)
    pupil_re[...] = amplitude * cosine
    pupil_im[...] = amplitude * sine
    half_re, half_im = left(
        forward, SPAN, [(LOW, split(pupil_re[...])), (HIGH, split(pupil_im[...]))]
    )
    half = [split(half_re), split(half_im)]
    far = right(half, inverse, ALL)
    far_re[...] = far[:, FULL]
    far_im[...] = far[:, REST]
    spread = [split((far_re[...] * far_re[...] + far_im[...] * far_im[...]) * inverse_total)]
    put(mix_h, mix_l, FULL, right(spread, inverse, LOW))
    put(mix_h, mix_l, REST, right(spread, inverse, HIGH))
    spread_re[...], spread_im[...] = left(forward, SPAN, [(ALL, (mix_h[...], mix_l[...]))])


def gradient_kernel(
    place, table, amp_ref, observed, forward, inverse, pupil_re, pupil_im, far_re, far_im,
    spread_re, spread_im, spec_re, spec_im, out, mix_h, mix_l, wide_h, wide_l,
):
    inverse_total = inverse_sum(amp_ref[...])
    first, second = spread_re[...], spread_im[...]
    put(mix_h, mix_l, FULL, first * spec_re[...] - second * spec_im[...])
    put(mix_h, mix_l, REST, first * spec_im[...] + second * spec_re[...])
    first, second = left(inverse, CORE, [(ALL, (mix_h[...], mix_l[...]))])
    model = right([split(first), split(second)], forward, LOW)
    residual = [split((model - observed[0]) * float(SPAN))]
    grad_re = split(right(residual, inverse, LOW))
    grad_im = split(right(residual, inverse, HIGH))
    first, second = left(forward, SPAN, [(LOW, grad_re), (HIGH, grad_im)])
    put(mix_h, mix_l, FULL, first * spec_re[...] + second * spec_im[...])
    put(mix_h, mix_l, REST, second * spec_re[...] - first * spec_im[...])
    first, second = left(inverse, SPAN, [(ALL, (mix_h[...], mix_l[...]))])
    spread_grad = right([split(first), split(second)], forward, FULL)
    put(wide_h, wide_l, FULL, far_re[...] * spread_grad)
    put(wide_h, wide_l, REST, far_im[...] * spread_grad)
    first, second = left(inverse, CORE, [(ALL, (wide_h[...], wide_l[...]))])
    back = [split(first), split(second)]
    out_re = right(back, forward, LOW)
    out_im = right(back, forward, HIGH)
    gradient = (2.0 * inverse_total) * (pupil_re[...] * out_im - pupil_im[...] * out_re)
    turns = turns_of(place, table)
    for layer in range(2):
        sheet = pltpu.roll(gradient, turns[layer][1], 1)
        sheet = pltpu.roll(sheet, turns[layer][0], 0)
        out[:, layer] = sheet.reshape(32, 8, CORE)


SMEM = pl.BlockSpec(memory_space=pltpu.SMEM)
VMEM = pl.BlockSpec(memory_space=pltpu.VMEM)
ANY = pl.BlockSpec(memory_space=pl.ANY)


def limit(mib):
    return pltpu.CompilerParams(vmem_limit_bytes=mib << 20)


def cost(flops, moved):
    return pl.CostEstimate(flops=flops, bytes_accessed=moved, transcendentals=0)


def f32(*shape):
    return jax.ShapeDtypeStruct(shape, jnp.float32)


def far_call(*operands):
    matrix = jax.ShapeDtypeStruct((4, SPAN, 2 * SPAN), jnp.bfloat16)
    return pl.pallas_call(
        far_kernel,
        out_shape=[matrix] * 2 + [f32(CORE, CORE)] * 2 + [f32(SPAN, SPAN)] * 2 + [f32(SPAN, HALF)] * 2,
        in_specs=[SMEM] * 2 + [VMEM] * 3,
        out_specs=[VMEM] * 8,
        scratch_shapes=[pltpu.VMEM((2 * SPAN, HALF), jnp.bfloat16)] * 2,
        compiler_params=limit(28),
        cost_estimate=cost(3 * 2 * 500 * 10**6, 7 * 10**6),
        name="far_field",
    )(*operands)


def gradient_call(*operands):
    return pl.pallas_call(
        gradient_kernel,
        out_shape=f32(32, 2, 8, CORE),
        in_specs=[SMEM] * 2 + [VMEM] * 12,
        out_specs=VMEM,
        scratch_shapes=[
            pltpu.VMEM((2 * SPAN, HALF), jnp.bfloat16),
            pltpu.VMEM((2 * SPAN, HALF), jnp.bfloat16),
            pltpu.VMEM((2 * SPAN, SPAN), jnp.bfloat16),
            pltpu.VMEM((2 * SPAN, SPAN), jnp.bfloat16),
        ],
        compiler_params=limit(28),
        cost_estimate=cost(3 * 2 * 722 * 10**6, 7 * 10**6),
        name="gradient",
    )(*operands)


def up(values):
    count = lax.axis_size("z")
    return lax.ppermute(values, "z", [(i, (i + 1) % count) for i in range(count)])


def down(values):
    count = lax.axis_size("z")
    return lax.ppermute(values, "z", [((i + 1) % count, i) for i in range(count)])


def ring_gather(own):
    chunks = {(0, 0): own[0], (0, 1): own[1]}
    for step in range(1, 4):
        for layer in range(2):
            chunks[8 - step, layer] = up(chunks[(9 - step) % 8, layer])
            chunks[step, layer] = down(chunks[step - 1, layer])
    chunks[4, 0] = up(chunks[5, 0])
    chunks[4, 1] = down(chunks[3, 1])
    return [chunks[step, layer] for step in range(8) for layer in range(2)]


def ring_scatter(partial):
    top, bottom = (4, 3), (3, 4)
    rise = [partial[2 * top[half] + half] for half in range(2)]
    fall = [partial[2 * (8 - bottom[half]) + half] for half in range(2)]
    for step in range(1, 5):
        for half in range(2):
            if step <= top[half]:
                rise[half] = up(rise[half])
                if step < top[half]:
                    rise[half] = rise[half] + partial[2 * (top[half] - step) + half]
            if step <= bottom[half]:
                fall[half] = down(fall[half])
                if step < bottom[half]:
                    fall[half] = fall[half] + partial[2 * (8 - bottom[half] + step) + half]
    return jnp.concatenate([partial[half] + rise[half] + fall[half] for half in range(2)])


def body(screens, row_offsets, col_offsets, amplitude, object_strip, observed):
    slab = lax.axis_index("z")
    across = lax.axis_index("x")
    frame_id = lax.axis_index(FRAME)
    patches = lax.axis_size("z") * lax.axis_size("x")
    place = jnp.stack([slab, across * 64 + frame_id * 8, frame_id * 8]).astype(jnp.int32)
    table = row_offsets * SCOLS + col_offsets
    own = pl.pallas_call(
        cut_kernel,
        out_shape=[pltpu.VMEM((8, screens.shape[2]), jnp.float32)] * 2,
        in_specs=[SMEM, ANY],
        out_specs=[VMEM] * 2,
        scratch_shapes=[pltpu.SemaphoreType.DMA((2,))],
        compiler_params=limit(58),
        name="cut_rows",
    )(jnp.reshape(frame_id, (1,)).astype(jnp.int32), screens)
    chunks = ring_gather(own)
    sent = pl.pallas_call(
        select_kernel,
        out_shape=f32(32, 2, 8, CORE),
        in_specs=[SMEM] * 2 + [VMEM] * 16,
        out_specs=VMEM,
        scratch_shapes=[pltpu.VMEM((16, 8, screens.shape[2]), jnp.float32)],
        compiler_params=limit(20),
        cost_estimate=cost(0, 3 * 10**6),
        name="select_rows",
    )(place, table, *chunks)
    sent, strip = lax.optimization_barrier((sent, object_strip))
    received = lax.all_to_all(sent, SLAB, split_axis=0, concat_axis=0, tiled=True)
    ends = patches - 1
    half = SPAN // 2
    core = lax.axis_index("core")
    tail, head = strip[:, CORE - HALO :], strip[:, :HALO]
    edge = jnp.where(core == 0, tail, head)
    mine = lax.ppermute(
        jnp.concatenate([edge[:half], edge[half:]], axis=1),
        ("z", "x", "core"),
        [(2 * i, 2 * i + 2) for i in range(ends)]
        + [(2 * i + 3, 2 * i + 1) for i in range(ends)],
    )
    other = lax.ppermute(mine, "core", [(0, 1), (1, 0)])
    base = pl.pallas_call(
        base_kernel,
        out_shape=jax.ShapeDtypeStruct((4, SPAN, SPAN), jnp.bfloat16),
        out_specs=VMEM,
        compiler_params=limit(20),
        cost_estimate=cost(10**6, 10**6),
        name="dft_base",
    )()
    forward, inverse, *fields = far_call(place, table, received, amplitude, base)
    spec_re, spec_im = pl.pallas_call(
        object_kernel,
        out_shape=[f32(SPAN, HALF)] * 2,
        in_specs=[SMEM] + [VMEM] * 5,
        out_specs=[VMEM] * 2,
        compiler_params=limit(28),
        cost_estimate=cost(3 * 2 * 226 * 10**6, 7 * 10**6),
        name="object_spectrum",
    )(place, forward, inverse, strip, mine, other)
    placed = gradient_call(
        place, table, amplitude, observed, forward, inverse, *fields, spec_re, spec_im
    )
    returned = lax.all_to_all(placed, SLAB, split_axis=0, concat_axis=0, tiled=True)

    partial = pl.pallas_call(
        scatter_kernel,
        out_shape=[f32(4, 2, 8, 512)] * 16,
        in_specs=[SMEM] * 2 + [VMEM],
        out_specs=[VMEM] * 16,
        scratch_shapes=[pltpu.VMEM((8, 8, 2, 8, 512), jnp.float32)],
        compiler_params=limit(20),
        cost_estimate=cost(0, 3 * 10**6),
        name="scatter_rows",
    )(place, table, returned)
    summed = ring_scatter(partial)
    turned = lax.all_to_all(summed, FRAME, split_axis=0, concat_axis=0, tiled=True)
    return turned.transpose(1, 0, 2, 3).reshape(2, 64, 512)


def solution(mesh):
    fine = Mesh(mesh.devices.reshape(8, 4, 4, 2), ("z", "x", "y", "core"))
    patch = ("z", "x")
    in_specs = (
        P(None, patch, None), P(), P(), P(), P(None, patch), P(FRAME, None, patch),
    )
    out_specs = P(None, patch, FRAME)
    return jax.shard_map(body, mesh=fine, in_specs=in_specs, out_specs=out_specs, check_vma=False)
```

```python
import math

import jax
import jax.numpy as jnp
from jax import lax
from jax.experimental import pallas as pl
from jax.experimental.pallas import tpu as pltpu
from jax.sharding import Mesh, PartitionSpec as P


CORE = 256
HALO = 64
SPAN = 384
SCOLS = 4096
HALF = 256
SLAB = ("x", "y", "core")
FRAME = ("y", "core")


def split(values):
    high = values.astype(jnp.bfloat16)
    low = (values - high.astype(jnp.float32)).astype(jnp.bfloat16)
    return high, low


def dot(left, right):
    return jnp.dot(left, right, preferred_element_type=jnp.float32)


def left(matrix, rows, parts):
    totals = [None, None]
    for lanes, (high, low) in parts:
        for block in range(2):
            both = matrix[2 * block : 2 * block + 2, 0:rows, lanes].reshape(2 * rows, high.shape[0])
            term, small = dot(both, high), dot(both[0:rows], low)
            before = totals[block]
            totals[block] = (term, small) if before is None else (before[0] + term, before[1] + small)
    return tuple(term[0:rows] + (term[rows : 2 * rows] + small) for term, small in totals)


def right(parts, matrix, lanes):
    rows = parts[0][0].shape[0] // 2
    totals = [None, None]
    for part, (high, low) in enumerate(parts):
        depth = high.shape[1]
        weights = (matrix[2 * part, 0:depth, lanes], matrix[2 * part + 1, 0:depth, lanes])
        for block in range(2):
            at = slice(block * rows, block * rows + rows)
            term = dot(jnp.concatenate([high[at], low[at]], axis=0), weights[0])
            small = dot(high[at], weights[1])
            before = totals[block]
            totals[block] = (term, small) if before is None else (before[0] + term, before[1] + small)
    return jnp.concatenate(
        [term[0:rows] + (term[rows : 2 * rows] + small) for term, small in totals], axis=0
    )


def build(matrix, base, sign):
    for part in range(2):
        cosine, sine = base[2 * part], base[2 * part + 1]
        matrix[part, :, FULL] = cosine
        matrix[part, :, REST] = sine if sign > 0 else -sine
        matrix[2 + part, :, FULL] = -sine if sign > 0 else sine
        matrix[2 + part, :, REST] = cosine


def sine_cosine(angle):
    turns = jnp.round(angle * (2.0 / math.pi))
    rest = angle - turns * 1.5703125
    rest = rest - turns * 4.83826794896619e-4
    square = rest * rest
    sine = rest + rest * square * (
        -1.6666654611e-1 + square * (8.3321608736e-3 + square * -1.9515295891e-4)
    )
    cosine = 1.0 - 0.5 * square + square * square * (
        4.166664568298827e-2 + square * (-1.388731625493765e-3 + square * 2.443315711809948e-5)
    )
    quarter = turns.astype(jnp.int32)
    odd = (quarter & 1) == 1
    sine, cosine = jnp.where(odd, cosine, sine), jnp.where(odd, sine, cosine)
    sine = jnp.where((quarter & 2) == 2, -sine, sine)
    cosine = jnp.where(((quarter + 1) & 2) == 2, -cosine, cosine)
    return sine, cosine


LOW = slice(0, CORE)
HIGH = slice(SPAN, SPAN + CORE)
FULL = slice(0, SPAN)
REST = slice(SPAN, 2 * SPAN)
ALL = slice(None)


def frame_index():
    return lax.axis_index("y") * 2 + lax.axis_index("core")


def base_kernel(base):
    block = SPAN // 8
    row = lax.broadcasted_iota(jnp.int32, (block, SPAN), 0)
    column = lax.broadcasted_iota(jnp.int32, (block, SPAN), 1)

    def fill(index, carry):
        begin = pl.multiple_of(index * block, block)
        steps = ((row + begin) * column).astype(jnp.float32)
        steps = steps - SPAN * jnp.floor((steps + 0.5) * (1.0 / SPAN))
        sine, cosine = sine_cosine(steps * (2.0 * math.pi / SPAN))
        at = pl.ds(begin, block)
        base[0, at], base[2, at] = split(cosine)
        base[1, at], base[3, at] = split(sine)
        return carry

    lax.fori_loop(0, 8, fill, 0)


def object_kernel(forward, inverse, strip, mine, other, spec_re, spec_im):
    lane = lax.broadcasted_iota(jnp.int32, (SPAN // 2, 2 * HALO), 1)
    first = lax.axis_index("core") == 0
    before = jnp.where(first, mine[...], other[...])
    after = jnp.where(first, other[...], mine[...])
    top = jnp.where(lane < HALO, after, pltpu.roll(before, HALO, 1))
    bottom = jnp.where(lane < HALO, pltpu.roll(after, HALO, 1), before)
    halo = jnp.concatenate([top, bottom], axis=0)
    window = jnp.concatenate([strip[...], halo], axis=1)
    window = jnp.concatenate([window[HALO:], window[:HALO]], axis=0)
    seen = split(window)
    part_re = split(right([seen], inverse, LOW))
    part_im = split(right([seen], inverse, HIGH))
    real, imag = left(forward, SPAN, [(FULL, part_re), (REST, part_im)])
    column = lax.broadcasted_iota(jnp.int32, (SPAN, HALF), 1)
    ends = (column == 0) | (column == SPAN // 2)
    weight = jnp.where(ends, 1.0, jnp.where(column < SPAN // 2, 2.0, 0.0)) / (SPAN * SPAN)
    spec_re[...] = real * weight
    spec_im[...] = imag * weight


def cut_kernel(screens, first, second, sems):
    at = pl.ds(pl.multiple_of(frame_index() * 8, 8), 8)
    copies = [
        pltpu.make_async_copy(screens.at[layer, at, :], target, sems.at[layer])
        for layer, target in enumerate((first, second))
    ]
    for copy in copies:
        copy.start()
    for copy in copies:
        copy.wait()


def select_kernel(table, *refs):
    chunks, out, gathered = refs[:16], refs[16], refs[17]
    slab, first = lax.axis_index("z"), lax.axis_index("x") * 64 + frame_index() * 8
    for step in range(8):
        source = (slab + step) & 7
        for layer in range(2):
            gathered[source * 2 + layer] = chunks[step * 2 + layer][...]
    row_index = first + lax.broadcasted_iota(jnp.int32, (8, CORE), 0)
    lane = lax.broadcasted_iota(jnp.int32, (8, CORE), 1)

    def one(member, carry):
        patch = slab * 4 + (member >> 3)
        frame = member & 7
        for layer in range(2):
            both = table[frame, layer, patch]
            row, col = both >> 12, both & (SCOLS - 1)
            block, residue = row >> 8, row & 255
            after = jnp.minimum(block + 1, 7)
            strip, turn = col >> 8, col & 255
            at = pl.ds(pl.multiple_of(strip * CORE, CORE), CORE)
            beside = pl.ds(pl.multiple_of(jnp.minimum(strip + 1, 15) * CORE, CORE), CORE)
            right = lane >= turn
            upper = jnp.where(
                right, gathered[block * 2 + layer, :, at], gathered[block * 2 + layer, :, beside]
            )
            lower = jnp.where(
                right, gathered[after * 2 + layer, :, at], gathered[after * 2 + layer, :, beside]
            )
            out[member, layer] = jnp.where(row_index >= residue, upper, lower)
        return carry

    lax.fori_loop(0, 32, one, 0, unroll=8)


def scatter_kernel(table, values, *refs):
    pieces, out = refs[:16], refs[16]
    slab, first = lax.axis_index("z"), lax.axis_index("x") * 64 + frame_index() * 8
    row_index = first + lax.broadcasted_iota(jnp.int32, (8, CORE), 0)
    lane = lax.broadcasted_iota(jnp.int32, (8, CORE), 1)
    out[...] = jnp.zeros_like(out)

    def one(member, carry):
        patch = slab * 4 + (member >> 3)
        frame = member & 7
        for layer in range(2):
            both = table[frame, layer, patch]
            row, col = both >> 12, both & (SCOLS - 1)
            block, residue = row >> 8, row & 255
            after = jnp.minimum(block + 1, 7)
            strip, turn = col >> 8, col & 255
            beside = jnp.minimum(strip + 1, 15)
            value = values[member, layer]
            here = row_index >= residue
            right = lane >= turn
            for target, keep_row in ((block, here), (after, ~here)):
                where = (target + 8 - slab) & 7
                for place_col, keep_col in ((strip, right), (beside, ~right)):
                    at = pl.ds(pl.multiple_of((place_col & 1) * CORE, CORE), CORE)
                    chunk = place_col >> 1
                    out[where, chunk, layer, :, at] = out[where, chunk, layer, :, at] + jnp.where(
                        keep_row & keep_col, value, 0.0
                    )
        return carry

    lax.fori_loop(0, 32, one, 0, unroll=4)
    for index, piece in enumerate(pieces):
        piece[...] = out[index // 2, 4 * (index % 2) : 4 * (index % 2) + 4]


def put(high, low, at, values):
    high[at], low[at] = split(values)


def inverse_sum(amplitude):
    return 1.0 / (SPAN * SPAN * jnp.sum(amplitude * amplitude))


def turns_of(table):
    frame = frame_index()
    patch = lax.axis_index("z") * 4 + lax.axis_index("x")
    both = [table[frame, layer, patch] for layer in range(2)]
    return [((value >> 12) & 255, value & 255) for value in both]


def far_kernel(
    table, received, amp_ref, base, forward, inverse, pupil_re, pupil_im, far_re, far_im,
    spread_re, spread_im, mix_h, mix_l,
):
    build(forward, base, 1)
    build(inverse, base, -1)
    turns = turns_of(table)
    phases = None
    for layer in range(2):
        sheet = received[:, layer].reshape(CORE, CORE)
        sheet = pltpu.roll(sheet, (CORE - turns[layer][0]) & 255, 0)
        sheet = pltpu.roll(sheet, (CORE - turns[layer][1]) & 255, 1)
        phases = sheet if phases is None else phases + sheet
    amplitude = amp_ref[...]
    inverse_total = inverse_sum(amplitude)
    sine, cosine = sine_cosine(phases)
    pupil_re[...] = amplitude * cosine
    pupil_im[...] = amplitude * sine
    half_re, half_im = left(
        forward, SPAN, [(LOW, split(pupil_re[...])), (HIGH, split(pupil_im[...]))]
    )
    half = [split(half_re), split(half_im)]
    far = right(half, inverse, ALL)
    far_re[...] = far[:, FULL]
    far_im[...] = far[:, REST]
    spread = [split((far_re[...] * far_re[...] + far_im[...] * far_im[...]) * inverse_total)]
    put(mix_h, mix_l, FULL, right(spread, inverse, LOW))
    put(mix_h, mix_l, REST, right(spread, inverse, HIGH))
    spread_re[...], spread_im[...] = left(forward, SPAN, [(ALL, (mix_h[...], mix_l[...]))])


def gradient_kernel(
    table, amp_ref, observed, forward, inverse, pupil_re, pupil_im, far_re, far_im,
    spread_re, spread_im, spec_re, spec_im, out, mix_h, mix_l, wide_h, wide_l,
):
    inverse_total = inverse_sum(amp_ref[...])
    first, second = spread_re[...], spread_im[...]
    put(mix_h, mix_l, FULL, first * spec_re[...] - second * spec_im[...])
    put(mix_h, mix_l, REST, first * spec_im[...] + second * spec_re[...])
    first, second = left(inverse, CORE, [(ALL, (mix_h[...], mix_l[...]))])
    model = right([split(first), split(second)], forward, LOW)
    residual = [split((model - observed[0]) * float(SPAN))]
    grad_re = split(right(residual, inverse, LOW))
    grad_im = split(right(residual, inverse, HIGH))
    first, second = left(forward, SPAN, [(LOW, grad_re), (HIGH, grad_im)])
    put(mix_h, mix_l, FULL, first * spec_re[...] + second * spec_im[...])
    put(mix_h, mix_l, REST, second * spec_re[...] - first * spec_im[...])
    first, second = left(inverse, SPAN, [(ALL, (mix_h[...], mix_l[...]))])
    spread_grad = right([split(first), split(second)], forward, FULL)
    put(wide_h, wide_l, FULL, far_re[...] * spread_grad)
    put(wide_h, wide_l, REST, far_im[...] * spread_grad)
    first, second = left(inverse, CORE, [(ALL, (wide_h[...], wide_l[...]))])
    back = [split(first), split(second)]
    out_re = right(back, forward, LOW)
    out_im = right(back, forward, HIGH)
    gradient = (2.0 * inverse_total) * (pupil_re[...] * out_im - pupil_im[...] * out_re)
    turns = turns_of(table)
    for layer in range(2):
        sheet = pltpu.roll(gradient, turns[layer][1], 1)
        sheet = pltpu.roll(sheet, turns[layer][0], 0)
        out[:, layer] = sheet.reshape(32, 8, CORE)


SMEM = pl.BlockSpec(memory_space=pltpu.SMEM)
VMEM = pl.BlockSpec(memory_space=pltpu.VMEM)
ANY = pl.BlockSpec(memory_space=pl.ANY)


def limit(mib):
    return pltpu.CompilerParams(vmem_limit_bytes=mib << 20)


def cost(flops, moved):
    return pl.CostEstimate(flops=flops, bytes_accessed=moved, transcendentals=0)


def f32(*shape):
    return jax.ShapeDtypeStruct(shape, jnp.float32)


def far_call(*operands):
    matrix = jax.ShapeDtypeStruct((4, SPAN, 2 * SPAN), jnp.bfloat16)
    return pl.pallas_call(
        far_kernel,
        out_shape=[matrix] * 2 + [f32(CORE, CORE)] * 2 + [f32(SPAN, SPAN)] * 2 + [f32(SPAN, HALF)] * 2,
        in_specs=[SMEM] + [VMEM] * 3,
        out_specs=[VMEM] * 8,
        scratch_shapes=[pltpu.VMEM((2 * SPAN, HALF), jnp.bfloat16)] * 2,
        compiler_params=limit(28),
        cost_estimate=cost(3 * 2 * 500 * 10**6, 7 * 10**6),
        name="far_field",
    )(*operands)


def gradient_call(*operands):
    return pl.pallas_call(
        gradient_kernel,
        out_shape=f32(32, 2, 8, CORE),
        in_specs=[SMEM] + [VMEM] * 12,
        out_specs=VMEM,
        scratch_shapes=[
            pltpu.VMEM((2 * SPAN, HALF), jnp.bfloat16),
            pltpu.VMEM((2 * SPAN, HALF), jnp.bfloat16),
            pltpu.VMEM((2 * SPAN, SPAN), jnp.bfloat16),
            pltpu.VMEM((2 * SPAN, SPAN), jnp.bfloat16),
        ],
        compiler_params=limit(28),
        cost_estimate=cost(3 * 2 * 722 * 10**6, 7 * 10**6),
        name="gradient",
    )(*operands)


def up(values):
    count = lax.axis_size("z")
    return lax.ppermute(values, "z", [(i, (i + 1) % count) for i in range(count)])


def down(values):
    count = lax.axis_size("z")
    return lax.ppermute(values, "z", [((i + 1) % count, i) for i in range(count)])


def ring_gather(own):
    chunks = {(0, 0): own[0], (0, 1): own[1]}
    for step in range(1, 4):
        for layer in range(2):
            chunks[8 - step, layer] = up(chunks[(9 - step) % 8, layer])
            chunks[step, layer] = down(chunks[step - 1, layer])
    chunks[4, 0] = up(chunks[5, 0])
    chunks[4, 1] = down(chunks[3, 1])
    return [chunks[step, layer] for step in range(8) for layer in range(2)]


def ring_scatter(partial):
    top, bottom = (4, 3), (3, 4)
    rise = [partial[2 * top[half] + half] for half in range(2)]
    fall = [partial[2 * (8 - bottom[half]) + half] for half in range(2)]
    for step in range(1, 5):
        for half in range(2):
            if step <= top[half]:
                rise[half] = up(rise[half])
                if step < top[half]:
                    rise[half] = rise[half] + partial[2 * (top[half] - step) + half]
            if step <= bottom[half]:
                fall[half] = down(fall[half])
                if step < bottom[half]:
                    fall[half] = fall[half] + partial[2 * (8 - bottom[half] + step) + half]
    return jnp.concatenate([partial[half] + rise[half] + fall[half] for half in range(2)])


def body(screens, row_offsets, col_offsets, amplitude, object_strip, observed):
    patches = lax.axis_size("z") * lax.axis_size("x")
    table = row_offsets * SCOLS + col_offsets
    own = pl.pallas_call(
        cut_kernel,
        out_shape=[pltpu.VMEM((8, screens.shape[2]), jnp.float32)] * 2,
        in_specs=[ANY],
        out_specs=[VMEM] * 2,
        scratch_shapes=[pltpu.SemaphoreType.DMA((2,))],
        compiler_params=limit(58),
        name="cut_rows",
    )(screens)
    chunks = ring_gather(own)
    sent = pl.pallas_call(
        select_kernel,
        out_shape=f32(32, 2, 8, CORE),
        in_specs=[SMEM] + [VMEM] * 16,
        out_specs=VMEM,
        scratch_shapes=[pltpu.VMEM((16, 8, screens.shape[2]), jnp.float32)],
        compiler_params=limit(20),
        cost_estimate=cost(0, 3 * 10**6),
        name="select_rows",
    )(table, *chunks)
    sent, strip = lax.optimization_barrier((sent, object_strip))
    received = lax.all_to_all(sent, SLAB, split_axis=0, concat_axis=0, tiled=True)
    ends = patches - 1
    half = SPAN // 2
    core = lax.axis_index("core")
    tail, head = strip[:, CORE - HALO :], strip[:, :HALO]
    edge = jnp.where(core == 0, tail, head)
    mine = lax.ppermute(
        jnp.concatenate([edge[:half], edge[half:]], axis=1),
        ("z", "x", "core"),
        [(2 * i, 2 * i + 2) for i in range(ends)]
        + [(2 * i + 3, 2 * i + 1) for i in range(ends)],
    )
    other = lax.ppermute(mine, "core", [(0, 1), (1, 0)])
    base = pl.pallas_call(
        base_kernel,
        out_shape=jax.ShapeDtypeStruct((4, SPAN, SPAN), jnp.bfloat16),
        out_specs=VMEM,
        compiler_params=limit(20),
        cost_estimate=cost(10**6, 10**6),
        name="dft_base",
    )()
    forward, inverse, *fields = far_call(table, received, amplitude, base)
    spec_re, spec_im = pl.pallas_call(
        object_kernel,
        out_shape=[f32(SPAN, HALF)] * 2,
        in_specs=[VMEM] * 5,
        out_specs=[VMEM] * 2,
        compiler_params=limit(28),
        cost_estimate=cost(3 * 2 * 226 * 10**6, 7 * 10**6),
        name="object_spectrum",
    )(forward, inverse, strip, mine, other)
    placed = gradient_call(
        table, amplitude, observed, forward, inverse, *fields, spec_re, spec_im
    )
    returned = lax.all_to_all(placed, SLAB, split_axis=0, concat_axis=0, tiled=True)

    partial = pl.pallas_call(
        scatter_kernel,
        out_shape=[f32(4, 2, 8, 512)] * 16,
        in_specs=[SMEM] + [VMEM],
        out_specs=[VMEM] * 16,
        scratch_shapes=[pltpu.VMEM((8, 8, 2, 8, 512), jnp.float32)],
        compiler_params=limit(20),
        cost_estimate=cost(0, 3 * 10**6),
        name="scatter_rows",
    )(table, returned)
    summed = ring_scatter(partial)
    turned = lax.all_to_all(summed, FRAME, split_axis=0, concat_axis=0, tiled=True)
    return turned.transpose(1, 0, 2, 3).reshape(2, 64, 512)


def solution(mesh):
    fine = Mesh(mesh.devices.reshape(8, 4, 4, 2), ("z", "x", "y", "core"))
    patch = ("z", "x")
    in_specs = (
        P(None, patch, None), P(), P(), P(), P(None, patch), P(FRAME, None, patch),
    )
    out_specs = P(None, patch, FRAME)
    return jax.shard_map(body, mesh=fine, in_specs=in_specs, out_specs=out_specs, check_vma=False)
```

```python
import math

import jax
import jax.numpy as jnp
from jax import lax
from jax.experimental import pallas as pl
from jax.experimental.pallas import tpu as pltpu
from jax.sharding import Mesh, PartitionSpec as P


CORE = 256
HALO = 64
SPAN = 384
SCOLS = 4096
HALF = 256
SLAB = ("x", "y", "core")
FRAME = ("y", "core")


def split(values):
    high = values.astype(jnp.bfloat16)
    low = (values - high.astype(jnp.float32)).astype(jnp.bfloat16)
    return high, low


def dot(left, right):
    return jnp.dot(left, right, preferred_element_type=jnp.float32)


def left(matrix, rows, parts):
    totals = [None, None]
    for lanes, (high, low) in parts:
        for block in range(2):
            both = matrix[2 * block : 2 * block + 2, 0:rows, lanes].reshape(2 * rows, high.shape[0])
            term, small = dot(both, high), dot(both[0:rows], low)
            before = totals[block]
            totals[block] = (term, small) if before is None else (before[0] + term, before[1] + small)
    return tuple(term[0:rows] + (term[rows : 2 * rows] + small) for term, small in totals)


def right(parts, matrix, lanes):
    rows = parts[0][0].shape[0] // 2
    totals = [None, None]
    for part, (high, low) in enumerate(parts):
        depth = high.shape[1]
        weights = (matrix[2 * part, 0:depth, lanes], matrix[2 * part + 1, 0:depth, lanes])
        for block in range(2):
            at = slice(block * rows, block * rows + rows)
            term = dot(jnp.concatenate([high[at], low[at]], axis=0), weights[0])
            small = dot(high[at], weights[1])
            before = totals[block]
            totals[block] = (term, small) if before is None else (before[0] + term, before[1] + small)
    return jnp.concatenate(
        [term[0:rows] + (term[rows : 2 * rows] + small) for term, small in totals], axis=0
    )


def build(matrix, base, sign):
    for part in range(2):
        cosine, sine = base[2 * part], base[2 * part + 1]
        matrix[part, :, FULL] = cosine
        matrix[part, :, REST] = sine if sign > 0 else -sine
        matrix[2 + part, :, FULL] = -sine if sign > 0 else sine
        matrix[2 + part, :, REST] = cosine


def sine_cosine(angle):
    turns = jnp.round(angle * (2.0 / math.pi))
    rest = angle - turns * 1.5703125
    rest = rest - turns * 4.83826794896619e-4
    square = rest * rest
    sine = rest + rest * square * (
        -1.6666654611e-1 + square * (8.3321608736e-3 + square * -1.9515295891e-4)
    )
    cosine = 1.0 - 0.5 * square + square * square * (
        4.166664568298827e-2 + square * (-1.388731625493765e-3 + square * 2.443315711809948e-5)
    )
    quarter = turns.astype(jnp.int32)
    odd = (quarter & 1) == 1
    sine, cosine = jnp.where(odd, cosine, sine), jnp.where(odd, sine, cosine)
    sine = jnp.where((quarter & 2) == 2, -sine, sine)
    cosine = jnp.where(((quarter + 1) & 2) == 2, -cosine, cosine)
    return sine, cosine


LOW = slice(0, CORE)
HIGH = slice(SPAN, SPAN + CORE)
FULL = slice(0, SPAN)
REST = slice(SPAN, 2 * SPAN)
ALL = slice(None)


def frame_index():
    return lax.axis_index("y") * 2 + lax.axis_index("core")


def base_kernel(base):
    block = SPAN // 8
    row = lax.broadcasted_iota(jnp.int32, (block, SPAN), 0)
    column = lax.broadcasted_iota(jnp.int32, (block, SPAN), 1)

    def fill(index, carry):
        begin = pl.multiple_of(index * block, block)
        steps = ((row + begin) * column).astype(jnp.float32)
        steps = steps - SPAN * jnp.floor((steps + 0.5) * (1.0 / SPAN))
        sine, cosine = sine_cosine(steps * (2.0 * math.pi / SPAN))
        at = pl.ds(begin, block)
        base[0, at], base[2, at] = split(cosine)
        base[1, at], base[3, at] = split(sine)
        return carry

    lax.fori_loop(0, 8, fill, 0)


def object_kernel(forward, inverse, strip, mine, other, spec_re, spec_im):
    lane = lax.broadcasted_iota(jnp.int32, (SPAN // 2, 2 * HALO), 1)
    first = lax.axis_index("core") == 0
    before = jnp.where(first, mine[...], other[...])
    after = jnp.where(first, other[...], mine[...])
    top = jnp.where(lane < HALO, after, pltpu.roll(before, HALO, 1))
    bottom = jnp.where(lane < HALO, pltpu.roll(after, HALO, 1), before)
    halo = jnp.concatenate([top, bottom], axis=0)
    window = jnp.concatenate([strip[...], halo], axis=1)
    window = jnp.concatenate([window[HALO:], window[:HALO]], axis=0)
    seen = split(window)
    part_re = split(right([seen], inverse, LOW))
    part_im = split(right([seen], inverse, HIGH))
    real, imag = left(forward, SPAN, [(FULL, part_re), (REST, part_im)])
    column = lax.broadcasted_iota(jnp.int32, (SPAN, HALF), 1)
    ends = (column == 0) | (column == SPAN // 2)
    weight = jnp.where(ends, 1.0, jnp.where(column < SPAN // 2, 2.0, 0.0)) / (SPAN * SPAN)
    spec_re[...] = real * weight
    spec_im[...] = imag * weight


def cut_kernel(screens, first, second, sems):
    at = pl.ds(pl.multiple_of(frame_index() * 8, 8), 8)
    copies = [
        pltpu.make_async_copy(screens.at[layer, at, :], target, sems.at[layer])
        for layer, target in enumerate((first, second))
    ]
    for copy in copies:
        copy.start()
    for copy in copies:
        copy.wait()


def select_kernel(table, *refs):
    chunks, out, gathered = refs[:16], refs[16], refs[17]
    slab, first = lax.axis_index("z"), lax.axis_index("x") * 64 + frame_index() * 8
    for step in range(8):
        source = (slab + step) & 7
        for layer in range(2):
            gathered[source * 2 + layer] = chunks[step * 2 + layer][...]
    row_index = first + lax.broadcasted_iota(jnp.int32, (8, CORE), 0)
    lane = lax.broadcasted_iota(jnp.int32, (8, CORE), 1)

    def one(member, carry):
        patch = slab * 4 + (member >> 3)
        frame = member & 7
        for layer in range(2):
            both = table[frame, layer, patch]
            row, col = both >> 12, both & (SCOLS - 1)
            block, residue = row >> 8, row & 255
            after = jnp.minimum(block + 1, 7)
            strip, turn = col >> 8, col & 255
            at = pl.ds(pl.multiple_of(strip * CORE, CORE), CORE)
            beside = pl.ds(pl.multiple_of(jnp.minimum(strip + 1, 15) * CORE, CORE), CORE)
            right = lane >= turn
            upper = jnp.where(
                right, gathered[block * 2 + layer, :, at], gathered[block * 2 + layer, :, beside]
            )
            lower = jnp.where(
                right, gathered[after * 2 + layer, :, at], gathered[after * 2 + layer, :, beside]
            )
            out[member, layer] = jnp.where(row_index >= residue, upper, lower)
        return carry

    lax.fori_loop(0, 32, one, 0, unroll=8)


def scatter_kernel(table, values, *refs):
    pieces, out = refs[:16], refs[16]
    slab, first = lax.axis_index("z"), lax.axis_index("x") * 64 + frame_index() * 8
    row_index = first + lax.broadcasted_iota(jnp.int32, (8, CORE), 0)
    lane = lax.broadcasted_iota(jnp.int32, (8, CORE), 1)
    out[...] = jnp.zeros_like(out)

    def one(member, carry):
        patch = slab * 4 + (member >> 3)
        frame = member & 7
        for layer in range(2):
            both = table[frame, layer, patch]
            row, col = both >> 12, both & (SCOLS - 1)
            block, residue = row >> 8, row & 255
            after = jnp.minimum(block + 1, 7)
            strip, turn = col >> 8, col & 255
            beside = jnp.minimum(strip + 1, 15)
            value = values[member, layer]
            here = row_index >= residue
            right = lane >= turn
            for target, keep_row in ((block, here), (after, ~here)):
                where = (target + 8 - slab) & 7
                for place_col, keep_col in ((strip, right), (beside, ~right)):
                    at = pl.ds(pl.multiple_of((place_col & 1) * CORE, CORE), CORE)
                    chunk = place_col >> 1
                    out[where, chunk, layer, :, at] = out[where, chunk, layer, :, at] + jnp.where(
                        keep_row & keep_col, value, 0.0
                    )
        return carry

    lax.fori_loop(0, 32, one, 0, unroll=4)
    for index, piece in enumerate(pieces):
        piece[...] = out[index // 2, 4 * (index % 2) : 4 * (index % 2) + 4]


def put(high, low, at, values):
    high[at], low[at] = split(values)


def inverse_sum(amplitude):
    return 1.0 / (SPAN * SPAN * jnp.sum(amplitude * amplitude))


def turns_of(table):
    frame = frame_index()
    patch = lax.axis_index("z") * 4 + lax.axis_index("x")
    both = [table[frame, layer, patch] for layer in range(2)]
    return [((value >> 12) & 255, value & 255) for value in both]


def far_kernel(
    table, received, amp_ref, base, forward, inverse, pupil_re, pupil_im, far_re, far_im,
    spread_re, spread_im, mix_h, mix_l,
):
    build(forward, base, 1)
    build(inverse, base, -1)
    turns = turns_of(table)
    phases = None
    for layer in range(2):
        sheet = received[:, layer].reshape(CORE, CORE)
        sheet = pltpu.roll(sheet, (CORE - turns[layer][0]) & 255, 0)
        sheet = pltpu.roll(sheet, (CORE - turns[layer][1]) & 255, 1)
        phases = sheet if phases is None else phases + sheet
    amplitude = amp_ref[...]
    inverse_total = inverse_sum(amplitude)
    sine, cosine = sine_cosine(phases)
    pupil_re[...] = amplitude * cosine
    pupil_im[...] = amplitude * sine
    half_re, half_im = left(
        forward, SPAN, [(LOW, split(pupil_re[...])), (HIGH, split(pupil_im[...]))]
    )
    half = [split(half_re), split(half_im)]
    far = right(half, inverse, ALL)
    far_re[...] = far[:, FULL]
    far_im[...] = far[:, REST]
    spread = [split((far_re[...] * far_re[...] + far_im[...] * far_im[...]) * inverse_total)]
    put(mix_h, mix_l, FULL, right(spread, inverse, LOW))
    put(mix_h, mix_l, REST, right(spread, inverse, HIGH))
    spread_re[...], spread_im[...] = left(forward, SPAN, [(ALL, (mix_h[...], mix_l[...]))])


def gradient_kernel(
    table, amp_ref, observed, forward, inverse, pupil_re, pupil_im, far_re, far_im,
    spread_re, spread_im, spec_re, spec_im, out, mix_h, mix_l, wide_h, wide_l,
):
    inverse_total = inverse_sum(amp_ref[...])
    first, second = spread_re[...], spread_im[...]
    put(mix_h, mix_l, FULL, first * spec_re[...] - second * spec_im[...])
    put(mix_h, mix_l, REST, first * spec_im[...] + second * spec_re[...])
    first, second = left(inverse, CORE, [(ALL, (mix_h[...], mix_l[...]))])
    model = right([split(first), split(second)], forward, LOW)
    residual = [split((model - observed[0]) * float(SPAN))]
    grad_re = split(right(residual, inverse, LOW))
    grad_im = split(right(residual, inverse, HIGH))
    first, second = left(forward, SPAN, [(LOW, grad_re), (HIGH, grad_im)])
    put(mix_h, mix_l, FULL, first * spec_re[...] + second * spec_im[...])
    put(mix_h, mix_l, REST, second * spec_re[...] - first * spec_im[...])
    first, second = left(inverse, SPAN, [(ALL, (mix_h[...], mix_l[...]))])
    spread_grad = right([split(first), split(second)], forward, FULL)
    put(wide_h, wide_l, FULL, far_re[...] * spread_grad)
    put(wide_h, wide_l, REST, far_im[...] * spread_grad)
    first, second = left(inverse, CORE, [(ALL, (wide_h[...], wide_l[...]))])
    back = [split(first), split(second)]
    out_re = right(back, forward, LOW)
    out_im = right(back, forward, HIGH)
    gradient = (2.0 * inverse_total) * (pupil_re[...] * out_im - pupil_im[...] * out_re)
    turns = turns_of(table)
    for layer in range(2):
        sheet = pltpu.roll(gradient, turns[layer][1], 1)
        sheet = pltpu.roll(sheet, turns[layer][0], 0)
        out[:, layer] = sheet.reshape(32, 8, CORE)


SMEM = pl.BlockSpec(memory_space=pltpu.SMEM)
VMEM = pl.BlockSpec(memory_space=pltpu.VMEM)
ANY = pl.BlockSpec(memory_space=pl.ANY)


def limit(mib):
    return pltpu.CompilerParams(vmem_limit_bytes=mib << 20)


def cost(flops, moved):
    return pl.CostEstimate(flops=flops, bytes_accessed=moved, transcendentals=0)


def f32(*shape):
    return jax.ShapeDtypeStruct(shape, jnp.float32)


def far_call(*operands):
    matrix = jax.ShapeDtypeStruct((4, SPAN, 2 * SPAN), jnp.bfloat16)
    return pl.pallas_call(
        far_kernel,
        out_shape=[matrix] * 2 + [f32(CORE, CORE)] * 2 + [f32(SPAN, SPAN)] * 2 + [f32(SPAN, HALF)] * 2,
        in_specs=[SMEM] + [VMEM] * 3,
        out_specs=[VMEM] * 8,
        scratch_shapes=[pltpu.VMEM((2 * SPAN, HALF), jnp.bfloat16)] * 2,
        compiler_params=limit(28),
        cost_estimate=cost(3 * 2 * 500 * 10**6, 7 * 10**6),
        name="far_field",
    )(*operands)


def gradient_call(*operands):
    return pl.pallas_call(
        gradient_kernel,
        out_shape=f32(32, 2, 8, CORE),
        in_specs=[SMEM] + [VMEM] * 12,
        out_specs=VMEM,
        scratch_shapes=[
            pltpu.VMEM((2 * SPAN, HALF), jnp.bfloat16),
            pltpu.VMEM((2 * SPAN, HALF), jnp.bfloat16),
            pltpu.VMEM((2 * SPAN, SPAN), jnp.bfloat16),
            pltpu.VMEM((2 * SPAN, SPAN), jnp.bfloat16),
        ],
        compiler_params=limit(28),
        cost_estimate=cost(3 * 2 * 722 * 10**6, 7 * 10**6),
        name="gradient",
    )(*operands)


def up(values):
    count = lax.axis_size("z")
    return lax.ppermute(values, "z", [(i, (i + 1) % count) for i in range(count)])


def down(values):
    count = lax.axis_size("z")
    return lax.ppermute(values, "z", [((i + 1) % count, i) for i in range(count)])


def send(way, values):
    return up(values) if way == "up" else down(values)


def ring_gather(own):
    chunks = {(0, 0): own[0], (0, 1): own[1]}
    for step in range(1, 4):
        for layer in range(2):
            chunks[8 - step, layer] = send("up", chunks[(9 - step) % 8, layer])
            chunks[step, layer] = send("down", chunks[step - 1, layer])
    chunks[4, 0] = send("up", chunks[5, 0])
    chunks[4, 1] = send("down", chunks[3, 1])
    return [chunks[step, layer] for step in range(8) for layer in range(2)]


def ring_scatter(partial):
    top, bottom = (4, 3), (3, 4)
    rise = [partial[2 * top[half] + half] for half in range(2)]
    fall = [partial[2 * (8 - bottom[half]) + half] for half in range(2)]
    for step in range(1, 5):
        for half in range(2):
            if step <= top[half]:
                rise[half] = send("up", rise[half])
                if step < top[half]:
                    rise[half] = rise[half] + partial[2 * (top[half] - step) + half]
            if step <= bottom[half]:
                fall[half] = send("down", fall[half])
                if step < bottom[half]:
                    fall[half] = fall[half] + partial[2 * (8 - bottom[half] + step) + half]
    return jnp.concatenate([partial[half] + rise[half] + fall[half] for half in range(2)])


def body(screens, row_offsets, col_offsets, amplitude, object_strip, observed):
    patches = lax.axis_size("z") * lax.axis_size("x")
    table = row_offsets * SCOLS + col_offsets
    own = pl.pallas_call(
        cut_kernel,
        out_shape=[pltpu.VMEM((8, screens.shape[2]), jnp.float32)] * 2,
        in_specs=[ANY],
        out_specs=[VMEM] * 2,
        scratch_shapes=[pltpu.SemaphoreType.DMA((2,))],
        compiler_params=limit(58),
        name="cut_rows",
    )(screens)
    chunks = ring_gather(own)
    sent = pl.pallas_call(
        select_kernel,
        out_shape=f32(32, 2, 8, CORE),
        in_specs=[SMEM] + [VMEM] * 16,
        out_specs=VMEM,
        scratch_shapes=[pltpu.VMEM((16, 8, screens.shape[2]), jnp.float32)],
        compiler_params=limit(20),
        cost_estimate=cost(0, 3 * 10**6),
        name="select_rows",
    )(table, *chunks)
    sent, strip = lax.optimization_barrier((sent, object_strip))
    received = lax.all_to_all(sent, SLAB, split_axis=0, concat_axis=0, tiled=True)
    ends = patches - 1
    half = SPAN // 2
    core = lax.axis_index("core")
    tail, head = strip[:, CORE - HALO :], strip[:, :HALO]
    edge = jnp.where(core == 0, tail, head)
    mine = lax.ppermute(
        jnp.concatenate([edge[:half], edge[half:]], axis=1),
        ("z", "x", "core"),
        [(2 * i, 2 * i + 2) for i in range(ends)]
        + [(2 * i + 3, 2 * i + 1) for i in range(ends)],
    )
    other = lax.ppermute(mine, "core", [(0, 1), (1, 0)])
    base = pl.pallas_call(
        base_kernel,
        out_shape=jax.ShapeDtypeStruct((4, SPAN, SPAN), jnp.bfloat16),
        out_specs=VMEM,
        compiler_params=limit(20),
        cost_estimate=cost(10**6, 10**6),
        name="dft_base",
    )()
    forward, inverse, *fields = far_call(table, received, amplitude, base)
    spec_re, spec_im = pl.pallas_call(
        object_kernel,
        out_shape=[f32(SPAN, HALF)] * 2,
        in_specs=[VMEM] * 5,
        out_specs=[VMEM] * 2,
        compiler_params=limit(28),
        cost_estimate=cost(3 * 2 * 226 * 10**6, 7 * 10**6),
        name="object_spectrum",
    )(forward, inverse, strip, mine, other)
    placed = gradient_call(
        table, amplitude, observed, forward, inverse, *fields, spec_re, spec_im
    )
    returned = lax.all_to_all(placed, SLAB, split_axis=0, concat_axis=0, tiled=True)

    partial = pl.pallas_call(
        scatter_kernel,
        out_shape=[f32(4, 2, 8, 512)] * 16,
        in_specs=[SMEM] + [VMEM],
        out_specs=[VMEM] * 16,
        scratch_shapes=[pltpu.VMEM((8, 8, 2, 8, 512), jnp.float32)],
        compiler_params=limit(20),
        cost_estimate=cost(0, 3 * 10**6),
        name="scatter_rows",
    )(table, returned)
    summed = ring_scatter(partial)
    turned = lax.all_to_all(summed, FRAME, split_axis=0, concat_axis=0, tiled=True)
    return turned.transpose(1, 0, 2, 3).reshape(2, 64, 512)


def solution(mesh):
    fine = Mesh(mesh.devices.reshape(8, 4, 4, 2), ("z", "x", "y", "core"))
    patch = ("z", "x")
    in_specs = (
        P(None, patch, None), P(), P(), P(), P(None, patch), P(FRAME, None, patch),
    )
    out_specs = P(None, patch, FRAME)
    return jax.shard_map(body, mesh=fine, in_specs=in_specs, out_specs=out_specs, check_vma=False)
```
